32 devices in a mesh: rep: 8 (over y, x, core), shard: 4 (over z).
Axes of the slice: x: 2, y: 2, z: 4, core: 2. Of those that a mesh axis runs over, the one named last changes fastest.
Arguments:
- tokens: bfloat16 [16384, 1536], P(('rep', 'shard')), may hold values from -6 to 6
- cotangent: bfloat16 [16384, 1536], P(('rep', 'shard')), may hold values from -6 to 6
- norm_first: bfloat16 [1536], P('shard'), may hold values from 0.5 to 1.5
- branch_weight: bfloat16 [1536, 2048], P(None, 'shard'), may hold values from -0.15625 to 0.15625
- gelu_weight: bfloat16 [1536, 2048], P(None, 'shard'), may hold values from -0.15625 to 0.15625
- conv_weight: bfloat16 [4, 2048], P(None, 'shard'), may hold values from -2.5 to 2.5
- conv_bias: bfloat16 [2048], P('shard'), may hold values from -2.5 to 2.5
- gate_weight: bfloat16 [16, 128, 256], P('shard'), may hold values from -0.5 to 0.5
- gate_bias: bfloat16 [16, 256], P('shard'), may hold values from -2.5 to 2.5
- decay_param: bfloat16 [2048], P('shard'), may hold values from 2.1875 to 6.875
- merge_weight: bfloat16 [2048, 1536], P('shard'), may hold values from -0.375 to 0.375
- norm_second: bfloat16 [1536], P('shard'), may hold values from 0.5 to 1.5
- feed_gate: bfloat16 [1536, 4608], P(None, 'shard'), may hold values from -0.15625 to 0.15625
- feed_up: bfloat16 [1536, 4608], P(None, 'shard'), may hold values from -0.15625 to 0.15625
- feed_down: bfloat16 [4608, 1536], P('shard'), may hold values from -0.1875 to 0.1875
- down_branch: bfloat16 [1536, 128], P(None, 'shard'), may hold values from -0.15625 to 0.15625
- up_branch: bfloat16 [128, 2048], P('shard'), may hold values from -0.75 to 0.75
- down_gelu: bfloat16 [1536, 128], P(None, 'shard'), may hold values from -0.15625 to 0.15625
- up_gelu: bfloat16 [128, 2048], P('shard'), may hold values from -0.75 to 0.75
- down_gates: bfloat16 [2048, 128], P(None, 'shard'), may hold values from -0.125 to 0.125
- up_gates: bfloat16 [128, 4096], P('shard'), may hold values from -0.75 to 0.75
- down_merge: bfloat16 [2048, 128], P(None, 'shard'), may hold values from -0.125 to 0.125
- up_merge: bfloat16 [128, 1536], P('shard'), may hold values from -0.75 to 0.75
- down_feed_gate: bfloat16 [1536, 128], P(None, 'shard'), may hold values from -0.15625 to 0.15625
- up_feed_gate: bfloat16 [128, 4608], P('shard'), may hold values from -0.75 to 0.75
- down_feed_up: bfloat16 [1536, 128], P(None, 'shard'), may hold values from -0.15625 to 0.15625
- up_feed_up: bfloat16 [128, 4608], P('shard'), may hold values from -0.75 to 0.75
- down_feed_down: bfloat16 [4608, 128], P(None, 'shard'), may hold values from -0.09375 to 0.09375
- up_feed_down: bfloat16 [128, 1536], P('shard'), may hold values from -0.75 to 0.75
- seq_lengths: int32 [32, 4], P(('rep', 'shard')), may hold values from 1 to 256, 384 in all within a row
- adapter_index: int32 [32, 4], P(('rep', 'shard')), may hold values from 0 to 7
- deal_order: int32 [8, 2048], P('rep'), may hold values from 0 to 2047, as said below
Outputs:
- layer_out: float32 [16384, 1536], P(('rep', 'shard'))
- grad_tokens: float32 [16384, 1536], P(('rep', 'shard'))
- grad_down_branch: float32 [1536, 128], P(None, 'shard')
- grad_up_branch: float32 [128, 2048], P('shard')
- grad_down_gelu: float32 [1536, 128], P(None, 'shard')
- grad_up_gelu: float32 [128, 2048], P('shard')
- grad_down_gates: float32 [2048, 128], P(None, 'shard')
- grad_up_gates: float32 [128, 4096], P('shard')
- grad_down_merge: float32 [2048, 128], P(None, 'shard')
- grad_up_merge: float32 [128, 1536], P('shard')
- grad_down_feed_gate: float32 [1536, 128], P(None, 'shard')
- grad_up_feed_gate: float32 [128, 4608], P('shard')
- grad_down_feed_up: float32 [1536, 128], P(None, 'shard')
- grad_up_feed_up: float32 [128, 4608], P('shard')
- grad_down_feed_down: float32 [4608, 128], P(None, 'shard')
- grad_up_feed_down: float32 [128, 1536], P('shard')
The draws below stay inside these ranges and needn't reach their ends.
Inputs may be any that keep to these rules, and one draw needn't show every extreme that they name: Each row of deal_order is a permutation of 0 to 2047. Exactly 128 of the arrival rows of one device (rows b * 512 to b * 512 + 511 of its group) fill slots of each block of its group. `seq_lengths`: in every block the lengths sum to 384 and the longest is 256.
All inputs are finite; a program needn't handle non-finite values.
Results may differ from the reference program's by a relative error of at most 0.015.
Values may be sent and summed in bfloat16 or wider, within the bound.
A program may use at most 320 MiB of HBM per device.

```python
import math
import jax
import jax.numpy as jnp
import numpy as np
from jax import lax

D = 1536
LRU = 2048
FF = 4608
H = 16
DH = 128
KW = 4
NA = 8
R = 16
NAR = 128
NSEQ = 4
TOK_DEV = 512
SEQ_MAX = 256
FILL_TOK = 384
CAP = 128
GROUP_TOK = 2048
BLOCKS = 32
TOKENS = 16384
N_REP = 8
N_SHARD = 4


def deal_group(key):
    total = TOK_DEV * N_SHARD
    key_ranks, key_shuffle = jax.random.split(key, 2)
    ranks = jax.vmap(lambda k: jax.random.permutation(k, TOK_DEV))(jax.random.split(key_ranks, N_SHARD)).astype(jnp.int32)
    target = (ranks // CAP).astype(jnp.int32)
    shuffle = jax.random.permutation(key_shuffle, total).astype(jnp.int32).reshape(N_SHARD, TOK_DEV)
    score = (target * total + shuffle).reshape(-1)
    return jnp.argsort(score, stable=True).astype(jnp.int32)


def draw_deal_order(key, part):
    return jax.vmap(deal_group)(jax.random.split(key, N_REP))


def place_ends(drawn, key, smallest, top_value):
    dims = drawn.shape
    place = [jax.random.randint(jax.random.fold_in(key, axis), (), 0, dims[axis]) for axis in range(len(dims))]
    drawn = drawn.at[tuple(place)].set(smallest)
    longest = dims.index(max(dims))
    place[longest] = (place[longest] + 1) % dims[longest]
    return drawn.at[tuple(place)].set(top_value)


def block_levels(stream_key, shape, shards, low, top_value):
    def one(dim, shards_of):
        steps = jax.random.uniform(jax.random.fold_in(jax.random.fold_in(stream_key, 6), dim), (shards_of,), jnp.float32, low / len(shards), top_value / len(shards))
        return jnp.repeat(jnp.exp(steps), shape[dim] // shards_of).reshape((-1,) + (1,) * (len(shape) - dim - 1))

    factor_of = one(*shards[0])
    for cut in shards[1:]:
        factor_of = factor_of * one(*cut)
    return factor_of


def length_profile(amount, total, bound, lean):
    portions = [(1 << 20) // math.isqrt(standing ** lean) + 1 for standing in range(2, amount + 1)]
    rest, holding = total - bound - (amount - 1), [1] * (amount - 1)
    while rest > 0:
        free = [i for i in range(amount - 1) if holding[i] < bound]
        whole, left = sum([portions[i] for i in free]), rest
        for i in free:
            more = min(bound - holding[i], max(1, left * portions[i] // whole), rest)
            holding[i] = holding[i] + more
            rest = rest - more
    return np.array([bound] + holding)


def ragged_sizes(key, count, total, most, skew):
    if count == 2:
        one = jax.random.randint(key, (), max(1, total - most), min(most, total - 1) + 1)
        return jnp.stack([one, total - one])
    lengths = jnp.asarray(length_profile(count, total, most, skew), jnp.int32)
    pairs = (count - 1) // 2
    donor, receiver = lengths[1:1 + 2 * pairs:2], lengths[2:2 + 2 * pairs:2]
    room = jnp.minimum(donor - 1, most - receiver)
    moved = jax.random.randint(jax.random.fold_in(key, 1), (pairs,), 0, 1 << 20) % (room + 1)
    lengths = lengths.at[1:1 + 2 * pairs:2].set(donor - moved).at[2:2 + 2 * pairs:2].set(receiver + moved)
    return lengths[jax.random.permutation(jax.random.fold_in(key, 2), count)]


def normal_values(own_key, extent, deviation, limit, pieces=(), kind=jnp.bfloat16):
    array = jax.random.normal(own_key, extent, jnp.float32) * deviation
    if len(pieces) > 0:
        array = block_levels(own_key, extent, pieces, -0.22, 0.18) * array
    return jnp.clip(array, min=-limit, max=limit).astype(kind)


def setup_inputs(seed: int = 0) -> dict:
    splits = jax.random.split(jax.random.key(seed), 33)
    tokens = normal_values(splits[0], (TOKENS, D), 1.0, 6.0, ((0, 32),))
    cotangent = normal_values(splits[1], (TOKENS, D), 1.0, 6.0, ((0, 32),))
    norm_first = jnp.clip(1.0 + 0.1 * jax.random.normal(splits[2], (D,), jnp.float32), 0.5, 1.5).astype(jnp.bfloat16)
    branch_weight = normal_values(splits[3], (D, LRU), D ** -0.5, 0.15625, ((1, 4),))
    gelu_weight = normal_values(splits[4], (D, LRU), D ** -0.5, 0.15625, ((1, 4),))
    conv_weight = normal_values(splits[5], (KW, LRU), 0.5, 2.5, ((1, 4),))
    conv_bias = normal_values(splits[6], (LRU,), 0.5, 2.5, ((0, 4),))
    gate_weight = normal_values(splits[7], (H, DH, 2 * DH), DH ** -0.5, 0.5, ((0, 4),))
    gate_bias = normal_values(splits[8], (H, 2 * DH), 0.5, 2.5, ((0, 4),))
    decay_param = jnp.clip(2.1875 + 4.6875 * jax.random.uniform(splits[9], (LRU,), jnp.float32) ** block_levels(splits[9], (LRU,), ((0, 4),), -0.2, 0.2), 2.1875, 6.875).astype(jnp.bfloat16)
    merge_weight = normal_values(splits[10], (LRU, D), (LRU // 8) ** -0.5, 0.375, ((0, 4),))
    norm_second = jnp.clip(1.0 + 0.1 * jax.random.normal(splits[11], (D,), jnp.float32), 0.5, 1.5).astype(jnp.bfloat16)
    feed_gate = normal_values(splits[12], (D, FF), D ** -0.5, 0.15625, ((1, 4),))
    feed_up = normal_values(splits[13], (D, FF), D ** -0.5, 0.15625, ((1, 4),))
    feed_down = normal_values(splits[14], (FF, D), (FF // 4) ** -0.5, 0.1875, ((0, 4),))
    down_branch = normal_values(splits[15], (D, NAR), D ** -0.5, 0.15625, ((1, 4),))
    up_branch = normal_values(splits[16], (NAR, LRU), (4 * R) ** -0.5, 0.75, ((0, 4),))
    down_gelu = normal_values(splits[17], (D, NAR), D ** -0.5, 0.15625, ((1, 4),))
    up_gelu = normal_values(splits[18], (NAR, LRU), (4 * R) ** -0.5, 0.75, ((0, 4),))
    down_gates = normal_values(splits[19], (LRU, NAR), LRU ** -0.5, 0.125, ((1, 4),))
    up_gates = normal_values(splits[20], (NAR, 2 * LRU), (4 * R) ** -0.5, 0.75, ((0, 4),))
    down_merge = normal_values(splits[21], (LRU, NAR), LRU ** -0.5, 0.125, ((1, 4),))
    up_merge = normal_values(splits[22], (NAR, D), (4 * R) ** -0.5, 0.75, ((0, 4),))
    down_feed_gate = normal_values(splits[23], (D, NAR), D ** -0.5, 0.15625, ((1, 4),))
    up_feed_gate = normal_values(splits[24], (NAR, FF), (4 * R) ** -0.5, 0.75, ((0, 4),))
    down_feed_up = normal_values(splits[25], (D, NAR), D ** -0.5, 0.15625, ((1, 4),))
    up_feed_up = normal_values(splits[26], (NAR, FF), (4 * R) ** -0.5, 0.75, ((0, 4),))
    down_feed_down = normal_values(splits[27], (FF, NAR), FF ** -0.5, 0.09375, ((1, 4),))
    up_feed_down = normal_values(splits[28], (NAR, D), (4 * R) ** -0.5, 0.75, ((0, 4),))
    seq_lengths = jax.vmap(lambda own: ragged_sizes(own, NSEQ, FILL_TOK, SEQ_MAX, 1))(jax.random.split(splits[29], BLOCKS)).reshape((BLOCKS, NSEQ)).astype(jnp.int32)
    adapter_index = place_ends(jax.random.randint(splits[30], (BLOCKS, NSEQ), 0, NA), jax.random.fold_in(splits[30], 1), 0, NA - 1).astype(jnp.int32)
    deal_order = draw_deal_order(jax.random.fold_in(splits[32], 71), 0)
    return dict(tokens=tokens, cotangent=cotangent, norm_first=norm_first, branch_weight=branch_weight, gelu_weight=gelu_weight, conv_weight=conv_weight, conv_bias=conv_bias, gate_weight=gate_weight, gate_bias=gate_bias, decay_param=decay_param, merge_weight=merge_weight, norm_second=norm_second, feed_gate=feed_gate, feed_up=feed_up, feed_down=feed_down, down_branch=down_branch, up_branch=up_branch, down_gelu=down_gelu, up_gelu=up_gelu, down_gates=down_gates, up_gates=up_gates, down_merge=down_merge, up_merge=up_merge, down_feed_gate=down_feed_gate, up_feed_gate=up_feed_gate, down_feed_up=down_feed_up, up_feed_up=up_feed_up, down_feed_down=down_feed_down, up_feed_down=up_feed_down, seq_lengths=seq_lengths, adapter_index=adapter_index, deal_order=deal_order)


@jax.custom_vjp
def low(v):
    return lax.optimization_barrier(v.astype(jnp.bfloat16)).astype(jnp.float32)

@jax.custom_vjp
def low_back(v):
    return v

def low_keep(v):
    return (low(v), None)

def low_pass(kept, grad):
    return (grad,)

def back_keep(v):
    return (v, None)

def back_low(kept, grad):
    return (low(grad),)
low.defvjp(low_keep, low_pass)
low_back.defvjp(back_keep, back_low)
PRECISE = lax.Precision.HIGHEST
NORM_EPSILON = 1e-06
DECAY_SCALE = 8.0

def matmul(left, right):
    return jnp.dot(left, right, precision=PRECISE, preferred_element_type=jnp.float32)

def root_norm(values, gain):
    return values * lax.rsqrt(lax.optimization_barrier(jnp.mean(values * values, axis=-1, keepdims=True)) + NORM_EPSILON) * gain

def layout(lengths_row, index_row, slots_count):
    seq_count = lengths_row.shape[0]
    ends = jnp.cumsum(lengths_row).astype(jnp.int32)
    starts = (ends - lengths_row).astype(jnp.int32)
    slots = jnp.arange(slots_count, dtype=jnp.int32)
    segment = lax.optimization_barrier(jnp.sum((slots[:, None] >= ends[None, :]).astype(jnp.int32), axis=1)).astype(jnp.int32)
    start_all = jnp.concatenate([starts, ends[-1:]]).astype(jnp.int32)
    member = segment[:, None] == jnp.arange(seq_count + 1, dtype=jnp.int32)[None, :]
    position = (slots - lax.optimization_barrier(jnp.sum(jnp.where(member, start_all[None, :], 0), axis=1))).astype(jnp.int32)
    live_rows = segment < seq_count
    chosen = lax.optimization_barrier(jnp.sum(jnp.where(member[:, :seq_count], index_row[None, :], 0), axis=1)).astype(jnp.int32)
    adapter_hit = (chosen[:, None] == jnp.arange(NA, dtype=jnp.int32)[None, :]) & live_rows[:, None]
    adapter_mask = jnp.repeat(adapter_hit.astype(jnp.float32), R, axis=1)
    return (position, live_rows.astype(jnp.float32), adapter_mask)

def conv_apply(values, weight, bias, position):
    total = bias[None, :] + weight[0][None, :] * values
    for offset in range(1, weight.shape[0]):
        moved = jnp.concatenate([jnp.zeros((offset, values.shape[1]), values.dtype), values[:-offset]], axis=0)
        keeper = (position >= offset).astype(values.dtype)[:, None]
        total = total + weight[offset][None, :] * moved * keeper
    return total

def combine(earlier, later):
    return (earlier[0] * later[0], later[0] * earlier[1] + later[1])

def recurrence(gate_logits, conv_out, gelu_in, decay, position):
    rows_count = conv_out.shape[0]
    shaped = gate_logits.reshape(rows_count, H, 2 * DH)
    input_gate = jax.nn.sigmoid(shaped[:, :, :DH]).reshape(rows_count, H * DH)
    rec_gate = jax.nn.sigmoid(shaped[:, :, DH:]).reshape(rows_count, H * DH)
    log_decay = -DECAY_SCALE * rec_gate * jax.nn.softplus(-decay)[None, :]
    decay_now = jnp.exp(log_decay)
    first = (position == 0)[:, None]
    scale_in = jnp.where(first, 1.0, jnp.sqrt(-jnp.expm1(2.0 * log_decay)))
    carried = jnp.where(first, 0.0, decay_now)
    driven = scale_in * input_gate * conv_out
    unused, state = lax.associative_scan(combine, (carried, driven), axis=0)
    return state * jax.nn.gelu(gelu_in)

def adapter_apply(act, down, up, adapter_mask):
    rank_part = low(low_back(matmul(act, down) * adapter_mask))
    return matmul(rank_part, up)

def block_forward(rows, frozen, adapters, lengths_row, index_row):
    norm_first, branch_weight, gelu_weight, conv_weight, conv_bias, gate_weight, gate_bias, decay_param, merge_weight, norm_second, feed_gate, feed_up, feed_down = frozen
    down_branch, up_branch, down_gelu, up_gelu, down_gates, up_gates, down_merge, up_merge, down_feed_gate, up_feed_gate, down_feed_up, up_feed_up, down_feed_down, up_feed_down = adapters
    rows_count = rows.shape[0]
    position, live_rows, adapter_mask = layout(lengths_row, index_row, rows_count)
    act_first = low(root_norm(rows, norm_first))
    branch = low_back(matmul(act_first, branch_weight) + adapter_apply(act_first, down_branch, up_branch, adapter_mask))
    gelu_in = low_back(matmul(act_first, gelu_weight) + adapter_apply(act_first, down_gelu, up_gelu, adapter_mask))
    conv_out = conv_apply(branch, conv_weight, conv_bias, position)
    conv_low = low(conv_out)
    heads = conv_low.reshape(rows_count, H, DH)
    blockwise = jnp.einsum('thd,hde->the', heads, gate_weight, precision=PRECISE).reshape(rows_count, 2 * H * DH)
    gate_logits = low_back(blockwise + gate_bias.reshape(-1)[None, :] + adapter_apply(conv_low, down_gates, up_gates, adapter_mask))
    mixed_low = low(recurrence(gate_logits, conv_out, gelu_in, decay_param, position))
    merged = low_back(matmul(mixed_low, merge_weight) + adapter_apply(mixed_low, down_merge, up_merge, adapter_mask))
    resid = rows + merged
    act_second = low(root_norm(resid, norm_second))
    hidden_gate = low_back(matmul(act_second, feed_gate) + adapter_apply(act_second, down_feed_gate, up_feed_gate, adapter_mask))
    hidden_up = low_back(matmul(act_second, feed_up) + adapter_apply(act_second, down_feed_up, up_feed_up, adapter_mask))
    hidden = low(jax.nn.gelu(hidden_gate) * hidden_up)
    lowered = low_back(matmul(hidden, feed_down) + adapter_apply(hidden, down_feed_down, up_feed_down, adapter_mask))
    return (resid + lowered) * live_rows[:, None]

def reference(tokens, cotangent, norm_first, branch_weight, gelu_weight, conv_weight, conv_bias, gate_weight, gate_bias, decay_param, merge_weight, norm_second, feed_gate, feed_up, feed_down, down_branch, up_branch, down_gelu, up_gelu, down_gates, up_gates, down_merge, up_merge, down_feed_gate, up_feed_gate, down_feed_up, up_feed_up, down_feed_down, up_feed_down, seq_lengths, adapter_index, deal_order):
    frozen = tuple((w.astype(jnp.float32) for w in (norm_first, branch_weight, gelu_weight, conv_weight, conv_bias, gate_weight, gate_bias, decay_param, merge_weight, norm_second, feed_gate, feed_up, feed_down)))
    adapters = tuple((w.astype(jnp.float32) for w in (down_branch, up_branch, down_gelu, up_gelu, down_gates, up_gates, down_merge, up_merge, down_feed_gate, up_feed_gate, down_feed_up, up_feed_up, down_feed_down, up_feed_down)))
    group_base = (jnp.arange(N_REP, dtype=jnp.int32) * GROUP_TOK)[:, None]
    rows_global = (deal_order + group_base).reshape(-1).astype(jnp.int32)
    checked = jax.checkpoint(block_forward)

    def forward(inputs, adapter_set):
        work = inputs[rows_global].reshape(BLOCKS, TOK_DEV, D)

        def step(carry, packed):
            rows, lengths_row, index_row = packed
            return (carry, checked(rows, frozen, adapter_set, lengths_row, index_row))
        unused, outputs = lax.scan(step, jnp.zeros((), jnp.float32), (work, seq_lengths, adapter_index))
        return jnp.zeros((TOKENS, D), jnp.float32).at[rows_global].set(outputs.reshape(TOKENS, D))
    layer_out, pull = jax.vjp(forward, tokens.astype(jnp.float32), adapters)
    grad_tokens, grads = pull(cotangent.astype(jnp.float32))
    return (layer_out, grad_tokens, grads[0], grads[1], grads[2], grads[3], grads[4], grads[5], grads[6], grads[7], grads[8], grads[9], grads[10], grads[11], grads[12], grads[13])
```

```python
import functools
from types import SimpleNamespace

import jax
import jax.numpy as jnp
from jax import lax
from jax.experimental import pallas as pl
from jax.experimental.pallas import tpu as pltpu
from jax.sharding import PartitionSpec as P

NA = 8
R = 16
NAR = NA * R
DH = 128
LIVE = 384
PLANE = 8
EPS = 1e-06
DECAY = 8.0
F32 = jnp.float32
BF16 = jnp.bfloat16
MESH_ID = pl.DeviceIdType.MESH
DMA = pltpu.SemaphoreType.DMA
ANY = pl.BlockSpec(memory_space=pl.ANY)
VM = pl.BlockSpec(memory_space=pltpu.VMEM)
VLIMIT = 60 << 20
GC = 0.7978845608028654
GA = 0.044715


def up_to(size, step):
    return -(-size // step) * step


def nn(a, b):
    return lax.dot_general(a, b, (((1,), (0,)), ((), ())), preferred_element_type=F32)


def nt(a, b):
    return lax.dot_general(a, b, (((1,), (1,)), ((), ())), preferred_element_type=F32)


def tn(a, b):
    return lax.dot_general(a, b, (((0,), (0,)), ((), ())), preferred_element_type=F32)


def gelu_parts(x):
    x2 = x * x
    th = jnp.tanh(GC * x * (1.0 + GA * x2))
    half = 0.5 * (1.0 + th)
    return x * half, half + 0.5 * x * (1.0 - th * th) * (GC * (1.0 + 3.0 * GA * x2))


def neg_expm1(x):
    series = x * (1.0 + x * (1 / 2) * (1.0 + x * (1 / 3) * (1.0 + x * (1 / 4) * (1.0 + x * (1 / 5) * (1.0 + x * (1 / 6))))))
    return jnp.where(x > -0.5, -series, 1.0 - jnp.exp(x))


class Sizes:
    def __init__(self, n, width, lru, ff, rows):
        self.n, self.d, self.rows = n, width, rows
        self.w = lru // n
        self.h = ff // n
        self.hp = up_to(self.h, 128)
        self.heads = self.w // DH
        self.cap = rows // n
        d, w, hp = width, self.w, self.hp
        self.rec = {}
        at = 0
        for name, size in (
            ("db", d), ("dg", d), ("dgates", n * w), ("dm", n * w),
            ("ub", n * w), ("ug", n * w), ("ugates", 2 * n * w), ("um", d),
        ):
            self.rec[name] = at
            at += size
        self.rec_used, self.rec_cols = at, up_to(at, 128 * PLANE)
        self.ffn = {}
        at = 0
        for name, size in (("dfg", d), ("dfu", d), ("dfd", n * hp), ("ufg", n * hp), ("ufu", n * hp), ("ufd", d)):
            self.ffn[name] = at
            at += size
        self.ffn_used, self.ffn_cols = at, up_to(at, 128 * PLANE)


def item(k, s, n):
    m = jnp.minimum(s, n - 1 - s)
    paired = k <= 2 * m
    t = jnp.where(paired, (k + 1) // 2, k - m)
    below = jnp.where(paired, k % 2 == 1, s > n - 1 - s)
    return jnp.where(below, s - t, s + t), below


def remote(src, dst, send, recv, device):
    return pltpu.make_async_remote_copy(src, dst, send, recv, device_id=device, device_id_type=MESH_ID)


def gather_kernel(n, geo, groups, *refs):
    na = len(geo)
    src, toks, sm = refs[:na], refs[na : na + 2], refs[na + 2]
    refs = refs[na + 3 :]
    dst, rtok, rsm = refs[:na], refs[na : na + 2], refs[na + 2]
    sz, sp, rz, rp, tsem, trsem = refs[na + 3 :]
    rep, s = lax.axis_index("rep"), lax.axis_index("shard")
    p = rep % PLANE

    def flip(bit):
        return rep + bit * (1 - 2 * ((rep // bit) % 2))

    def dev(r, z):
        return {"rep": r, "shard": z}

    barrier = pltpu.get_barrier_semaphore()
    for bit in (1, 2, 4):
        pl.semaphore_signal(barrier, inc=1, device_id=dev(flip(bit), s), device_id_type=MESH_ID)
    for r in range(1, n):
        pl.semaphore_signal(barrier, inc=1, device_id=dev(rep, lax.rem(s + r, n)), device_id_type=MESH_ID)
    pl.semaphore_wait(barrier, 3 + n - 1)

    def part(view, a, q):
        axis, size = geo[a]
        if axis == 0:
            return view.at[pl.ds(pl.multiple_of(q * size, 8), size)]
        return view.at[:, pl.ds(pl.multiple_of(q * size, 128), size)]

    def own(a):
        @pl.when(s < n - 1)
        def _():
            remote(part(src[a], a, p), part(dst[a].at[s], a, p), sz.at[0, a], rz.at[a, s], dev(rep, s + 1)).start()

        @pl.when(s > 0)
        def _():
            remote(part(src[a], a, p), part(dst[a].at[s], a, p), sz.at[1, a], rz.at[a, s], dev(rep, s - 1)).start()

    def own_wait(a):
        @pl.when(s < n - 1)
        def _():
            remote(part(src[a], a, p), part(dst[a].at[s], a, p), sz.at[0, a], rz.at[a, s], dev(rep, s + 1)).wait_send()

        @pl.when(s > 0)
        def _():
            remote(part(src[a], a, p), part(dst[a].at[s], a, p), sz.at[1, a], rz.at[a, s], dev(rep, s - 1)).wait_send()

    pending = []

    def plane(a, j, k, kind, q, target):
        view = part(dst[a].at[j], a, q)
        copy = remote(view, view, sp.at[kind, a, k - 1], rp.at[kind, a, j], dev(target, s))
        copy.start()
        pending.append(copy)

    def plane_wait(a, j, kind, q):
        view = part(dst[a].at[j], a, q)
        remote(view, view, sp.at[kind, a, 0], rp.at[kind, a, j], dev(rep, s)).wait_recv()

    q1, q2, q4 = p + flip(1) - rep, p + flip(2) - rep, p + flip(4) - rep
    q6 = q4 + flip(2) - rep
    q3, q5, q7 = q1 + q2 - p, q1 + q4 - p, q1 + q6 - p

    def forward(a, k):
        j, below = item(k, s, n)
        target = jnp.where(below, s + 1, s - 1)
        view = part(dst[a].at[j], a, p)
        copy = remote(view, view, sz.at[1 + k, a], rz.at[a, j], dev(rep, jnp.clip(target, 0, n - 1)))
        return (target >= 0) & (target < n), copy

    def stage1(a, k):
        j, _ = item(k, s, n)
        view = part(dst[a].at[j], a, p)
        remote(view, view, sz.at[0, a], rz.at[a, j], dev(rep, s)).wait_recv()
        valid, copy = forward(a, k)
        pl.when(valid)(copy.start)
        plane(a, j, k, 0, p, flip(2))
        plane(a, j, k, 1, p, flip(4))
        plane(a, j, k, 3, p, flip(1))

    def stage2(a, k):
        j, _ = item(k, s, n)
        plane_wait(a, j, 0, q2)
        if (a + k) % 2:
            plane(a, j, k, 2, q2, flip(4))
        plane(a, j, k, 4, q2, flip(1))
        plane_wait(a, j, 1, q4)
        if (a + k) % 2 == 0:
            plane(a, j, k, 2, q4, flip(2))
        plane(a, j, k, 5, q4, flip(1))

    def stage3(a, k):
        j, _ = item(k, s, n)
        plane_wait(a, j, 2, q6)
        plane(a, j, k, 6, q6, flip(1))

    def stage4(a, k):
        j, _ = item(k, s, n)
        for kind, q in ((3, q1), (4, q3), (5, q5), (6, q7)):
            plane_wait(a, j, kind, q)

    def line(i, view_of, into):
        copies = []
        for r in range(1, n):
            d = lax.rem(s + r, n)
            copy = remote(view_of(d), into.at[s], tsem.at[i, r], trsem.at[i, s], dev(rep, d))
            copy.start()
            copies.append(copy)
        return copies

    def line_wait(i, copies, into):
        for copy in copies:
            copy.wait_send()
        for r in range(1, n):
            d = lax.rem(s + r, n)
            remote(into.at[d], into.at[d], tsem.at[i, r], trsem.at[i, d], dev(rep, d)).wait_recv()

    items = [(a, k) for g in groups for k in range(1, n) for a in g]
    order = [a for g in groups for a in g]
    ahead, first, second = 3, len(groups[0]), len(groups[1])
    keep = pltpu.make_async_copy(sm, rsm.at[s], tsem.at[2, 0])
    keep.start()
    for a in order[:ahead]:
        own(a)
    sent = {}
    for i in range(len(items) + 6):
        if i == 3:
            sent[2] = line(2, lambda d: sm, rsm)
            sent[0] = line(0, lambda d: toks[0].at[d], rtok[0])
        if i == first * (n - 1) + 3:
            sent[1] = line(1, lambda d: toks[1].at[d], rtok[1])
        if i < len(items):
            stage1(*items[i])
        if i + ahead < first:
            own(order[i + ahead])
        m = i - (first * (n - 1) - second - ahead)
        if 0 <= m < second:
            own(groups[1][m])
        if 0 <= i - 3 < len(items):
            stage2(*items[i - 3])
        if 0 <= i - 6 < len(items):
            stage3(*items[i - 6])
    for a, k in items:
        stage4(a, k)
    line_wait(2, sent[2], rsm)
    line_wait(0, sent[0], rtok[0])
    line_wait(1, sent[1], rtok[1])
    for copy in pending:
        copy.wait_send()
    for a in order:
        own_wait(a)
    for a, k in items:
        valid, copy = forward(a, k)
        pl.when(valid)(copy.wait_send)
    keep.wait()


def gather_all(z, arrays, axes, groups, toks, sm):
    n, na = z.n, len(arrays)
    geo = [(axis, x.shape[axis] // PLANE) for x, axis in zip(arrays, axes)]
    outs = [jax.ShapeDtypeStruct((n,) + x.shape, x.dtype) for x in arrays]
    outs += [jax.ShapeDtypeStruct(t.shape, t.dtype) for t in toks]
    outs += [jax.ShapeDtypeStruct((n,) + sm.shape, sm.dtype)]
    return pl.pallas_call(
        functools.partial(gather_kernel, n, geo, groups),
        out_shape=outs,
        in_specs=[ANY] * (na + 3),
        out_specs=[ANY] * len(outs),
        scratch_shapes=[
            DMA((2 + n, na)), DMA((7, na, n - 1)), DMA((na, n)), DMA((7, na, n)), DMA((3, n)), DMA((3, n)),
        ],
        compiler_params=pltpu.CompilerParams(collective_id=1, has_side_effects=True),
        name="gather",
    )(*arrays, *toks, sm)


def start_either(s, j, own, gathered, dst, sem):
    @pl.when(j == s)
    def _():
        pltpu.make_async_copy(own, dst, sem).start()

    @pl.when(j != s)
    def _():
        pltpu.make_async_copy(gathered, dst, sem).start()


def wide(mask, width):
    return jnp.tile(mask, (1, width // 128))


def scan_rows(a_ref, x_ref, out, width, reverse):
    groups = LIVE // 8
    a = a_ref[...].reshape(groups, 8, width)
    x = x_ref[...].reshape(groups, 8, width)
    row = lax.broadcasted_iota(jnp.int32, (groups, 8, width), 1)
    for step in (1, 2, 4):
        shift = 8 - step if reverse else step
        inside = row < 8 - step if reverse else row >= step
        am = jnp.where(inside, pltpu.roll(a, shift, 1), 1.0)
        xm = jnp.where(inside, pltpu.roll(x, shift, 1), 0.0)
        x = x + a * xm
        a = a * am
    a_ref[...] = a.reshape(LIVE, width)
    x_ref[...] = x.reshape(LIVE, width)
    edge = 0 if reverse else 7

    def body(i, carry):
        g = groups - 1 - i if reverse else i
        at = pl.ds(pl.multiple_of(g * 8, 8), 8)
        value = x_ref[at, :] + a_ref[at, :] * carry
        out[at, :] = value
        return jnp.broadcast_to(value[edge : edge + 1, :], (8, width))

    lax.fori_loop(0, groups, body, jnp.zeros((8, width), F32), unroll=4)


def norm_scale(values):
    return lax.rsqrt(jnp.mean(values * values, axis=-1, keepdims=True) + EPS)


def gain_row(smv, row, n, d):
    pieces = [smv[j, row : row + 1, : d // n].astype(F32) for j in range(n)]
    return jnp.concatenate(pieces, axis=1)


def gates_of(logits, z):
    heads = z.heads
    ig = jnp.concatenate([logits[:, 2 * i * DH : (2 * i + 1) * DH] for i in range(heads)], axis=1)
    rg = jnp.concatenate([logits[:, (2 * i + 1) * DH : (2 * i + 2) * DH] for i in range(heads)], axis=1)
    return jax.nn.sigmoid(ig), jax.nn.sigmoid(rg)


def decay_of(s32, rg, first):
    soft = DECAY * jnp.log1p(jnp.exp(-s32[5:6, :]))
    log_a = -rg * soft
    a = jnp.where(first, 0.0, jnp.exp(log_a))
    scale = jnp.where(first, 1.0, jnp.sqrt(neg_expm1(2.0 * log_a)))
    return soft, a, scale


def forward_kernel(z, *refs):
    n, w, d = z.n, z.w, z.d
    (ob, og, ogw, om, oadp, otok, gb, gg, ggw, gm, gadp, gtok, sm_r, gain1, gain2, perm_r, mask_r, pos_r,
     act1_o, act2_o, resid_o, mixed_o, ranks_o, xin_o, conv_o, gi_o, ig_o, rg_o, st_o,
     wb, wg, wgw, wm, adp, tok, acc, cl, sa, sx, sem) = refs
    s = lax.axis_index("shard")
    rows = NAR // n
    waits = []

    def fetch(own, gathered, dst, sm):
        start_either(s, fetch.j, own, gathered, dst, sm)
        waits.append((own, dst, sm))

    for j in range(n):
        fetch.j = j
        fetch(otok.at[j], gtok.at[j], tok.at[pl.ds(j * z.cap, z.cap)], sem.at[0, j])
        fetch(oadp, gadp.at[j], adp.at[pl.ds(j * rows, rows)], sem.at[1, j])
    for j in range(n):
        fetch.j = j
        fetch(ob, gb.at[j], wb.at[j], sem.at[2, j])
        fetch(og, gg.at[j], wg.at[j], sem.at[3, j])
    for j in range(n):
        fetch.j = j
        fetch(ogw, ggw.at[j], wgw.at[j], sem.at[4, j])
        fetch(om, gm.at[j], wm.at[j], sem.at[5, j])
    smv, mask = sm_r, mask_r[...]
    for own, dst, sm in waits[: 2 * n]:
        pltpu.make_async_copy(own, dst, sm).wait()
    xin = nn(perm_r[...], tok[...])
    xin_o[...] = xin.astype(BF16)
    gain = gain1[...]
    act1_o[...] = (xin * norm_scale(xin) * gain).astype(BF16)
    resid_o[...] = xin
    col = z.rec

    def cols(name, size, j=0):
        return pl.ds(pl.multiple_of(col[name] + j * size, 128), size)

    ranks_o[0] = (nt(act1_o[...], adp[:, cols("db", d)]) * mask).astype(BF16)
    ranks_o[1] = (nt(act1_o[...], adp[:, cols("dg", d)]) * mask).astype(BF16)
    acc[...] = jnp.zeros_like(acc)
    for own, dst, sm in waits[2 * n : 4 * n]:
        pltpu.make_async_copy(own, dst, sm).wait()

    def first_pass(j, carry):
        s32 = smv[j].astype(F32)
        gi_o[j] = nn(act1_o[...], wg[j]) + nn(ranks_o[1], adp[:, cols("ug", w, j)])
        br = nn(act1_o[...], wb[j]) + nn(ranks_o[0], adp[:, cols("ub", w, j)])
        pos = wide(pos_r[...], w)
        total = s32[4:5, :] + s32[0:1, :] * br
        for k in range(1, 4):
            total = total + jnp.where(pos >= k, pltpu.roll(br, k, 0), 0.0) * s32[k : k + 1, :]
        conv_o[j] = total
        cl[j] = total.astype(BF16)
        acc[...] += nt(cl[j], adp[:, cols("dgates", w, j)])
        return carry

    lax.fori_loop(0, n, first_pass, 0)
    ranks_o[2] = (acc[...] * mask).astype(BF16)
    acc[...] = jnp.zeros_like(acc)
    for own, dst, sm in waits[4 * n :]:
        pltpu.make_async_copy(own, dst, sm).wait()

    def second_pass(j, carry):
        s32 = smv[j].astype(F32)
        low = cl[j]
        lift = nn(ranks_o[2], adp[:, cols("ugates", 2 * w, j)])
        bias = jnp.concatenate([s32[6:7, :], s32[7:8, :]], axis=1)
        logits = jnp.concatenate(
            [nn(low[:, i * DH : (i + 1) * DH], wgw[j, i * DH : (i + 1) * DH, :]) for i in range(z.heads)], axis=1
        ) + bias + lift
        ig, rg = gates_of(logits, z)
        first = wide(pos_r[...], w) == 0
        _, a, scale = decay_of(s32, rg, first)
        ig_o[j] = ig
        rg_o[j] = rg
        sa[...] = a
        sx[...] = scale * ig * conv_o[j]
        scan_rows(sa, sx, st_o.at[j], w, False)
        act, _ = gelu_parts(gi_o[j])
        mixed_o[j] = (st_o[j] * act).astype(BF16)
        acc[...] += nt(mixed_o[j], adp[:, cols("dm", w, j)])
        resid_o[...] += nn(mixed_o[j], wm[j])
        return carry

    lax.fori_loop(0, n, second_pass, 0)
    ranks_o[3] = (acc[...] * mask).astype(BF16)
    resid = resid_o[...] + nn(ranks_o[3], adp[:, cols("um", d)])
    resid_o[...] = resid
    act2_o[...] = (resid * norm_scale(resid) * gain2[...]).astype(BF16)


def forward_pass(z, own, gathered, tok_own, tok_all, sm, gain1, gain2, perm, mask, pos):
    n, w, d = z.n, z.w, z.d
    S = jax.ShapeDtypeStruct
    outs = [S((LIVE, d), BF16), S((LIVE, d), BF16), S((LIVE, d), F32), S((n, LIVE, w), BF16), S((4, LIVE, NAR), BF16)]
    outs += [S((LIVE, d), BF16)] + [S((n, LIVE, w), F32)] * 5
    return pl.pallas_call(
        functools.partial(forward_kernel, z),
        out_shape=outs,
        in_specs=[ANY] * 12 + [VM] * 6,
        out_specs=[VM] * len(outs),
        scratch_shapes=[
            pltpu.VMEM((n, d, w), BF16), pltpu.VMEM((n, d, w), BF16), pltpu.VMEM((n, w, 2 * DH), BF16),
            pltpu.VMEM((n, w, d), BF16), pltpu.VMEM((NAR, z.rec_cols), BF16), pltpu.VMEM((z.rows, d), BF16),
            pltpu.VMEM((LIVE, NAR), F32), pltpu.VMEM((n, LIVE, w), BF16),
            pltpu.VMEM((LIVE, w), F32), pltpu.VMEM((LIVE, w), F32), DMA((6, n)),
        ],
        compiler_params=pltpu.CompilerParams(vmem_limit_bytes=VLIMIT),
        name="forward",
    )(*own, tok_own, *gathered, tok_all, sm, gain1, gain2, perm, mask, pos)


def feed_kernel(z, *refs):
    n, d, h, hp = z.n, z.d, z.h, z.hp
    (ofg, ofu, ofd, oadp, ocot, gfg, gfu, gfd, gadp, gcot, perm_r, mask_r, gain2, act2, resid,
     out_o, gres_o, grad_o,
     wg, wu, wd, adp, tok, gl, acc_o, acc_g, rk, ra, sem, wsem) = refs
    s = lax.axis_index("shard")
    rows = NAR // n
    col = z.ffn

    def cols(name, size, j=0, stride=0):
        return pl.ds(pl.multiple_of(col[name] + j * stride, 128), size)

    for j in range(n):
        start_either(s, j, ocot.at[j], gcot.at[j], tok.at[pl.ds(j * z.cap, z.cap)], sem.at[0, j])
        start_either(s, j, oadp, gadp.at[j], adp.at[pl.ds(j * rows, rows)], sem.at[1, j])

    def load(j, slot):
        start_either(s, j, ofg, gfg.at[j], wg.at[slot], wsem.at[slot, 0])
        start_either(s, j, ofu, gfu.at[j], wu.at[slot], wsem.at[slot, 1])
        start_either(s, j, ofd, gfd.at[j], wd.at[slot], wsem.at[slot, 2])

    load(jnp.int32(0), 0)
    mask = mask_r[...]
    for j in range(n):
        pltpu.make_async_copy(ocot.at[j], tok.at[pl.ds(j * z.cap, z.cap)], sem.at[0, j]).wait()
        pltpu.make_async_copy(oadp, adp.at[pl.ds(j * rows, rows)], sem.at[1, j]).wait()
    gl[...] = nn(perm_r[...], tok[...]).astype(BF16)
    rk[0] = (nt(act2[...], adp[:, cols("dfg", d)]) * mask).astype(BF16)
    rk[1] = (nt(act2[...], adp[:, cols("dfu", d)]) * mask).astype(BF16)
    rk[2] = (nt(gl[...], adp[:, cols("ufd", d)]) * mask).astype(BF16)
    acc_o[...] = jnp.zeros_like(acc_o)
    acc_g[...] = jnp.zeros_like(acc_g)
    ra[...] = jnp.zeros_like(ra)

    def step(j, carry):
        slot = lax.rem(j, 2)
        pltpu.make_async_copy(ofg, wg.at[slot], wsem.at[slot, 0]).wait()
        pltpu.make_async_copy(ofu, wu.at[slot], wsem.at[slot, 1]).wait()
        pltpu.make_async_copy(ofd, wd.at[slot], wsem.at[slot, 2]).wait()

        @pl.when(j + 1 < n)
        def _():
            load(j + 1, 1 - slot)

        fg, fu, fd = cols("ufg", h, j, hp), cols("ufu", h, j, hp), cols("dfd", h, j, hp)
        hg = nn(act2[...], wg[slot]) + nn(rk[0], adp[:, fg])
        hu = nn(act2[...], wu[slot]) + nn(rk[1], adp[:, fu])
        gh = nt(gl[...], wd[slot]) + nn(rk[2], adp[:, fd])
        act, slope = gelu_parts(hg)
        low = (act * hu).astype(BF16)
        ghg = (gh * hu * slope).astype(BF16)
        ghu = (gh * act).astype(BF16)
        acc_o[...] += nn(low, wd[slot])
        acc_g[...] += nt(ghg, wg[slot]) + nt(ghu, wu[slot])
        ra[0] += nt(low, adp[:, fd])
        ra[1] += nt(ghg, adp[:, fg])
        ra[2] += nt(ghu, adp[:, fu])
        grad_o[:, fd] = tn(rk[2], low).astype(BF16)
        grad_o[:, fg] = tn(rk[0], ghg).astype(BF16)
        grad_o[:, fu] = tn(rk[1], ghu).astype(BF16)
        return carry

    lax.fori_loop(0, n, step, 0)
    rank = (ra[0] * mask).astype(BF16)
    work = resid[...] + acc_o[...] + nn(rank, adp[:, cols("ufd", d)])
    out_o[...] = tn(perm_r[...], work.astype(BF16)).astype(BF16)
    grad_o[:, cols("ufd", d)] = tn(rank, gl[...]).astype(BF16)
    rank_g = (ra[1] * mask).astype(BF16)
    rank_u = (ra[2] * mask).astype(BF16)
    grad_o[:, cols("dfg", d)] = tn(rank_g, act2[...]).astype(BF16)
    grad_o[:, cols("dfu", d)] = tn(rank_u, act2[...]).astype(BF16)
    gact = acc_g[...] + nn(rank_g, adp[:, cols("dfg", d)]) + nn(rank_u, adp[:, cols("dfu", d)])
    gres_o[...] = gl[...].astype(F32) + norm_back(resid[...], gact * gain2[...])


def norm_back(values, u):
    scale = norm_scale(values)
    return scale * u - values * (scale * scale * scale * jnp.mean(u * values, axis=-1, keepdims=True))


def feed_pass(z, own, gathered, cot_own, cot_all, perm, mask, gain2, act2, resid):
    n, d, h = z.n, z.d, z.h
    S = jax.ShapeDtypeStruct
    outs = [S((z.rows, d), BF16), S((LIVE, d), F32), S((NAR, z.ffn_cols), BF16)]
    return pl.pallas_call(
        functools.partial(feed_kernel, z),
        out_shape=outs,
        in_specs=[ANY] * 10 + [VM] * 5,
        out_specs=[VM] * len(outs),
        scratch_shapes=[
            pltpu.VMEM((2, d, h), BF16), pltpu.VMEM((2, d, h), BF16), pltpu.VMEM((2, h, d), BF16),
            pltpu.VMEM((NAR, z.ffn_cols), BF16), pltpu.VMEM((z.rows, d), BF16), pltpu.VMEM((LIVE, d), BF16),
            pltpu.VMEM((LIVE, d), F32), pltpu.VMEM((LIVE, d), F32),
            pltpu.VMEM((3, LIVE, NAR), BF16), pltpu.VMEM((3, LIVE, NAR), F32), DMA((2, n)), DMA((2, 3)),
        ],
        compiler_params=pltpu.CompilerParams(vmem_limit_bytes=VLIMIT),
        name="feed",
    )(*own, cot_own, *gathered, cot_all, perm, mask, gain2, act2, resid)


def backward_kernel(z, *refs):
    n, w, d = z.n, z.w, z.d
    (ob, og, ogw, om, oadp, gb, gg, ggw, gm, gadp, conv_h, gi_h, ig_h, rg_h, st_h,
     sm_r, gain1, perm_r, mask_r, pos_r, act1, mixed, ranks, xin_tok, gres,
     out_o, grad_o,
     wb, wg, wgw, wm, adp, gdir, glow, gilow, accg, acc, rk, sa, sx, st2, sav, sem, ssem) = refs
    s = lax.axis_index("shard")
    rows = NAR // n
    col = z.rec

    def cols(name, size, j=0):
        return pl.ds(pl.multiple_of(col[name] + j * size, 128), size)

    saved = (conv_h, gi_h, ig_h, rg_h, st_h)

    def load(j, slot, count=5):
        for i, ref in enumerate(saved[:count]):
            pltpu.make_async_copy(ref.at[j], sav.at[slot, i], ssem.at[slot, i]).start()

    def load_wait(j, slot, count=5):
        for i, ref in enumerate(saved[:count]):
            pltpu.make_async_copy(ref.at[j], sav.at[slot, i], ssem.at[slot, i]).wait()

    for j in range(n):
        start_either(s, j, oadp, gadp.at[j], adp.at[pl.ds(j * rows, rows)], sem.at[0, j])

    def load_merge(j, slot):
        start_either(s, j, om, gm.at[j], wm.at[slot], sem.at[1, slot])

    load_merge(jnp.int32(0), 0)
    load(0, 0)
    def load_weights(j, slot):
        start_either(s, j, ogw, ggw.at[j], wgw.at[slot], sem.at[2, slot])
        start_either(s, j, ob, gb.at[j], wb.at[slot], sem.at[3, slot])
        start_either(s, j, og, gg.at[j], wg.at[slot], sem.at[4, slot])

    load_weights(jnp.int32(0), 0)
    mask = mask_r[...]
    for j in range(n):
        pltpu.make_async_copy(oadp, adp.at[pl.ds(j * rows, rows)], sem.at[0, j]).wait()
    glm = gres[...].astype(BF16)
    rk[0] = (nt(glm, adp[:, cols("um", d)]) * mask).astype(BF16)
    grad_o[:, cols("um", d)] = tn(ranks[3], glm).astype(BF16)
    acc[...] = jnp.zeros_like(acc)

    def first_pass(j, carry):
        slot = lax.rem(j, 2)
        load_wait(j, slot)
        pltpu.make_async_copy(om, wm.at[slot], sem.at[1, slot]).wait()

        @pl.when(j + 1 < n)
        def _():
            load(j + 1, 1 - slot)
            load_merge(j + 1, 1 - slot)

        s32 = sm_r[j].astype(F32)
        conv, ig, rg, st = sav[slot, 0], sav[slot, 2], sav[slot, 3], sav[slot, 4]
        glm = gres[...].astype(BF16)
        gmix = nt(glm, wm[slot]) + nn(rk[0], adp[:, cols("dm", w, j)])
        grad_o[:, cols("dm", w, j)] = tn(rk[0], mixed[j]).astype(BF16)
        act, slope = gelu_parts(sav[slot, 1])
        gilow[j] = (gmix * st * slope).astype(BF16)
        pos = wide(pos_r[...], w)
        first = pos == 0
        soft, a, scale = decay_of(s32, rg, first)
        last = lax.broadcasted_iota(jnp.int32, (LIVE, w), 0) == LIVE - 1
        sa[...] = jnp.where(last, 0.0, pltpu.roll(a, LIVE - 1, 0))
        sx[...] = gmix * act
        scan_rows(sa, sx, st2, w, True)
        total = st2[...]
        before = jnp.where(first, 0.0, pltpu.roll(st, 1, 0))
        drive = total * scale
        gdir[j] = drive * ig
        g_in = drive * conv
        g_scale = total * ig * conv
        g_log = jnp.where(first, 0.0, total * before * a - g_scale * a * a / scale)
        g_rec = -soft * g_log
        l_in = g_in * ig * (1.0 - ig)
        l_rec = g_rec * rg * (1.0 - rg)
        pieces = []
        for i in range(z.heads):
            pieces += [l_in[:, i * DH : (i + 1) * DH], l_rec[:, i * DH : (i + 1) * DH]]
        low = jnp.concatenate(pieces, axis=1).astype(BF16)
        glow[j] = low
        acc[...] += nt(low, adp[:, cols("ugates", 2 * w, j)])
        grad_o[:, cols("ugates", 2 * w, j)] = tn(ranks[2], low).astype(BF16)
        return carry

    lax.fori_loop(0, n, first_pass, 0)
    rk[1] = (acc[...] * mask).astype(BF16)
    load(0, 0, 1)
    accg[...] = jnp.zeros_like(accg)
    rk_f = (jnp.zeros((LIVE, NAR), F32),) * 2

    def second_pass(j, carry):
        to_branch, to_gelu = carry
        slot = lax.rem(j, 2)
        load_wait(j, slot, 1)
        pltpu.make_async_copy(ogw, wgw.at[slot], sem.at[2, slot]).wait()
        pltpu.make_async_copy(ob, wb.at[slot], sem.at[3, slot]).wait()
        pltpu.make_async_copy(og, wg.at[slot], sem.at[4, slot]).wait()

        @pl.when(j + 1 < n)
        def _():
            load(j + 1, 1 - slot, 1)
            load_weights(j + 1, 1 - slot)

        s32 = sm_r[j].astype(F32)
        conv_low = sav[slot, 0].astype(BF16)
        grad_o[:, cols("dgates", w, j)] = tn(rk[1], conv_low).astype(BF16)
        low = glow[j]
        heads = jnp.concatenate(
            [nt(low[:, 2 * i * DH : 2 * (i + 1) * DH], wgw[slot, i * DH : (i + 1) * DH, :]) for i in range(z.heads)], axis=1
        )
        gconv = gdir[j] + heads + nn(rk[1], adp[:, cols("dgates", w, j)])
        pos = wide(pos_r[...], w)
        gbr = gconv * s32[0:1, :]
        for k in range(1, 4):
            gbr = gbr + pltpu.roll(jnp.where(pos >= k, gconv, 0.0), LIVE - k, 0) * s32[k : k + 1, :]
        blow = gbr.astype(BF16)
        gil = gilow[j]
        grad_o[:, cols("ub", w, j)] = tn(ranks[0], blow).astype(BF16)
        grad_o[:, cols("ug", w, j)] = tn(ranks[1], gil).astype(BF16)
        accg[...] += nt(blow, wb[slot]) + nt(gil, wg[slot])
        return (
            to_branch + nt(blow, adp[:, cols("ub", w, j)]),
            to_gelu + nt(gil, adp[:, cols("ug", w, j)]),
        )

    to_branch, to_gelu = lax.fori_loop(0, n, second_pass, rk_f)
    rank_b = (to_branch * mask).astype(BF16)
    rank_g = (to_gelu * mask).astype(BF16)
    grad_o[:, cols("db", d)] = tn(rank_b, act1[...]).astype(BF16)
    grad_o[:, cols("dg", d)] = tn(rank_g, act1[...]).astype(BF16)
    gact = accg[...] + nn(rank_b, adp[:, cols("db", d)]) + nn(rank_g, adp[:, cols("dg", d)])
    xin = xin_tok[...].astype(F32)
    gwork = gres[...] + norm_back(xin, gact * gain1[...])
    out_o[...] = tn(perm_r[...], gwork.astype(BF16)).astype(BF16)


def backward_pass(z, own, gathered, saved, sm, gain1, perm, mask, pos, act1, mixed, ranks, xin, gres):
    n, w, d = z.n, z.w, z.d
    S = jax.ShapeDtypeStruct
    V = pltpu.VMEM
    outs = [S((z.rows, d), BF16), S((NAR, z.rec_cols), BF16)]
    return pl.pallas_call(
        functools.partial(backward_kernel, z),
        out_shape=outs,
        in_specs=[ANY] * 15 + [VM] * 10,
        out_specs=[VM] * 2,
        scratch_shapes=[
            V((2, d, w), BF16), V((2, d, w), BF16), V((2, w, 2 * DH), BF16), V((2, w, d), BF16),
            V((NAR, z.rec_cols), BF16), V((n, LIVE, w), F32), V((n, LIVE, 2 * w), BF16), V((n, LIVE, w), BF16),
            V((LIVE, d), F32), V((LIVE, NAR), F32), V((2, LIVE, NAR), BF16),
            V((LIVE, w), F32), V((LIVE, w), F32), V((LIVE, w), F32), V((2, 5, LIVE, w), F32),
            DMA((5, n)), DMA((2, 5)),
        ],
        compiler_params=pltpu.CompilerParams(vmem_limit_bytes=VLIMIT),
        name="backward",
    )(*own, *gathered, *saved, sm, gain1, perm, mask, pos, act1, mixed, ranks, xin, gres)


def reduce_kernel(n, clusters, widths, *refs):
    grads, backs = refs[:2], refs[2:4]
    fins, rbacks = refs[4:6], refs[6:8]
    scratch = refs[8:]
    bufs = [SimpleNamespace(**dict(zip(("rc", "buf", "r1", "own1", "r2", "own2", "rg", "rz", "fin"), scratch[9 * t : 9 * t + 9]))) for t in range(2)]
    ssem, rsem, zs, zr, gs, gr, ps, pr, ts, tr = scratch[18:]
    rep, s = lax.axis_index("rep"), lax.axis_index("shard")
    p = rep % PLANE
    core, x, y = p % 2, (p // 2) % 2, p // 4
    rows = NAR // n
    half = NAR // 2

    def flip(bit):
        return rep + bit * (1 - 2 * ((rep // bit) % 2))

    def dev(r, place):
        return {"rep": r, "shard": place}

    barrier = pltpu.get_barrier_semaphore()
    for bit in (1, 2, 4):
        pl.semaphore_signal(barrier, inc=1, device_id=dev(flip(bit), s), device_id_type=MESH_ID)
    for r in range(1, n):
        pl.semaphore_signal(barrier, inc=1, device_id=dev(rep, lax.rem(s + r, n)), device_id_type=MESH_ID)
    for r in range(1, clusters):
        pl.semaphore_signal(barrier, inc=1, device_id=dev(lax.rem(rep + r * PLANE, clusters * PLANE), s), device_id_type=MESH_ID)
    pl.semaphore_wait(barrier, 3 + n - 1 + clusters - 1)
    pending = []

    def send(src, dst, a, b, target):
        copy = remote(src, dst, a, b, target)
        copy.start()
        pending.append(copy)

    def arrived(dst, a, b):
        remote(dst, dst, a, b, dev(rep, s)).wait_recv()

    def cut(t, q):
        return pl.ds(pl.multiple_of(q * widths[t], 128), widths[t])

    def returns(i):
        for r in range(1, n):
            d = lax.rem(s + r, n)
            send(backs[i].at[d], rbacks[i].at[s], ts.at[i, r], tr.at[i, s], dev(rep, d))

    def to_core(t):
        for c in range(4):
            send(grads[t].at[:, cut(t, 2 * c + 1 - core)], bufs[t].rc.at[c], ssem.at[t, c], rsem.at[t, c], dev(flip(1), s))

    def to_first(t):
        b = bufs[t]
        for c in range(4):
            arrived(b.rc.at[c], ssem.at[t, c], rsem.at[t, c])
            b.buf[c] = (grads[t][:, cut(t, 2 * c + core)].astype(F32) + b.rc[c].astype(F32)).astype(BF16)
        for i in range(2):
            send(b.buf.at[2 * i + 1 - x, pl.ds(0, half)], b.r1.at[0, i], ssem.at[t, 4 + i], rsem.at[t, 4 + i], dev(flip(2), s))
            send(b.buf.at[2 * (1 - y) + i, pl.ds(half, half)], b.r1.at[1, i], ssem.at[t, 6 + i], rsem.at[t, 6 + i], dev(flip(4), s))

    def to_second(t):
        b = bufs[t]
        for i in range(2):
            arrived(b.r1.at[0, i], ssem.at[t, 4 + i], rsem.at[t, 4 + i])
            b.own1[0, i] = (b.buf[2 * i + x, pl.ds(0, half)].astype(F32) + b.r1[0, i].astype(F32)).astype(BF16)
            arrived(b.r1.at[1, i], ssem.at[t, 6 + i], rsem.at[t, 6 + i])
            b.own1[1, i] = (b.buf[2 * y + i, pl.ds(half, half)].astype(F32) + b.r1[1, i].astype(F32)).astype(BF16)
        send(b.own1.at[0, 1 - y], b.r2.at[0], ssem.at[t, 8], rsem.at[t, 8], dev(flip(4), s))
        send(b.own1.at[1, 1 - x], b.r2.at[1], ssem.at[t, 9], rsem.at[t, 9], dev(flip(2), s))

    def to_line(t):
        b = bufs[t]
        arrived(b.r2.at[0], ssem.at[t, 8], rsem.at[t, 8])
        arrived(b.r2.at[1], ssem.at[t, 9], rsem.at[t, 9])
        b.own2[0, pl.ds(0, half)] = (b.own1[0, y].astype(F32) + b.r2[0].astype(F32)).astype(BF16)
        b.own2[0, pl.ds(half, half)] = (b.own1[1, x].astype(F32) + b.r2[1].astype(F32)).astype(BF16)
        if clusters > 1:
            mine = rep // PLANE
            for r in range(1, clusters):
                target = dev(lax.rem(rep + r * PLANE, clusters * PLANE), s)
                send(b.own2.at[0], b.rg.at[mine], gs.at[t, r], gr.at[t, mine], target)
            total = b.own2[0].astype(F32)
            for r in range(1, clusters):
                other = lax.rem(mine + r, clusters)
                arrived(b.rg.at[other], gs.at[t, r], gr.at[t, other])
                total = total + b.rg[other].astype(F32)
            b.own2[1] = total.astype(BF16)
        slot = 1 if clusters > 1 else 0
        for r in range(1, n):
            d = lax.rem(s + r, n)
            send(b.own2.at[slot, pl.ds(pl.multiple_of(d * rows, rows), rows)], b.rz.at[s], zs.at[t, r], zr.at[t, s], dev(rep, d))

    def to_plane(t):
        b = bufs[t]
        slot = 1 if clusters > 1 else 0
        total = b.own2[slot, pl.ds(pl.multiple_of(s * rows, rows), rows)].astype(F32)
        for r in range(1, n):
            d = lax.rem(s + r, n)
            arrived(b.rz.at[d], zs.at[t, r], zr.at[t, d])
            total = total + b.rz[d].astype(F32)
        b.fin[...] = total.astype(BF16)
        fins[t][:, cut(t, p)] = total.astype(BF16)
        spread(t, 0, p, flip(2), b.fin)
        spread(t, 1, p, flip(4), b.fin)
        spread(t, 3, p, flip(1), b.fin)

    def spread(t, kind, q, target, src=None):
        view = fins[t].at[:, cut(t, q)]
        send(view if src is None else src, view, ps.at[t, kind], pr.at[t, kind], dev(target, s))

    def spread_wait(t, kind, q):
        view = fins[t].at[:, cut(t, q)]
        arrived(view, ps.at[t, kind], pr.at[t, kind])

    q1, q2, q4 = p + flip(1) - rep, p + flip(2) - rep, p + flip(4) - rep
    q6 = q4 + flip(2) - rep
    q3, q5, q7 = q1 + q2 - p, q1 + q4 - p, q1 + q6 - p

    def across(t):
        spread_wait(t, 0, q2)
        if t == 0:
            spread(t, 2, q2, flip(4))
        spread(t, 4, q2, flip(1))
        spread_wait(t, 1, q4)
        if t == 1:
            spread(t, 2, q4, flip(2))
        spread(t, 5, q4, flip(1))

    def last(t):
        spread_wait(t, 2, q6)
        spread(t, 6, q6, flip(1))

    def end(t):
        for kind, q in ((3, q1), (4, q3), (5, q5), (6, q7)):
            spread_wait(t, kind, q)

    for i in range(2):
        returns(i)
    for step in (to_core, to_first, to_second, to_line, to_plane, across, last, end):
        for t in range(2):
            step(t)
    for i in range(2):
        for r in range(1, n):
            d = lax.rem(s + r, n)
            arrived(rbacks[i].at[d], ts.at[i, r], tr.at[i, d])
    for copy in pending:
        copy.wait_send()


def reduce_all(z, clusters, grads, backs):
    n = z.n
    rows, half = NAR // n, NAR // 2
    widths = [g.shape[1] // PLANE for g in grads]
    S = jax.ShapeDtypeStruct
    V = pltpu.VMEM
    outs = [S((rows, g.shape[1]), BF16) for g in grads] + [S(b.shape, b.dtype) for b in backs]
    scratch = []
    for c in widths:
        scratch += [
            V((4, NAR, c), BF16), V((4, NAR, c), BF16), V((2, 2, half, c), BF16), V((2, 2, half, c), BF16),
            V((2, half, c), BF16), V((2, NAR, c), BF16), V((max(clusters, 1), NAR, c), BF16), V((n, rows, c), BF16),
            V((rows, c), BF16),
        ]
    scratch += [DMA((2, 10)), DMA((2, 10)), DMA((2, n)), DMA((2, n)), DMA((2, clusters)), DMA((2, clusters)), DMA((2, 7)), DMA((2, 7)), DMA((2, n)), DMA((2, n))]
    return pl.pallas_call(
        functools.partial(reduce_kernel, n, clusters, widths),
        out_shape=outs,
        in_specs=[VM, VM, ANY, ANY],
        out_specs=[VM, VM, ANY, ANY],
        scratch_shapes=scratch,
        compiler_params=pltpu.CompilerParams(collective_id=2, has_side_effects=True, vmem_limit_bytes=VLIMIT),
        name="reduce",
    )(*grads, *backs)


def positions(lengths_row, index_row):
    ends = jnp.cumsum(lengths_row)
    starts = ends - lengths_row
    slots = jnp.arange(LIVE, dtype=jnp.int32)
    segment = jnp.sum((slots[:, None] >= ends[None, :]).astype(jnp.int32), axis=1)
    member = segment[:, None] == jnp.arange(lengths_row.shape[0], dtype=jnp.int32)[None, :]
    position = slots - jnp.sum(jnp.where(member, starts[None, :], 0), axis=1)
    chosen = jnp.sum(jnp.where(member, index_row[None, :], 0), axis=1)
    live = segment < lengths_row.shape[0]
    lanes = jnp.arange(NAR, dtype=jnp.int32) // R
    mask = ((chosen[:, None] == lanes[None, :]) & live[:, None]).astype(F32)
    return jnp.broadcast_to(position[:, None], (LIVE, NAR)), mask


def permutations(deal_row, s, n, rows):
    cap = rows // n
    deal = deal_row.reshape(n, rows)
    source = deal // rows
    slots = jnp.arange(rows, dtype=jnp.int32)
    earlier = slots[None, :] < slots[:, None]

    def rank_of(src):
        return jnp.sum((earlier[None] & (src[:, None, :] == src[:, :, None])).astype(jnp.int32), axis=2)

    rank = rank_of(source)
    mine = lax.dynamic_index_in_dim(source * cap + rank, s, 0, False)[:LIVE]
    collect = (mine[:, None] == jnp.arange(rows, dtype=jnp.int32)[None, :]).astype(BF16)
    local = deal - s * rows
    wanted = jnp.arange(cap, dtype=jnp.int32)
    hit = (source == s)[:, :, None] & (rank[:, :, None] == wanted[None, None, :])
    row = jnp.sum(jnp.where(hit, local[:, :, None], 0), axis=1).reshape(rows)
    deal_out = (row[:, None] == jnp.arange(rows, dtype=jnp.int32)[None, :]).astype(BF16)
    return collect, deal_out


def local(
    tokens, cotangent, norm_first, branch_weight, gelu_weight, conv_weight, conv_bias, gate_weight, gate_bias,
    decay_param, merge_weight, norm_second, feed_gate, feed_up, feed_down, down_branch, up_branch, down_gelu,
    up_gelu, down_gates, up_gates, down_merge, up_merge, down_feed_gate, up_feed_gate, down_feed_up, up_feed_up,
    down_feed_down, up_feed_down, seq_lengths, adapter_index, deal_order,
):
    n = lax.axis_size("shard")
    s = lax.axis_index("shard")
    clusters = lax.axis_size("rep") // PLANE
    rows, d = tokens.shape
    z = Sizes(n, d, branch_weight.shape[1] * n, feed_gate.shape[1] * n, rows)
    collect, deal_out = permutations(deal_order[0], s, n, rows)
    pos, mask = positions(seq_lengths[0], adapter_index[0])

    def send_rows(values):
        return nn(deal_out, values).astype(BF16).reshape(n, z.cap, d)

    tok_own, cot_own = send_rows(tokens), send_rows(cotangent)
    pad = z.hp - z.h

    def spaced(values):
        if pad == 0:
            return values
        parts = values.reshape(values.shape[0], n, z.h)
        return jnp.pad(parts, ((0, 0), (0, 0), (0, pad))).reshape(values.shape[0], n * z.hp)

    def packed(pieces, width):
        used = sum(x.shape[1] for x in pieces)
        pieces = list(pieces)
        if width > used:
            pieces.append(jnp.zeros((pieces[0].shape[0], width - used), BF16))
        return jnp.concatenate(pieces, axis=1)

    rec_own = packed(
        (down_branch.T, down_gelu.T, down_gates.T, down_merge.T, up_branch, up_gelu, up_gates, up_merge), z.rec_cols
    )
    ffn_own = packed(
        (down_feed_gate.T, down_feed_up.T, spaced(down_feed_down.T), spaced(up_feed_gate), spaced(up_feed_up), up_feed_down),
        z.ffn_cols,
    )
    w = z.w

    def gain(values):
        return jnp.pad(values, (0, w - values.shape[0]))[None]

    small = jnp.concatenate(
        [conv_weight, conv_bias[None], decay_param[None], gate_bias.reshape(2, w), gain(norm_first), gain(norm_second)], axis=0
    )
    small = jnp.pad(small, ((0, 16 - small.shape[0]), (0, 0)))
    gates = gate_weight.reshape(w, 2 * DH)
    arrays = [branch_weight, gelu_weight, gates, rec_own, merge_weight, feed_gate, feed_up, ffn_own, feed_down]
    axes = [0, 0, 0, 1, 0, 0, 0, 1, 0]
    got = gather_all(z, arrays, axes, [[0, 1, 2, 3, 4], [5, 6, 7, 8]], [tok_own, cot_own], small)
    branch_all, gelu_all, gates_all, rec_all, merge_all, fg_all, fu_all, ffn_all, fd_all, tok_all, cot_all, sm = got
    gain1 = sm[:, 8, : d // n].reshape(1, d).astype(F32)
    gain2 = sm[:, 9, : d // n].reshape(1, d).astype(F32)
    own = (branch_weight, gelu_weight, gates, merge_weight, rec_own)
    gathered = (branch_all, gelu_all, gates_all, merge_all, rec_all)
    act1, act2, resid, mixed, ranks, xin, *saved = forward_pass(
        z, own, gathered, tok_own, tok_all, sm, gain1, gain2, collect, mask, pos
    )
    out_send, gres, grad_ffn = feed_pass(
        z, (feed_gate, feed_up, feed_down, ffn_own), (fg_all, fu_all, fd_all, ffn_all), cot_own, cot_all,
        collect, mask, gain2, act2, resid,
    )
    tok_send, grad_rec = backward_pass(
        z, own, gathered, saved, sm, gain1, collect, mask, pos, act1, mixed, ranks, xin, gres
    )
    backs = [out_send.reshape(n, z.cap, d), tok_send.reshape(n, z.cap, d)]
    fin_ffn, fin_rec, back_out, back_tok = reduce_all(z, clusters, [grad_ffn, grad_rec], backs)

    def arrival(sent, received):
        own_block = lax.dynamic_index_in_dim(sent, s, 0, True)
        whole = lax.dynamic_update_slice_in_dim(received, own_block, s, 0)
        return tn(deal_out, whole.reshape(rows, d))

    def take(values, name, size):
        at = (z.rec if values is fin_rec else z.ffn)[name]
        return values[:, at : at + size].astype(F32)

    def unspaced(values):
        if pad == 0:
            return values
        return values.reshape(values.shape[0], n, z.hp)[:, :, : z.h].reshape(values.shape[0], n * z.h)

    lru, ffp = n * w, n * z.hp
    return (
        arrival(backs[0], back_out),
        arrival(backs[1], back_tok),
        take(fin_rec, "db", d).T,
        take(fin_rec, "ub", lru),
        take(fin_rec, "dg", d).T,
        take(fin_rec, "ug", lru),
        take(fin_rec, "dgates", lru).T,
        take(fin_rec, "ugates", 2 * lru),
        take(fin_rec, "dm", lru).T,
        take(fin_rec, "um", d),
        take(fin_ffn, "dfg", d).T,
        unspaced(take(fin_ffn, "ufg", ffp)),
        take(fin_ffn, "dfu", d).T,
        unspaced(take(fin_ffn, "ufu", ffp)),
        unspaced(take(fin_ffn, "dfd", ffp)).T,
        take(fin_ffn, "ufd", d),
    )


def solution(mesh):
    tok, line, col, row = P(("rep", "shard"), None), P("shard"), P(None, "shard"), P("shard", None)
    in_specs = (
        tok, tok, line, col, col, col, line, P("shard", None, None), row, line, row, line, col, col, row,
    ) + (col, row) * 7 + (tok, tok, P("rep", None))
    out_specs = (tok, tok) + (col, row) * 7
    return jax.shard_map(local, mesh=mesh, in_specs=in_specs, out_specs=out_specs, check_vma=False)
```

```python
import functools

import jax
import jax.numpy as jnp
from jax import lax
from jax.experimental import pallas as pl
from jax.experimental.pallas import tpu as pltpu
from jax.sharding import PartitionSpec as P

NA = 8
R = 16
NAR = NA * R
DH = 128
LIVE = 384
PLANE = 8
EPS = 1e-06
DECAY = 8.0
F32 = jnp.float32
BF16 = jnp.bfloat16
MESH_ID = pl.DeviceIdType.MESH
DMA = pltpu.SemaphoreType.DMA
ANY = pl.BlockSpec(memory_space=pl.ANY)
VM = pl.BlockSpec(memory_space=pltpu.VMEM)
VLIMIT = 60 << 20
GC = 0.7978845608028654
GA = 0.044715


def up_to(size, step):
    return -(-size // step) * step


def nn(a, b):
    return lax.dot_general(a, b, (((1,), (0,)), ((), ())), preferred_element_type=F32)


def nt(a, b):
    return lax.dot_general(a, b, (((1,), (1,)), ((), ())), preferred_element_type=F32)


def tn(a, b):
    return lax.dot_general(a, b, (((0,), (0,)), ((), ())), preferred_element_type=F32)


def gelu_parts(x):
    x2 = x * x
    th = jnp.tanh(GC * x * (1.0 + GA * x2))
    half = 0.5 * (1.0 + th)
    return x * half, half + 0.5 * x * (1.0 - th * th) * (GC * (1.0 + 3.0 * GA * x2))


def neg_expm1(x):
    series = x * (1.0 + x * (1 / 2) * (1.0 + x * (1 / 3) * (1.0 + x * (1 / 4) * (1.0 + x * (1 / 5) * (1.0 + x * (1 / 6))))))
    return jnp.where(x > -0.5, -series, 1.0 - jnp.exp(x))


class Sizes:
    def __init__(self, n, width, lru, ff, rows):
        self.n, self.d, self.rows = n, width, rows
        self.w = lru // n
        self.h = ff // n
        self.hp = up_to(self.h, 128)
        self.heads = self.w // DH
        self.cap = rows // n
        d, w, hp = width, self.w, self.hp
        self.rec = {}
        at = 0
        for name, size in (
            ("db", d), ("dg", d), ("dgates", n * w), ("dm", n * w),
            ("ub", n * w), ("ug", n * w), ("ugates", 2 * n * w), ("um", d),
        ):
            self.rec[name] = at
            at += size
        self.rec_used, self.rec_cols = at, up_to(at, 128 * PLANE)
        self.ffn = {}
        at = 0
        for name, size in (("dfg", d), ("dfu", d), ("dfd", n * hp), ("ufg", n * hp), ("ufu", n * hp), ("ufd", d)):
            self.ffn[name] = at
            at += size
        self.ffn_used, self.ffn_cols = at, up_to(at, 128 * PLANE)


def item(k, s, n):
    m = jnp.minimum(s, n - 1 - s)
    paired = k <= 2 * m
    t = jnp.where(paired, (k + 1) // 2, k - m)
    below = jnp.where(paired, k % 2 == 1, s > n - 1 - s)
    return jnp.where(below, s - t, s + t), below


def remote(src, dst, send, recv, device):
    return pltpu.make_async_remote_copy(src, dst, send, recv, device_id=device, device_id_type=MESH_ID)


def start_either(s, j, own, gathered, dst, sem):
    @pl.when(j == s)
    def _():
        pltpu.make_async_copy(own, dst, sem).start()

    @pl.when(j != s)
    def _():
        pltpu.make_async_copy(gathered, dst, sem).start()


def wide(mask, width):
    return jnp.tile(mask, (1, width // 128))


BLOCK = 32


def scan_block(a, x, carry, reverse):
    rows, width = a.shape
    groups = rows // 8
    a, x = a.reshape(groups, 8, width), x.reshape(groups, 8, width)
    row = lax.broadcasted_iota(jnp.int32, (groups, 8, width), 1)
    for step in (1, 2, 4):
        shift = 8 - step if reverse else step
        inside = row < 8 - step if reverse else row >= step
        x = x + a * jnp.where(inside, pltpu.roll(x, shift, 1), 0.0)
        a = a * jnp.where(inside, pltpu.roll(a, shift, 1), 1.0)
    order = range(groups - 1, -1, -1) if reverse else range(groups)
    edge, far, back = (0, 7, 7) if reverse else (7, 0, 1)
    line = lax.broadcasted_iota(jnp.int32, (8, width), 0)
    values, beside = [None] * groups, [None] * groups
    for g in order:
        value = x[g] + a[g] * carry
        values[g] = value
        beside[g] = jnp.where(line == far, carry, pltpu.roll(value, back, 0))
        carry = jnp.broadcast_to(value[edge : edge + 1, :], (8, width))
    return jnp.concatenate(values, axis=0), jnp.concatenate(beside, axis=0), carry


def norm_scale(values):
    return lax.rsqrt(jnp.mean(values * values, axis=-1, keepdims=True) + EPS)


def gain_row(smv, row, n, d):
    pieces = [smv[j, row : row + 1, : d // n].astype(F32) for j in range(n)]
    return jnp.concatenate(pieces, axis=1)


def gates_of(logits, z):
    heads = z.heads
    ig = jnp.concatenate([logits[:, 2 * i * DH : (2 * i + 1) * DH] for i in range(heads)], axis=1)
    rg = jnp.concatenate([logits[:, (2 * i + 1) * DH : (2 * i + 2) * DH] for i in range(heads)], axis=1)
    return jax.nn.sigmoid(ig), jax.nn.sigmoid(rg)


def decay_of(s32, rg, first):
    soft = DECAY * jnp.log1p(jnp.exp(-s32[5:6, :]))
    log_a = -rg * soft
    a = jnp.where(first, 0.0, jnp.exp(log_a))
    scale = jnp.where(first, 1.0, jnp.sqrt(neg_expm1(2.0 * log_a)))
    return soft, a, scale


def norm_back(values, u):
    scale = norm_scale(values)
    return scale * u - values * (scale * scale * scale * jnp.mean(u * values, axis=-1, keepdims=True))


class Plane:
    def __init__(self, n):
        self.n = n
        self.rep, self.s = lax.axis_index("rep"), lax.axis_index("shard")
        self.p = p = self.rep % PLANE
        self.q1, self.q2, self.q4 = p + self.flip(1) - self.rep, p + self.flip(2) - self.rep, p + self.flip(4) - self.rep
        self.q6 = self.q4 + self.flip(2) - self.rep
        self.q3, self.q5, self.q7 = self.q1 + self.q2 - p, self.q1 + self.q4 - p, self.q1 + self.q6 - p

    def flip(self, bit):
        return self.rep + bit * (1 - 2 * ((self.rep // bit) % 2))

    def across(self, bit):
        return {"rep": self.flip(bit), "shard": self.s}

    def along(self, place):
        return {"rep": self.rep, "shard": place}

    def greet(self, clusters=1):
        barrier = pltpu.get_barrier_semaphore()
        for bit in (1, 2, 4):
            pl.semaphore_signal(barrier, inc=1, device_id=self.across(bit), device_id_type=MESH_ID)
        for r in range(1, self.n):
            pl.semaphore_signal(barrier, inc=1, device_id=self.along(lax.rem(self.s + r, self.n)), device_id_type=MESH_ID)
        for r in range(1, clusters):
            other = {"rep": lax.rem(self.rep + r * PLANE, clusters * PLANE), "shard": self.s}
            pl.semaphore_signal(barrier, inc=1, device_id=other, device_id_type=MESH_ID)
        pl.semaphore_wait(barrier, 3 + self.n - 1 + clusters - 1)


class Gather:
    def __init__(self, at, geo, src, dst, sz, sp, rz, rp):
        self.at, self.geo, self.src, self.dst = at, geo, src, dst
        self.sz, self.sp, self.rz, self.rp = sz, sp, rz, rp

    def cut(self, view, a, start, size):
        if self.geo[a][0] == 0:
            return view.at[pl.ds(pl.multiple_of(start, 8), size)]
        return view.at[:, pl.ds(pl.multiple_of(start, 128), size)]

    def part(self, view, a, q):
        size = self.geo[a][1]
        return self.cut(view, a, q * size, size)

    def got(self, a, j, q):
        return self.part(self.dst[a].at[j], a, q)

    def half(self, a, j, q, second):
        axis, size = self.geo[a]
        step = 8 if axis == 0 else 128
        first = (size // step + 1) // 2 * step
        if second:
            return self.cut(self.dst[a].at[j], a, q * size + first, size - first)
        return self.cut(self.dst[a].at[j], a, q * size, first)

    def own_copy(self, a, up):
        at = self.at
        to = at.s + 1 if up else at.s - 1
        return remote(
            self.part(self.src[a], a, at.p), self.got(a, at.s, at.p), self.sz.at[0 if up else 1, a], self.rz.at[a, at.s],
            at.along(jnp.clip(to, 0, at.n - 1)),
        )

    def own(self, a):
        pl.when(self.at.s < self.at.n - 1)(lambda: self.own_copy(a, True).start())
        pl.when(self.at.s > 0)(lambda: self.own_copy(a, False).start())

    def forward(self, a, t, up):
        at = self.at
        j = at.s - t if up else at.s + t
        to = at.s + 1 if up else at.s - 1
        came = (j >= 0) if up else (j < at.n)
        goes = (to < at.n) if up else (to >= 0)
        view = self.got(a, jnp.clip(j, 0, at.n - 1), at.p)
        sem = self.rz.at[a, jnp.clip(j, 0, at.n - 1)]
        copy = remote(view, view, self.sz.at[2 * t + (0 if up else 1), a], sem, at.along(jnp.clip(to, 0, at.n - 1)))
        return came, came & goes, copy

    def line(self, a, t):
        for up in (True, False):
            came, goes, copy = self.forward(a, t, up)
            pl.when(came)(lambda: copy.wait_recv())
            pl.when(goes)(lambda: self.forward(a, t, up)[2].start())

    def send(self, view, a, j, k, kind, bit):
        remote(view, view, self.sp.at[kind, a, k - 1], self.rp.at[kind, a, j], self.at.across(bit)).start()

    def wait(self, view, a, j, kind):
        remote(view, view, self.sp.at[kind, a, 0], self.rp.at[kind, a, j], self.at.across(1)).wait_recv()

    def place(self, k):
        return item(k, self.at.s, self.at.n)[0]

    def spread(self, a, k):
        j = self.place(k)
        view = self.got(a, j, self.at.p)
        self.send(view, a, j, k, 0, 2)
        self.send(view, a, j, k, 1, 4)
        self.send(view, a, j, k, 3, 1)

    def corner(self, a, k):
        at, j = self.at, self.place(k)
        from_x, from_y = self.got(a, j, at.q2), self.got(a, j, at.q4)
        self.wait(from_x, a, j, 0)
        self.send(self.half(a, j, at.q2, True), a, j, k, 7, 4)
        self.send(from_x, a, j, k, 4, 1)
        self.wait(from_y, a, j, 1)
        self.send(self.half(a, j, at.q4, False), a, j, k, 2, 2)
        self.send(from_y, a, j, k, 5, 1)

    def twin(self, a, k):
        at, j = self.at, self.place(k)
        self.wait(self.half(a, j, at.q6, False), a, j, 2)
        self.wait(self.half(a, j, at.q6, True), a, j, 7)
        self.send(self.got(a, j, at.q6), a, j, k, 6, 1)

    def ready(self, a, k):
        at, j = self.at, self.place(k)
        for kind, q in ((3, at.q1), (4, at.q3), (5, at.q5), (6, at.q7)):
            self.wait(self.got(a, j, q), a, j, kind)

    def drain(self):
        at = self.at
        for a in range(len(self.geo)):
            pl.when(at.s < at.n - 1)(lambda: self.own_copy(a, True).wait_send())
            pl.when(at.s > 0)(lambda: self.own_copy(a, False).wait_send())

            def body(k, carry):
                for up in (True, False):
                    _, goes, copy = self.forward(a, k, up)
                    pl.when(goes)(lambda: copy.wait_send())
                j = self.place(k)
                whole = self.got(a, j, at.p)
                for kind, view in (
                    (0, whole), (1, whole), (2, self.half(a, j, at.p, False)), (3, whole), (4, whole), (5, whole), (6, whole),
                    (7, self.half(a, j, at.p, True)),
                ):
                    remote(view, view, self.sp.at[kind, a, k - 1], self.rp.at[kind, a, j], at.across(1)).wait_send()
                return carry

            lax.fori_loop(1, at.n, body, 0)


class Line:
    def __init__(self, at, i, ssem, rsem):
        self.at, self.i, self.ssem, self.rsem = at, i, ssem, rsem

    def start(self, view_of, into, only=None):
        at = self.at
        self.into = into
        for r in range(1, at.n) if only is None else (only,):
            d = lax.rem(at.s + r, at.n)
            remote(view_of(d), into.at[at.s], self.ssem.at[self.i, r], self.rsem.at[self.i, at.s], at.along(d)).start()

    def arrived(self):
        at = self.at
        for r in range(1, at.n):
            d = lax.rem(at.s + r, at.n)
            view = self.into.at[d]
            remote(view, view, self.ssem.at[self.i, r], self.rsem.at[self.i, d], at.along(d)).wait_recv()

    def sent(self):
        view = self.into.at[0]
        for r in range(1, self.at.n):
            remote(view, view, self.ssem.at[self.i, r], self.rsem.at[self.i, 0], self.at.across(1)).wait_send()


def iota(shape, axis):
    return lax.broadcasted_iota(jnp.int32, shape, axis)


def one_hot(hit):
    return jnp.where(hit, 1.0, 0.0).astype(BF16)


def sources(deal, n, rows):
    src = jnp.zeros_like(deal)
    for k in range(1, n):
        src = src + jnp.where(deal >= k * rows, 1, 0)
    return src


def sending_order(deal_ref, s, n, rows):
    cap = rows // n
    before = one_hot(iota((rows, rows), 0) < iota((rows, rows), 1))
    deal = jnp.concatenate([deal_ref[:, b * rows : (b + 1) * rows] for b in range(n)], axis=0)
    if n < 8:
        deal = jnp.concatenate([deal, jnp.full((8 - n, rows), -1, jnp.int32)], axis=0)
    hit = (sources(deal, n, rows) == s) & (deal >= 0)
    rank = nn(one_hot(hit), before).astype(jnp.int32)
    place = jnp.where(hit, rank + iota(deal.shape, 0) * cap, -1)
    mine = deal - s * rows
    total = jnp.zeros((rows, rows), F32)
    row = iota((rows, rows), 0)
    for b in range(n):
        total = total + nt(one_hot(row == place[b : b + 1, :]), one_hot(row == mine[b : b + 1, :]))
    return total.astype(BF16)


def collecting_order(deal_ref, before, s, n, rows):
    cap = rows // n
    deal = deal_ref[:, pl.ds(pl.multiple_of(s * rows, 128), rows)]
    kind = iota((8, rows), 0)
    hit = jnp.broadcast_to(sources(deal, n, rows), (8, rows)) == kind
    rank = nn(one_hot(hit), before).astype(jnp.int32)
    place = jnp.sum(jnp.where(hit, rank + kind * cap, 0).astype(F32), axis=0, keepdims=True).astype(jnp.int32)
    return one_hot(iota((rows, LIVE), 0) == place[:, :LIVE])


def slots_of(len_ref, idx_ref, pos_ref, mask_ref):
    slot = iota((LIVE, NAR), 0)
    lane = iota((LIVE, NAR), 1)
    count = len_ref.shape[1]
    start = jnp.zeros((LIVE, NAR), jnp.int32)
    chosen = jnp.full((LIVE, NAR), idx_ref[0, 0], jnp.int32)
    end = jnp.int32(0)
    for i in range(count):
        end = end + len_ref[0, i]
        passed = slot >= end
        start = jnp.where(passed, end, start)
        chosen = jnp.where(passed, idx_ref[0, i + 1] if i + 1 < count else -1, chosen)
    pos_ref[...] = slot - start
    low = chosen * R
    mask_ref[...] = jnp.where((lane >= low) & (lane < low + R), 1.0, 0.0)


REC_PARTS = ("db", "dg", "dgates", "dm", "ub", "ug", "ugates", "um")
FFN_PARTS = ("dfg", "dfu", "dfd", "ufg", "ufu", "ufd")


def first_kernel(z, geo, *refs):
    n, w, d, h, hp = z.n, z.w, z.d, z.h, z.hp
    refs = list(refs)

    def take(count):
        out, refs[:count] = refs[:count], []
        return out

    len_r, idx_r, deal_r, small_r = take(4)
    tokens, cotangent = take(2)
    ob, og, ogw, om, ofg, ofu, ofd = take(7)
    pieces_r, pieces_f = take(8), take(6)
    gb, gg, ggw, gr, gm, gfg, gfu, gf, gfd = gathered = take(9)
    gtok, gcot, gsm = take(3)
    act1_h, xin_h, mixed_h, ranks_h, rt_h, s_h = take(6)
    conv_h, gi_h, ig_h, rg_h, st_h = take(5)
    out_h, gres_h, grad_h = take(3)
    pack_r, pack_f, rows_out, smv, s_v, rt_v, pos_r, mask_r, act1, resid, ranks = take(11)
    sz, sp, rz, rp, lss, lrs, lsem, psem, osem = take(9)
    at = Plane(n)
    s = at.s
    at.greet()
    net = Gather(at, geo, [ob, og, ogw, pack_r, om, ofg, ofu, pack_f, ofd], gathered, sz, sp, rz, rp)
    rec, ffn = [0, 1, 3, 2, 4], [5, 6, 8]
    net.own(0)
    net.own(1)
    packing = []
    for i, (dst, table, names, parts) in enumerate(((pack_r, z.rec, REC_PARTS, pieces_r), (pack_f, z.ffn, FFN_PARTS, pieces_f))):
        for k, (name, ref) in enumerate(zip(names, parts)):
            size = ref.shape[1]
            copy = pltpu.make_async_copy(ref, dst.at[:, table[name] : table[name] + size], psem.at[i, k])
            copy.start()
            packing.append(copy)
    smv[s] = small_r[...]
    lines = [Line(at, i, lss, lrs) for i in range(3)]
    lines[2].start(lambda place: small_r, gsm)
    for copy in packing:
        copy.wait()
    net.own(3)

    def sending(rows_in):
        toks = [pltpu.make_async_copy(ref, rows_in.at[i], lsem.at[0, i]) for i, ref in enumerate((tokens, cotangent))]
        for copy in toks:
            copy.start()
        order = sending_order(deal_r, s, n, z.rows)
        s_v[...] = order
        for i in range(2):
            toks[i].wait()
            rows_out[i] = nn(order, rows_in[i]).astype(BF16).reshape(n, z.cap, d)

    pl.run_scoped(sending, pltpu.VMEM((2, z.rows, d), BF16))
    before = one_hot(iota((z.rows, z.rows), 0) < iota((z.rows, z.rows), 1))
    rt_v[...] = collecting_order(deal_r, before, s, n, z.rows)
    slots_of(len_r, idx_r, pos_r, mask_r)
    outs = []

    def put(src, dst):
        copy = pltpu.make_async_copy(src, dst, osem.at[len(outs)])
        copy.start()
        outs.append(copy)

    put(s_v, s_h)
    put(rt_v, rt_h)
    put(pack_r, gr.at[s])
    put(small_r, gsm.at[s])
    items = [(a, k) for k in range(1, n) for a in rec] + [(7, k) for k in range(1, n)] + [(a, 1) for a in ffn]
    count = len(items)
    for i in range(count):
        if i in (4, 7, 10):
            for r in range(1, n):
                if (r - 1) % 3 == (4, 7, 10).index(i):
                    lines[0].start(lambda place: rows_out.at[0, place], gtok, r)
        if i >= count - 3:
            for r in range(1, n):
                if (r - 1) % 3 == i - count + 3:
                    lines[1].start(lambda place: rows_out.at[1, place], gcot, r)
        if i + 3 < len(rec):
            net.own(rec[i + 3])
        if i == len(rec):
            net.own(7)
        if 0 <= i - 9 < len(ffn):
            net.own(ffn[i - 9])
        net.line(*items[i])
        net.spread(*items[i])
        if i >= 2 and items[i - 2][0] not in ffn:
            net.corner(*items[i - 2])
        if i >= 4 and items[i - 4][0] not in ffn:
            net.twin(*items[i - 4])
    for i in range(count - 4, count):
        if items[i][0] not in ffn:
            net.twin(*items[i])
    for a, k in items:
        if a in rec:
            net.ready(a, k)
    lines[2].arrived()
    small_in = []
    for r in range(1, n):
        o = lax.rem(s + r, n)
        copy = pltpu.make_async_copy(gsm.at[o], smv.at[o], lsem.at[1, r])
        copy.start()
        small_in.append(copy)
    lines[0].arrived()
    mask = mask_r[...]

    def rows_of(i, got, into, sem):
        keep = into.at[pl.ds(pl.multiple_of(s * z.cap, 8), z.cap)]
        copies = [pltpu.make_async_copy(rows_out.at[i, s], keep, sem.at[0])]
        for r in range(1, n):
            o = lax.rem(s + r, n)
            copies.append(pltpu.make_async_copy(got.at[o], into.at[pl.ds(pl.multiple_of(o * z.cap, 8), z.cap)], sem.at[r]))
        for copy in copies:
            copy.start()
        for copy in copies:
            copy.wait()

    for copy in small_in:
        copy.wait()
    gain1, gain2 = gain_row(smv, 8, n, d), gain_row(smv, 9, n, d)

    def load_pack(pack, got, into, sem):
        rows = NAR // n
        copies = []
        for j in range(n):
            dst = into.at[pl.ds(j * rows, rows)]
            start_either(s, j, pack, got.at[j], dst, sem.at[j])
            copies.append(pltpu.make_async_copy(got.at[j], dst, sem.at[j]))
        return copies

    def recurrent(tok, wb, wg, wgw, wm, adp, conv, gi, hold, cl, mix, acc, lg, tsem, wsem, hsem):
        col = z.rec

        def cols(name, size, j=0):
            return pl.ds(pl.multiple_of(col[name] + j * size, 128), size)

        def load_a(j, slot):
            start_either(s, j, ob, gb.at[j], wb.at[slot], wsem.at[slot, 0])
            start_either(s, j, og, gg.at[j], wg.at[slot], wsem.at[slot, 1])

        def load_b(j, slot):
            start_either(s, j, ogw, ggw.at[j], wgw.at[slot], wsem.at[slot, 2])
            start_either(s, j, om, gm.at[j], wm.at[slot], wsem.at[slot, 3])

        adp_in = load_pack(pack_r, gr, adp, tsem.at[1])
        load_a(jnp.int32(0), 0)
        load_b(jnp.int32(0), 0)
        rows_of(0, gtok, tok, tsem.at[0])
        xin = tn(rt_v[...], tok[...])
        resid[...] = xin
        tok[pl.ds(0, LIVE)] = xin.astype(BF16)
        put(tok.at[pl.ds(0, LIVE)], xin_h)
        act1[...] = (xin * norm_scale(xin) * gain1).astype(BF16)
        put(act1, act1_h)
        for copy in adp_in:
            copy.wait()
        ranks[0] = (nt(act1[...], adp[:, cols("db", d)]) * mask).astype(BF16)
        ranks[1] = (nt(act1[...], adp[:, cols("dg", d)]) * mask).astype(BF16)
        acc[...] = jnp.zeros_like(acc)

        def first_pass(j, carry):
            slot = lax.rem(j, 2)
            pltpu.make_async_copy(ob, wb.at[slot], wsem.at[slot, 0]).wait()
            pltpu.make_async_copy(og, wg.at[slot], wsem.at[slot, 1]).wait()

            @pl.when(j + 1 < n)
            def _():
                load_a(j + 1, 1 - slot)

            s32 = smv[j].astype(F32)
            gi[j] = nn(act1[...], wg[slot]) + nn(ranks[1], adp[:, cols("ug", w, j)])
            lg[:, :w] = nn(act1[...], wb[slot]) + nn(ranks[0], adp[:, cols("ub", w, j)])

            def block(r, last):
                at_rows = pl.ds(pl.multiple_of(r * BLOCK, BLOCK), BLOCK)
                br = lg[at_rows, :w]
                both = jnp.concatenate([last, br], axis=0)
                pos = wide(pos_r[at_rows, :], w)
                total = s32[4:5, :] + s32[0:1, :] * br
                for k in range(1, 4):
                    total = total + jnp.where(pos >= k, both[8 - k : 8 - k + BLOCK, :], 0.0) * s32[k : k + 1, :]
                conv[j, at_rows, :] = total
                cl[j, at_rows, :] = total.astype(BF16)
                return br[BLOCK - 8 :, :]

            lax.fori_loop(0, LIVE // BLOCK, block, jnp.zeros((8, w), F32))
            pltpu.make_async_copy(conv.at[j], conv_h.at[j], hsem.at[0, j]).start()
            pltpu.make_async_copy(gi.at[j], gi_h.at[j], hsem.at[1, j]).start()
            acc[...] += nt(cl[j], adp[:, cols("dgates", w, j)])
            for i, a in enumerate(ffn):
                @pl.when(j == i + 1)
                def _():
                    if n > 2:
                        net.line(a, 2)
                    net.corner(a, 1)
            return carry

        lax.fori_loop(0, n, first_pass, 0)
        ranks[2] = (acc[...] * mask).astype(BF16)
        acc[...] = jnp.zeros_like(acc)
        holds = (ig_h, rg_h, st_h)

        def second_pass(j, carry):
            slot = lax.rem(j, 2)
            pltpu.make_async_copy(ogw, wgw.at[slot], wsem.at[slot, 2]).wait()
            pltpu.make_async_copy(om, wm.at[slot], wsem.at[slot, 3]).wait()

            @pl.when(j + 1 < n)
            def _():
                load_b(j + 1, 1 - slot)

            @pl.when(j >= 2)
            def _():
                for i, ref in enumerate(holds):
                    pltpu.make_async_copy(hold.at[slot, i], ref.at[j - 2], hsem.at[2 + i, slot]).wait()

            s32 = smv[j].astype(F32)
            low = cl[j]
            lift = nn(ranks[2], adp[:, cols("ugates", 2 * w, j)])
            bias = jnp.concatenate([s32[6:7, :], s32[7:8, :]], axis=1)
            lg[...] = jnp.concatenate(
                [nn(low[:, i * DH : (i + 1) * DH], wgw[slot, i * DH : (i + 1) * DH, :]) for i in range(z.heads)], axis=1
            ) + bias + lift

            def block(r, carry):
                at_rows = pl.ds(pl.multiple_of(r * BLOCK, BLOCK), BLOCK)
                ig, rg = gates_of(lg[at_rows, :], z)
                first = wide(pos_r[at_rows, :], w) == 0
                _, a, scale = decay_of(s32, rg, first)
                hold[slot, 0, at_rows, :] = ig
                hold[slot, 1, at_rows, :] = rg
                state, _, carry = scan_block(a, scale * ig * conv[j, at_rows, :], carry, False)
                hold[slot, 2, at_rows, :] = state
                act, _ = gelu_parts(gi[j, at_rows, :])
                mix[j, at_rows, :] = (state * act).astype(BF16)
                return carry

            lax.fori_loop(0, LIVE // BLOCK, block, jnp.zeros((8, w), F32))
            for i, ref in enumerate(holds):
                pltpu.make_async_copy(hold.at[slot, i], ref.at[j], hsem.at[2 + i, slot]).start()
            acc[...] += nt(mix[j], adp[:, cols("dm", w, j)])
            resid[...] += nn(mix[j], wm[slot])
            for i, a in enumerate(ffn):
                @pl.when(j == i)
                def _():
                    if n > 2:
                        net.spread(a, 2)
                    if n > 3:
                        net.line(a, 3)
            return carry

        lax.fori_loop(0, n, second_pass, 0)
        put(mix, mixed_h)
        ranks[3] = (acc[...] * mask).astype(BF16)
        put(ranks, ranks_h)
        resid[...] = resid[...] + nn(ranks[3], adp[:, cols("um", d)])
        for j in range(n):
            pltpu.make_async_copy(conv.at[j], conv_h.at[j], hsem.at[0, j]).wait()
            pltpu.make_async_copy(gi.at[j], gi_h.at[j], hsem.at[1, j]).wait()
        for j in (n - 2, n - 1):
            for i, ref in enumerate(holds):
                pltpu.make_async_copy(hold.at[j % 2, i], ref.at[j], hsem.at[2 + i, j % 2]).wait()
        for copy in outs[4:]:
            copy.wait()

    V = pltpu.VMEM
    pl.run_scoped(
        recurrent,
        V((z.rows, d), BF16), V((2, d, w), BF16), V((2, d, w), BF16), V((2, w, 2 * DH), BF16), V((2, w, d), BF16),
        V((NAR, z.rec_cols), BF16), V((n, LIVE, w), F32), V((n, LIVE, w), F32), V((2, 3, LIVE, w), F32),
        V((n, LIVE, w), BF16), V((n, LIVE, w), BF16), V((LIVE, NAR), F32), V((LIVE, 2 * w), F32),
        DMA((2, n)), DMA((2, 4)), DMA((5, n)),
    )

    def feed(tok, wg, wu, wd, adp, act2, gl, acc_o, acc_g, rk, ra, grad_o, hgs, hus, ghs, low, ghg, ghu, tsem, wsem):
        col = z.ffn

        def cols(name, size, j=0, stride=0):
            return pl.ds(pl.multiple_of(col[name] + j * stride, 128), size)

        base = resid[...]
        act2[...] = (base * norm_scale(base) * gain2).astype(BF16)
        acc_o[...] = jnp.zeros_like(acc_o)
        acc_g[...] = jnp.zeros_like(acc_g)
        ra[...] = jnp.zeros_like(ra)
        weights = ((5, ofg, gfg, wg), (6, ofu, gfu, wu), (8, ofd, gfd, wd))
        for k in range(1, n):
            net.ready(7, k)
        lines[1].arrived()
        rows_of(1, gcot, tok, tsem.at[0])
        gl[...] = tn(rt_v[...], tok[...]).astype(BF16)

        def tick(i, q):
            a = ffn[i]

            @pl.when(q + 3 < n)
            def _():
                net.spread(a, q + 3)

            @pl.when(q + 4 < n)
            def _():
                net.line(a, q + 4)

            @pl.when(q + 2 < n)
            def _():
                net.corner(a, q + 2)

            @pl.when(q + 1 < n)
            def _():
                net.twin(a, q + 1)

        def step(q, carry):
            j = jnp.where(q == 0, s, item(jnp.maximum(q, 1), s, n)[0])
            for i, (a, mine, got, into) in enumerate(weights):
                @pl.when(q > 0)
                def _():
                    net.ready(a, q)
                    pltpu.make_async_copy(got.at[j], into, wsem.at[i]).start()

            fg, fu, fd = cols("ufg", h, j, hp), cols("ufu", h, j, hp), cols("dfd", h, j, hp)
            pltpu.make_async_copy(ofg, wg, wsem.at[0]).wait()
            hgs[...] = nn(act2[...], wg[...]) + nn(rk[0], adp[:, fg])
            pltpu.make_async_copy(ofu, wu, wsem.at[1]).wait()
            hus[...] = nn(act2[...], wu[...]) + nn(rk[1], adp[:, fu])
            tick(0, q)
            pltpu.make_async_copy(ofd, wd, wsem.at[2]).wait()
            ghs[...] = nt(gl[...], wd[...]) + nn(rk[2], adp[:, fd])

            def block(r, carry):
                at_rows = pl.ds(pl.multiple_of(r * 16, 16), 16)
                act, slope = gelu_parts(hgs[at_rows, :])
                hu, gh = hus[at_rows, :], ghs[at_rows, :]
                low[at_rows, :] = (act * hu).astype(BF16)
                ghg[at_rows, :] = (gh * hu * slope).astype(BF16)
                ghu[at_rows, :] = (gh * act).astype(BF16)
                return carry

            lax.fori_loop(0, LIVE // 16, block, 0)
            tick(1, q)
            acc_o[...] += nn(low[...], wd[...])
            ra[0] += nt(low[...], adp[:, fd])
            ra[1] += nt(ghg[...], adp[:, fg])
            ra[2] += nt(ghu[...], adp[:, fu])
            tick(2, q)
            acc_g[...] += nt(ghg[...], wg[...]) + nt(ghu[...], wu[...])
            grad_o[:, fd] = tn(rk[2], low[...]).astype(BF16)
            grad_o[:, fg] = tn(rk[0], ghg[...]).astype(BF16)
            grad_o[:, fu] = tn(rk[1], ghu[...]).astype(BF16)
            return carry

        adp_in = load_pack(pack_f, gf, adp, tsem.at[1])
        for i, (a, mine, got, into) in enumerate(weights):
            pltpu.make_async_copy(mine, into, wsem.at[i]).start()
        for copy in adp_in:
            copy.wait()
        rk[0] = (nt(act2[...], adp[:, cols("dfg", d)]) * mask).astype(BF16)
        rk[1] = (nt(act2[...], adp[:, cols("dfu", d)]) * mask).astype(BF16)
        rk[2] = (nt(gl[...], adp[:, cols("ufd", d)]) * mask).astype(BF16)
        lax.fori_loop(0, n, step, 0)
        rank = (ra[0] * mask).astype(BF16)
        work = resid[...] + acc_o[...] + nn(rank, adp[:, cols("ufd", d)])
        tok[...] = nn(rt_v[...], work.astype(BF16)).astype(BF16)
        put(tok, out_h)
        grad_o[:, cols("ufd", d)] = tn(rank, gl[...]).astype(BF16)
        rank_g = (ra[1] * mask).astype(BF16)
        rank_u = (ra[2] * mask).astype(BF16)
        grad_o[:, cols("dfg", d)] = tn(rank_g, act2[...]).astype(BF16)
        grad_o[:, cols("dfu", d)] = tn(rank_u, act2[...]).astype(BF16)
        gact = acc_g[...] + nn(rank_g, adp[:, cols("dfg", d)]) + nn(rank_u, adp[:, cols("dfu", d)])
        put(grad_o, grad_h)
        resid[...] = gl[...].astype(F32) + norm_back(resid[...], gact * gain2)
        put(resid, gres_h)
        for copy in outs[8:]:
            copy.wait()

    pl.run_scoped(
        feed,
        V((z.rows, d), BF16), V((d, h), BF16), V((d, h), BF16), V((h, d), BF16), V((NAR, z.ffn_cols), BF16),
        V((LIVE, d), BF16), V((LIVE, d), BF16), V((LIVE, d), F32), V((LIVE, d), F32),
        V((3, LIVE, NAR), BF16), V((3, LIVE, NAR), F32), V((NAR, z.ffn_cols), BF16),
        V((LIVE, h), F32), V((LIVE, h), F32), V((LIVE, h), F32), V((LIVE, h), BF16), V((LIVE, h), BF16), V((LIVE, h), BF16),
        DMA((2, n)), DMA((3,)),
    )
    for line in lines:
        line.sent()
    for copy in outs[:4]:
        copy.wait()
    net.drain()


def run_first(z, geo, *args):
    n, w, d = z.n, z.w, z.d
    S, V = jax.ShapeDtypeStruct, pltpu.VMEM
    sources_ = args[6:13]
    shapes = [sources_[0], sources_[1], sources_[2], (NAR // n, z.rec_cols), sources_[3], sources_[4], sources_[5], (NAR // n, z.ffn_cols), sources_[6]]
    outs = [S((n,) + tuple(x.shape if hasattr(x, "shape") else x), BF16) for x in shapes]
    na = len(outs)
    outs += [S((n, z.cap, d), BF16)] * 2 + [S((n, 16, w), BF16)]
    outs += [S((LIVE, d), BF16), S((LIVE, d), BF16), S((n, LIVE, w), BF16), S((4, LIVE, NAR), BF16), S((z.rows, LIVE), BF16), S((z.rows, z.rows), BF16)]
    outs += [S((n, LIVE, w), F32)] * 5
    outs += [S((z.rows, d), BF16), S((LIVE, d), F32), S((NAR, z.ffn_cols), BF16)]
    SM = pl.BlockSpec(memory_space=pltpu.SMEM)
    return pl.pallas_call(
        functools.partial(first_kernel, z, geo),
        out_shape=outs,
        in_specs=[SM, SM, VM, VM] + [ANY] * (len(args) - 4),
        out_specs=[ANY] * len(outs),
        scratch_shapes=[
            V((NAR // n, z.rec_cols), BF16), V((NAR // n, z.ffn_cols), BF16), V((2, n, z.cap, d), BF16), V((n, 16, w), BF16),
            V((z.rows, z.rows), BF16), V((z.rows, LIVE), BF16), V((LIVE, NAR), jnp.int32), V((LIVE, NAR), F32),
            V((LIVE, d), BF16), V((LIVE, d), F32), V((4, LIVE, NAR), BF16),
            DMA((2 * n, na)), DMA((8, na, n - 1)), DMA((na, n)), DMA((8, na, n)), DMA((3, n)), DMA((3, n)),
            DMA((2, n)), DMA((2, 8)), DMA((11,)),
        ],
        compiler_params=pltpu.CompilerParams(collective_id=1, has_side_effects=True, vmem_limit_bytes=VLIMIT),
        name="first",
    )(*args)


def add_rows(dst, left, right, rows, step=16):
    def body(r, carry):
        at_rows = pl.ds(pl.multiple_of(r * step, step), step)
        dst[at_rows, :] = (left[at_rows, :].astype(F32) + right[at_rows, :].astype(F32)).astype(BF16)
        return carry

    lax.fori_loop(0, rows // step, body, 0)


class Reduce:
    def __init__(self, at, t, clusters, width, source, own, fin, bufs, sems):
        self.at, self.t, self.clusters, self.c = at, t, clusters, width
        self.source, self.own, self.fin = source, own, fin
        self.rc, self.r1, self.r2, self.rg, self.rz, self.sm = bufs
        self.ss, self.rs, self.zs, self.zr, self.gs, self.gr, self.ps, self.pr = [x.at[t] for x in sems]
        p = at.p
        self.core, self.x, self.y = p % 2, (p // 2) % 2, p // 4
        self.rows, self.half = NAR // at.n, NAR // 2

    def cut(self, q):
        return pl.ds(pl.multiple_of(q * self.c, 128), self.c)

    def send(self, src, dst, a, b, device):
        remote(src, dst, a, b, device).start()

    def arrived(self, dst, a, b):
        remote(dst, dst, a, b, self.at.across(1)).wait_recv()

    def to_core(self):
        for c in range(4):
            self.send(self.source.at[:, self.cut(2 * c + 1 - self.core)], self.rc.at[c], self.ss.at[c], self.rs.at[c], self.at.across(1))

    def to_first(self):
        for c in range(4):
            self.arrived(self.rc.at[c], self.ss.at[c], self.rs.at[c])
            add_rows(self.rc.at[c], self.own(c), self.rc.at[c], NAR)
        low, high = pl.ds(0, self.half), pl.ds(self.half, self.half)
        for i in range(2):
            self.send(self.rc.at[2 * i + 1 - self.x, low], self.r1.at[0, i], self.ss.at[4 + i], self.rs.at[4 + i], self.at.across(2))
            self.send(self.rc.at[2 * (1 - self.y) + i, high], self.r1.at[1, i], self.ss.at[6 + i], self.rs.at[6 + i], self.at.across(4))

    def to_second(self):
        low, high = pl.ds(0, self.half), pl.ds(self.half, self.half)
        for i in range(2):
            self.arrived(self.r1.at[0, i], self.ss.at[4 + i], self.rs.at[4 + i])
            add_rows(self.r1.at[0, i], self.rc.at[2 * i + self.x, low], self.r1.at[0, i], self.half)
            self.arrived(self.r1.at[1, i], self.ss.at[6 + i], self.rs.at[6 + i])
            add_rows(self.r1.at[1, i], self.rc.at[2 * self.y + i, high], self.r1.at[1, i], self.half)
        self.send(self.r1.at[0, 1 - self.y], self.r2.at[0, low], self.ss.at[8], self.rs.at[8], self.at.across(4))
        self.send(self.r1.at[1, 1 - self.x], self.r2.at[0, high], self.ss.at[9], self.rs.at[9], self.at.across(2))

    def to_line(self):
        at = self.at
        low, high = pl.ds(0, self.half), pl.ds(self.half, self.half)
        self.arrived(self.r2.at[0, low], self.ss.at[8], self.rs.at[8])
        add_rows(self.r2.at[0, low], self.r1.at[0, self.y], self.r2.at[0, low], self.half)
        self.arrived(self.r2.at[0, high], self.ss.at[9], self.rs.at[9])
        add_rows(self.r2.at[0, high], self.r1.at[1, self.x], self.r2.at[0, high], self.half)
        if self.clusters > 1:
            mine = at.rep // PLANE
            for r in range(1, self.clusters):
                device = {"rep": lax.rem(at.rep + r * PLANE, self.clusters * PLANE), "shard": at.s}
                self.send(self.r2.at[0], self.rg.at[mine], self.gs.at[r], self.gr.at[mine], device)
            self.rg[mine] = self.r2[0]
            for r in range(1, self.clusters):
                other = lax.rem(mine + r, self.clusters)
                self.arrived(self.rg.at[other], self.gs.at[r], self.gr.at[other])
            add_rows(self.r2.at[1], self.rg.at[0], self.rg.at[1], NAR)
            for other in range(2, self.clusters):
                add_rows(self.r2.at[1], self.rg.at[other], self.r2.at[1], NAR)
        self.final = 1 if self.clusters > 1 else 0
        for r in range(1, at.n):
            d = lax.rem(at.s + r, at.n)
            chunk = pl.ds(pl.multiple_of(d * self.rows, self.rows), self.rows)
            self.send(self.r2.at[self.final, chunk], self.rz.at[at.s], self.zs.at[r], self.zr.at[at.s], at.along(d))

    def to_plane(self):
        at = self.at
        total = self.r2[self.final, pl.ds(pl.multiple_of(at.s * self.rows, self.rows), self.rows), :].astype(F32)
        for r in range(1, at.n):
            d = lax.rem(at.s + r, at.n)
            self.arrived(self.rz.at[d], self.zs.at[r], self.zr.at[d])
            total = total + self.rz[d].astype(F32)
        self.sm[...] = total.astype(BF16)
        self.fin[:, self.cut(at.p)] = total.astype(BF16)
        for kind, bit in ((0, 2), (1, 4), (3, 1)):
            self.spread(kind, at.p, bit, self.sm)

    def spread(self, kind, q, bit, src=None):
        view = self.fin.at[:, self.cut(q)]
        self.send(view if src is None else src, view, self.ps.at[kind], self.pr.at[kind], self.at.across(bit))

    def spread_wait(self, kind, q):
        self.arrived(self.fin.at[:, self.cut(q)], self.ps.at[kind], self.pr.at[kind])

    def over(self):
        at = self.at
        self.spread_wait(0, at.q2)
        if self.t % 2 == 0:
            self.spread(2, at.q2, 4)
        self.spread(4, at.q2, 1)
        self.spread_wait(1, at.q4)
        if self.t % 2 == 1:
            self.spread(2, at.q4, 2)
        self.spread(5, at.q4, 1)

    def last(self):
        self.spread_wait(2, self.at.q6)
        self.spread(6, self.at.q6, 1)

    def end(self):
        at = self.at
        for kind, q in ((3, at.q1), (4, at.q3), (5, at.q5), (6, at.q7)):
            self.spread_wait(kind, q)
        sent = [(self.rc.at[0], self.ss.at[c]) for c in range(4)]
        sent += [(self.r1.at[0, 0], self.ss.at[4 + i]) for i in range(4)]
        sent += [(self.r2.at[0, pl.ds(0, self.half)], self.ss.at[8 + i]) for i in range(2)]
        sent += [(self.rg.at[0], self.gs.at[r]) for r in range(1, self.clusters)]
        sent += [(self.rz.at[0], self.zs.at[r]) for r in range(1, at.n)]
        sent += [(self.sm, self.ps.at[kind]) for kind in range(7)]
        for view, sem in sent:
            remote(view, view, sem, sem, at.across(1)).wait_send()


def early_table(z):
    return {"um": 0, "dm": z.d, "ugates": z.d + z.n * z.w}, up_to(z.d + 3 * z.n * z.w, 128 * PLANE)


def late_table(z):
    lru = z.n * z.w
    return {"dgates": 0, "ub": lru, "ug": 2 * lru, "db": 3 * lru, "dg": 3 * lru + z.d}, up_to(3 * lru + 2 * z.d, 128 * PLANE)


def second_kernel(z, clusters, *refs):
    n, w, d = z.n, z.w, z.d
    refs = list(refs)

    def take(count):
        out, refs[:count] = refs[:count], []
        return out

    len_r, idx_r, rt_v, gres, ranks = take(5)
    sm_h, ob, og, ogw, om, gb, gg, ggw, gm, gr = take(10)
    conv_h, gi_h, ig_h, rg_h, st_h, act1_h, xin_h, mixed_h, out_h, gradf_h = take(10)
    back_out, back_tok, fin_f, fin_e, fin_l = take(5)
    pos_r, mask_r, smv, adp, glm, gdir, glow, gilow, gmix, acc, rk, accg, tokv, grad_e, grad_l, own_f = take(16)
    bufs = [take(6) for _ in range(3)]
    sems = take(8)
    lss, lrs, lsem = take(3)
    at = Plane(n)
    s = at.s
    at.greet(clusters)
    lines = [Line(at, i, lss, lrs) for i in range(2)]
    lines[0].start(lambda place: out_h.at[place], back_out)
    keep = pltpu.make_async_copy(out_h.at[s], back_out.at[s], lsem.at[0, 0])
    keep.start()
    (early, _), (late, _) = early_table(z), late_table(z)
    core = at.p % 2

    def own_of(ref, width):
        return lambda c: ref.at[:, pl.ds(pl.multiple_of((2 * c + core) * width, 128), width)]

    widths = [x.shape[2] for x in (bufs[0][0], bufs[1][0], bufs[2][0])]
    red_f = Reduce(at, 0, clusters, widths[0], gradf_h, lambda c: own_f.at[c], fin_f, bufs[0], sems)
    red_e = Reduce(at, 1, clusters, widths[1], grad_e, own_of(grad_e, widths[1]), fin_e, bufs[1], sems)
    red_l = Reduce(at, 2, clusters, widths[2], grad_l, own_of(grad_l, widths[2]), fin_l, bufs[2], sems)
    red_f.to_core()
    rows = NAR // n
    own_in = [pltpu.make_async_copy(own_of(gradf_h, widths[0])(c), own_f.at[c], lsem.at[1, c]) for c in range(4)]
    packs = [pltpu.make_async_copy(gr.at[j], adp.at[pl.ds(j * rows, rows)], lsem.at[2, j]) for j in range(n)]
    small_in = pltpu.make_async_copy(sm_h, smv, lsem.at[0, 1])
    for copy in own_in + packs + [small_in]:
        copy.start()
    slots_of(len_r, idx_r, pos_r, mask_r)
    mask = mask_r[...]
    col = z.rec

    def cols(name, size, j=0):
        return pl.ds(pl.multiple_of(col[name] + j * size, 128), size)

    def put_at(table, name, size, j=0):
        return pl.ds(pl.multiple_of(table[name] + j * size, 128), size)

    def rows_at(r):
        return pl.ds(pl.multiple_of(r * BLOCK, BLOCK), BLOCK)

    blocks = LIVE // BLOCK

    def state_pass(sav, wm, mixed, ssem):
        saved = (conv_h, gi_h, ig_h, rg_h, st_h)

        def load(j, slot):
            start_either(s, j, om, gm.at[j], wm.at[slot], ssem.at[slot, 5])
            for i, ref in enumerate(saved):
                pltpu.make_async_copy(ref.at[j], sav.at[slot, i], ssem.at[slot, i]).start()
            pltpu.make_async_copy(mixed_h.at[j], mixed.at[slot], ssem.at[slot, 6]).start()

        def load_wait(slot):
            pltpu.make_async_copy(om, wm.at[slot], ssem.at[slot, 5]).wait()
            for i, ref in enumerate(saved):
                pltpu.make_async_copy(ref.at[0], sav.at[slot, i], ssem.at[slot, i]).wait()
            pltpu.make_async_copy(mixed_h.at[0], mixed.at[slot], ssem.at[slot, 6]).wait()

        load(jnp.int32(0), 0)
        glm[...] = gres[...].astype(BF16)
        for copy in packs + [small_in]:
            copy.wait()
        rk[0] = (nt(glm[...], adp[:, cols("um", d)]) * mask).astype(BF16)
        grad_e[:, put_at(early, "um", d)] = tn(ranks[3], glm[...]).astype(BF16)
        acc[...] = jnp.zeros_like(acc)
        for copy in own_in:
            copy.wait()
        red_f.to_first()

        def body(j, carry):
            slot = lax.rem(j, 2)
            load_wait(slot)

            @pl.when(j + 1 < n)
            def _():
                load(j + 1, 1 - slot)

            s32 = smv[j].astype(F32)
            gmix[...] = nt(glm[...], wm[slot]) + nn(rk[0], adp[:, cols("dm", w, j)])
            grad_e[:, put_at(early, "dm", w, j)] = tn(rk[0], mixed[slot]).astype(BF16)

            def block(i, carry):
                at_rows = rows_at(blocks - 1 - i)
                gmx, conv, ig = gmix[at_rows, :], sav[slot, 0, at_rows, :], sav[slot, 2, at_rows, :]
                rg, state = sav[slot, 3, at_rows, :], sav[slot, 4, at_rows, :]
                act, slope = gelu_parts(sav[slot, 1, at_rows, :])
                gilow[j, at_rows, :] = (gmx * state * slope).astype(BF16)
                first = wide(pos_r[at_rows, :], w) == 0
                soft, a, scale = decay_of(s32, rg, first)
                x = gmx * act
                _, after, carry = scan_block(a, a * x, carry, True)
                total = x + after
                drive = total * scale
                gdir[j, at_rows, :] = drive * ig
                fed = ig * conv
                kept = total * (state - scale * fed)
                g_log = jnp.where(first, 0.0, kept - total * fed * (a * a) / scale)
                l_in = drive * conv * ig * (1.0 - ig)
                l_rec = -soft * g_log * rg * (1.0 - rg)
                for i in range(z.heads):
                    glow[j, at_rows, 2 * i * DH : (2 * i + 1) * DH] = l_in[:, i * DH : (i + 1) * DH].astype(BF16)
                    glow[j, at_rows, (2 * i + 1) * DH : (2 * i + 2) * DH] = l_rec[:, i * DH : (i + 1) * DH].astype(BF16)
                return carry

            lax.fori_loop(0, blocks, block, jnp.zeros((8, w), F32))
            acc[...] += nt(glow[j], adp[:, cols("ugates", 2 * w, j)])
            grad_e[:, put_at(early, "ugates", 2 * w, j)] = tn(ranks[2], glow[j]).astype(BF16)
            return carry

        lax.fori_loop(0, n, body, 0)

    V = pltpu.VMEM
    pl.run_scoped(state_pass, V((2, 5, LIVE, w), F32), V((2, w, d), BF16), V((2, LIVE, w), BF16), DMA((2, 7)))
    rk[1] = (acc[...] * mask).astype(BF16)
    red_e.to_core()

    def branch_pass(wb, wg, wgw, conv, blow, act1, xin, grads_rank, wsem, asem):
        def load(j, slot):
            start_either(s, j, ob, gb.at[j], wb.at[slot], wsem.at[slot, 0])
            start_either(s, j, og, gg.at[j], wg.at[slot], wsem.at[slot, 1])
            start_either(s, j, ogw, ggw.at[j], wgw.at[slot], wsem.at[slot, 2])
            pltpu.make_async_copy(conv_h.at[j], conv.at[slot], wsem.at[slot, 3]).start()

        ends = [pltpu.make_async_copy(act1_h, act1, asem.at[0]), pltpu.make_async_copy(xin_h, xin, asem.at[1])]
        load(jnp.int32(0), 0)
        for copy in ends:
            copy.start()
        red_f.to_second()
        accg[...] = jnp.zeros_like(accg)
        grads_rank[...] = jnp.zeros_like(grads_rank)

        def body(j, carry):
            slot = lax.rem(j, 2)
            for i, (ref, into) in enumerate(((ob, wb), (og, wg), (ogw, wgw), (conv_h.at[0], conv))):
                pltpu.make_async_copy(ref, into.at[slot], wsem.at[slot, i]).wait()

            @pl.when(j + 1 < n)
            def _():
                load(j + 1, 1 - slot)

            s32 = smv[j].astype(F32)
            grad_l[:, put_at(late, "dgates", w, j)] = tn(rk[1], conv[slot].astype(BF16)).astype(BF16)
            low = glow[j]
            heads = jnp.concatenate(
                [nt(low[:, 2 * i * DH : 2 * (i + 1) * DH], wgw[slot, i * DH : (i + 1) * DH, :]) for i in range(z.heads)], axis=1
            )
            gmix[...] = gdir[j] + heads + nn(rk[1], adp[:, cols("dgates", w, j)])

            def block(i, carry):
                later, later_pos = carry
                at_rows = rows_at(blocks - 1 - i)
                cur, pos = gmix[at_rows, :], pos_r[at_rows, :]
                both = jnp.concatenate([cur, later], axis=0)
                both_pos = jnp.concatenate([pos, later_pos], axis=0)
                total = cur * s32[0:1, :]
                for k in range(1, 4):
                    inside = wide(both_pos[k : k + BLOCK, :], w) >= k
                    total = total + jnp.where(inside, both[k : k + BLOCK, :], 0.0) * s32[k : k + 1, :]
                blow[at_rows, :] = total.astype(BF16)
                return cur[:8, :], pos[:8, :]

            lax.fori_loop(0, blocks, block, (jnp.zeros((8, w), F32), jnp.zeros((8, NAR), jnp.int32)))
            gil = gilow[j]
            grad_l[:, put_at(late, "ub", w, j)] = tn(ranks[0], blow[...]).astype(BF16)
            grad_l[:, put_at(late, "ug", w, j)] = tn(ranks[1], gil).astype(BF16)
            accg[...] += nt(blow[...], wb[slot]) + nt(gil, wg[slot])
            grads_rank[0] += nt(blow[...], adp[:, cols("ub", w, j)])
            grads_rank[1] += nt(gil, adp[:, cols("ug", w, j)])
            pl.when(j == 0)(red_e.to_first)
            pl.when(j == n - 1)(red_f.to_line)
            return carry

        lax.fori_loop(0, n, body, 0)
        rank_b = (grads_rank[0] * mask).astype(BF16)
        rank_g = (grads_rank[1] * mask).astype(BF16)
        for copy in ends:
            copy.wait()
        gain1 = gain_row(smv, 8, n, d)
        gact = accg[...] + nn(rank_b, adp[:, cols("db", d)]) + nn(rank_g, adp[:, cols("dg", d)])
        gwork = gres[...] + norm_back(xin[...].astype(F32), gact * gain1)
        tokv[...] = nn(rt_v[...], gwork.astype(BF16)).astype(BF16).reshape(n, z.cap, d)
        lines[1].start(lambda place: tokv.at[place], back_tok)
        grad_l[:, put_at(late, "db", d)] = tn(rank_b, act1[...]).astype(BF16)
        grad_l[:, put_at(late, "dg", d)] = tn(rank_g, act1[...]).astype(BF16)

    pl.run_scoped(
        branch_pass, V((2, d, w), BF16), V((2, d, w), BF16), V((2, w, 2 * DH), BF16), V((2, LIVE, w), F32),
        V((LIVE, w), BF16), V((LIVE, d), BF16), V((LIVE, d), BF16), V((2, LIVE, NAR), F32), DMA((2, 4)), DMA((2,)),
    )
    red_l.to_core()
    keep_tok = pltpu.make_async_copy(tokv.at[s], back_tok.at[s], lsem.at[0, 2])
    keep_tok.start()
    red_e.to_second()
    red_f.to_plane()
    red_l.to_first()
    red_e.to_line()
    red_f.over()
    red_l.to_second()
    red_e.to_plane()
    red_f.last()
    red_l.to_line()
    red_e.over()
    red_l.to_plane()
    red_e.last()
    red_l.over()
    red_l.last()
    for red in (red_f, red_e, red_l):
        red.end()
    for line in lines:
        line.arrived()
        line.sent()
    keep.wait()
    keep_tok.wait()


def run_second(z, clusters, *args):
    n, w, d = z.n, z.w, z.d
    S, V = jax.ShapeDtypeStruct, pltpu.VMEM
    cols = [z.ffn_cols, early_table(z)[1], late_table(z)[1]]
    rows, half = NAR // n, NAR // 2
    outs = [S((n, z.cap, d), BF16)] * 2 + [S((rows, c), BF16) for c in cols]
    scratch = [
        V((LIVE, NAR), jnp.int32), V((LIVE, NAR), F32), V((n, 16, w), BF16), V((NAR, z.rec_cols), BF16), V((LIVE, d), BF16),
        V((n, LIVE, w), F32), V((n, LIVE, 2 * w), BF16), V((n, LIVE, w), BF16), V((LIVE, w), F32), V((LIVE, NAR), F32),
        V((2, LIVE, NAR), BF16), V((LIVE, d), F32), V((n, z.cap, d), BF16), V((NAR, cols[1]), BF16), V((NAR, cols[2]), BF16),
        V((4, NAR, cols[0] // PLANE), BF16),
    ]
    more = clusters > 1
    for size in cols:
        c = size // PLANE
        scratch += [
            V((4, NAR, c), BF16), V((2, 2, half, c), BF16), V((2 if more else 1, NAR, c), BF16),
            V((clusters, NAR, c) if more else (1, 16, 128), BF16), V((n, rows, c), BF16), V((rows, c), BF16),
        ]
    scratch += [DMA((3, 10)), DMA((3, 10)), DMA((3, n)), DMA((3, n)), DMA((3, clusters)), DMA((3, clusters)), DMA((3, 7)), DMA((3, 7))]
    scratch += [DMA((2, n)), DMA((2, n)), DMA((3, max(n, 4)))]
    SM = pl.BlockSpec(memory_space=pltpu.SMEM)
    return pl.pallas_call(
        functools.partial(second_kernel, z, clusters),
        out_shape=outs,
        in_specs=[SM, SM, VM, VM, VM] + [ANY] * (len(args) - 5),
        out_specs=[ANY, ANY, VM, VM, VM],
        scratch_shapes=scratch,
        compiler_params=pltpu.CompilerParams(collective_id=2, has_side_effects=True, vmem_limit_bytes=VLIMIT),
        name="second",
    )(*args)


def local(
    tokens, cotangent, norm_first, branch_weight, gelu_weight, conv_weight, conv_bias, gate_weight, gate_bias,
    decay_param, merge_weight, norm_second, feed_gate, feed_up, feed_down, down_branch, up_branch, down_gelu,
    up_gelu, down_gates, up_gates, down_merge, up_merge, down_feed_gate, up_feed_gate, down_feed_up, up_feed_up,
    down_feed_down, up_feed_down, seq_lengths, adapter_index, deal_order,
):
    n = lax.axis_size("shard")
    clusters = lax.axis_size("rep") // PLANE
    rows, d = tokens.shape
    z = Sizes(n, d, branch_weight.shape[1] * n, feed_gate.shape[1] * n, rows)
    w, pad = z.w, z.hp - z.h

    def spaced(values):
        if pad == 0:
            return values
        parts = values.reshape(values.shape[0], n, z.h)
        return jnp.pad(parts, ((0, 0), (0, 0), (0, pad))).reshape(values.shape[0], n * z.hp)

    rec_own = (down_branch.T, down_gelu.T, down_gates.T, down_merge.T, up_branch, up_gelu, up_gates, up_merge)
    ffn_own = (
        down_feed_gate.T, down_feed_up.T, spaced(down_feed_down.T), spaced(up_feed_gate), spaced(up_feed_up), up_feed_down
    )

    def gain(values):
        return jnp.pad(values, (0, w - values.shape[0]))

    small = jnp.concatenate(
        [conv_weight.reshape(-1), conv_bias, decay_param, gate_bias.reshape(-1), gain(norm_first), gain(norm_second), jnp.zeros((6 * w,), BF16)]
    ).reshape(16, w)
    gates = gate_weight.reshape(w, 2 * DH)
    arrays = [branch_weight, gelu_weight, gates, None, merge_weight, feed_gate, feed_up, None, feed_down]
    sizes = [x.shape[0] if x is not None else 0 for x in arrays]
    geo = [(0, size // PLANE) for size in sizes]
    geo[3], geo[7] = (1, z.rec_cols // PLANE), (1, z.ffn_cols // PLANE)
    weights = (branch_weight, gelu_weight, gates, merge_weight)
    got = run_first(
        z, geo, seq_lengths, adapter_index, deal_order, small, tokens, cotangent, *weights, feed_gate, feed_up, feed_down,
        *rec_own, *ffn_own,
    )
    gb, gg, ggw, gr, gm, _, _, _, _, _, _, sm = got[:12]
    act1, xin, mixed, ranks, rt, order = got[12:18]
    saved = got[18:23]
    out_send, gres, grad_ffn = got[23:]
    back_out, back_tok, fin_f, fin_e, fin_l = run_second(
        z, clusters, seq_lengths, adapter_index, rt, gres, ranks, sm, *weights, gb, gg, ggw, gm, gr, *saved, act1, xin, mixed,
        out_send.reshape(n, z.cap, d), grad_ffn,
    )

    def arrival(received):
        return tn(order, received.reshape(rows, d))

    (early, _), (late, _) = early_table(z), late_table(z)

    def part(values, table, name, size):
        return values[:, table[name] : table[name] + size].astype(F32)

    def unspaced(values):
        if pad == 0:
            return values
        return values.reshape(values.shape[0], n, z.hp)[:, :, : z.h].reshape(values.shape[0], n * z.h)

    lru, ffp = n * w, n * z.hp
    return (
        arrival(back_out),
        arrival(back_tok),
        part(fin_l, late, "db", d).T,
        part(fin_l, late, "ub", lru),
        part(fin_l, late, "dg", d).T,
        part(fin_l, late, "ug", lru),
        part(fin_l, late, "dgates", lru).T,
        part(fin_e, early, "ugates", 2 * lru),
        part(fin_e, early, "dm", lru).T,
        part(fin_e, early, "um", d),
        part(fin_f, z.ffn, "dfg", d).T,
        unspaced(part(fin_f, z.ffn, "ufg", ffp)),
        part(fin_f, z.ffn, "dfu", d).T,
        unspaced(part(fin_f, z.ffn, "ufu", ffp)),
        unspaced(part(fin_f, z.ffn, "dfd", ffp)).T,
        part(fin_f, z.ffn, "ufd", d),
    )


def solution(mesh):
    tok, line, col, row = P(("rep", "shard"), None), P("shard"), P(None, "shard"), P("shard", None)
    in_specs = (
        tok, tok, line, col, col, col, line, P("shard", None, None), row, line, row, line, col, col, row,
    ) + (col, row) * 7 + (tok, tok, P("rep", None))
    out_specs = (tok, tok) + (col, row) * 7
    return jax.shard_map(local, mesh=mesh, in_specs=in_specs, out_specs=out_specs, check_vma=False)
```

```python
import functools

import jax
import jax.numpy as jnp
from jax import lax
from jax.experimental import pallas as pl
from jax.experimental.pallas import tpu as pltpu
from jax.sharding import PartitionSpec as P

NA = 8
R = 16
NAR = NA * R
DH = 128
LIVE = 384
PLANE = 8
EPS = 1e-06
DECAY = 8.0
F32 = jnp.float32
BF16 = jnp.bfloat16
MESH_ID = pl.DeviceIdType.MESH
DMA = pltpu.SemaphoreType.DMA
ANY = pl.BlockSpec(memory_space=pl.ANY)
VM = pl.BlockSpec(memory_space=pltpu.VMEM)
VLIMIT = 60 << 20
GC = 0.7978845608028654
GA = 0.044715


def up_to(size, step):
    return -(-size // step) * step


def nn(a, b):
    return lax.dot_general(a, b, (((1,), (0,)), ((), ())), preferred_element_type=F32)


def nt(a, b):
    return lax.dot_general(a, b, (((1,), (1,)), ((), ())), preferred_element_type=F32)


def tn(a, b):
    return lax.dot_general(a, b, (((0,), (0,)), ((), ())), preferred_element_type=F32)


def gelu_parts(x):
    x2 = x * x
    th = jnp.tanh(GC * x * (1.0 + GA * x2))
    half = 0.5 * (1.0 + th)
    return x * half, half + 0.5 * x * (1.0 - th * th) * (GC * (1.0 + 3.0 * GA * x2))


def neg_expm1(x):
    series = x * (1.0 + x * (1 / 2) * (1.0 + x * (1 / 3) * (1.0 + x * (1 / 4) * (1.0 + x * (1 / 5) * (1.0 + x * (1 / 6))))))
    return jnp.where(x > -0.5, -series, 1.0 - jnp.exp(x))


class Sizes:
    def __init__(self, n, width, lru, ff, rows):
        self.n, self.d, self.rows = n, width, rows
        self.w = lru // n
        self.h = ff // n
        self.hp = up_to(self.h, 128)
        self.heads = self.w // DH
        self.cap = rows // n
        d, w, hp = width, self.w, self.hp
        self.rec = {}
        at = 0
        for name, size in (
            ("db", d), ("dg", d), ("dgates", n * w), ("dm", n * w),
            ("ub", n * w), ("ug", n * w), ("ugates", 2 * n * w), ("um", d),
        ):
            self.rec[name] = at
            at += size
        self.rec_used, self.rec_cols = at, up_to(at, 128 * PLANE)
        self.ffn = {}
        at = 0
        for name, size in (("dfg", d), ("dfu", d), ("dfd", n * hp), ("ufg", n * hp), ("ufu", n * hp), ("ufd", d)):
            self.ffn[name] = at
            at += size
        self.ffn_used, self.ffn_cols = at, up_to(at, 128 * PLANE)


def item(k, s, n):
    m = jnp.minimum(s, n - 1 - s)
    paired = k <= 2 * m
    t = jnp.where(paired, (k + 1) // 2, k - m)
    below = jnp.where(paired, k % 2 == 1, s > n - 1 - s)
    return jnp.where(below, s - t, s + t), below


def remote(src, dst, send, recv, device):
    return pltpu.make_async_remote_copy(src, dst, send, recv, device_id=device, device_id_type=MESH_ID)


def start_either(s, j, own, gathered, dst, sem):
    @pl.when(j == s)
    def _():
        pltpu.make_async_copy(own, dst, sem).start()

    @pl.when(j != s)
    def _():
        pltpu.make_async_copy(gathered, dst, sem).start()


def wide(mask, width):
    return jnp.tile(mask, (1, width // 128))


BLOCK = 32


def scan_block(a, x, carry, reverse):
    rows, width = a.shape
    groups = rows // 8
    a, x = a.reshape(groups, 8, width), x.reshape(groups, 8, width)
    row = lax.broadcasted_iota(jnp.int32, (groups, 8, width), 1)
    for step in (1, 2, 4):
        shift = 8 - step if reverse else step
        inside = row < 8 - step if reverse else row >= step
        x = x + a * jnp.where(inside, pltpu.roll(x, shift, 1), 0.0)
        a = a * jnp.where(inside, pltpu.roll(a, shift, 1), 1.0)
    order = range(groups - 1, -1, -1) if reverse else range(groups)
    edge, far, back = (0, 7, 7) if reverse else (7, 0, 1)
    line = lax.broadcasted_iota(jnp.int32, (8, width), 0)
    values, beside = [None] * groups, [None] * groups
    for g in order:
        value = x[g] + a[g] * carry
        values[g] = value
        beside[g] = jnp.where(line == far, carry, pltpu.roll(value, back, 0))
        carry = jnp.broadcast_to(value[edge : edge + 1, :], (8, width))
    return jnp.concatenate(values, axis=0), jnp.concatenate(beside, axis=0), carry


def norm_scale(values):
    return lax.rsqrt(jnp.mean(values * values, axis=-1, keepdims=True) + EPS)


def gain_row(smv, row, n, d):
    pieces = [smv[j, row : row + 1, : d // n].astype(F32) for j in range(n)]
    return jnp.concatenate(pieces, axis=1)


def gates_of(logits, z):
    heads = z.heads
    ig = jnp.concatenate([logits[:, 2 * i * DH : (2 * i + 1) * DH] for i in range(heads)], axis=1)
    rg = jnp.concatenate([logits[:, (2 * i + 1) * DH : (2 * i + 2) * DH] for i in range(heads)], axis=1)
    return jax.nn.sigmoid(ig), jax.nn.sigmoid(rg)


def decay_of(s32, rg, first):
    soft = DECAY * jnp.log1p(jnp.exp(-s32[5:6, :]))
    log_a = -rg * soft
    a = jnp.where(first, 0.0, jnp.exp(log_a))
    scale = jnp.where(first, 1.0, jnp.sqrt(neg_expm1(2.0 * log_a)))
    return soft, a, scale


def norm_back(values, u):
    scale = norm_scale(values)
    return scale * u - values * (scale * scale * scale * jnp.mean(u * values, axis=-1, keepdims=True))


class Plane:
    def __init__(self, n):
        self.n = n
        self.rep, self.s = lax.axis_index("rep"), lax.axis_index("shard")
        self.p = p = self.rep % PLANE
        self.q1, self.q2, self.q4 = p + self.flip(1) - self.rep, p + self.flip(2) - self.rep, p + self.flip(4) - self.rep
        self.q6 = self.q4 + self.flip(2) - self.rep
        self.q3, self.q5, self.q7 = self.q1 + self.q2 - p, self.q1 + self.q4 - p, self.q1 + self.q6 - p

    def flip(self, bit):
        return self.rep + bit * (1 - 2 * ((self.rep // bit) % 2))

    def across(self, bit):
        return {"rep": self.flip(bit), "shard": self.s}

    def along(self, place):
        return {"rep": self.rep, "shard": place}

    def greet(self, clusters=1):
        barrier = pltpu.get_barrier_semaphore()
        for bit in (1, 2, 4):
            pl.semaphore_signal(barrier, inc=1, device_id=self.across(bit), device_id_type=MESH_ID)
        for r in range(1, self.n):
            pl.semaphore_signal(barrier, inc=1, device_id=self.along(lax.rem(self.s + r, self.n)), device_id_type=MESH_ID)
        for r in range(1, clusters):
            other = {"rep": lax.rem(self.rep + r * PLANE, clusters * PLANE), "shard": self.s}
            pl.semaphore_signal(barrier, inc=1, device_id=other, device_id_type=MESH_ID)
        pl.semaphore_wait(barrier, 3 + self.n - 1 + clusters - 1)


class Gather:
    def __init__(self, at, geo, src, dst, sz, sp, rz, rp):
        self.at, self.geo, self.src, self.dst = at, geo, src, dst
        self.sz, self.sp, self.rz, self.rp = sz, sp, rz, rp

    def cut(self, view, a, start, size):
        if self.geo[a][0] == 0:
            return view.at[pl.ds(pl.multiple_of(start, 8), size)]
        return view.at[:, pl.ds(pl.multiple_of(start, 128), size)]

    def part(self, view, a, q):
        size = self.geo[a][1]
        return self.cut(view, a, q * size, size)

    def got(self, a, j, q):
        return self.part(self.dst[a].at[j], a, q)

    def half(self, a, j, q, second):
        axis, size = self.geo[a]
        step = 8 if axis == 0 else 128
        first = (size // step + 1) // 2 * step
        if second:
            return self.cut(self.dst[a].at[j], a, q * size + first, size - first)
        return self.cut(self.dst[a].at[j], a, q * size, first)

    def own_copy(self, a, up):
        at = self.at
        to = at.s + 1 if up else at.s - 1
        return remote(
            self.part(self.src[a], a, at.p), self.got(a, at.s, at.p), self.sz.at[0 if up else 1, a], self.rz.at[a, at.s],
            at.along(jnp.clip(to, 0, at.n - 1)),
        )

    def own(self, a):
        pl.when(self.at.s < self.at.n - 1)(lambda: self.own_copy(a, True).start())
        pl.when(self.at.s > 0)(lambda: self.own_copy(a, False).start())

    def forward(self, a, t, up):
        at = self.at
        j = at.s - t if up else at.s + t
        to = at.s + 1 if up else at.s - 1
        came = (j >= 0) if up else (j < at.n)
        goes = (to < at.n) if up else (to >= 0)
        view = self.got(a, jnp.clip(j, 0, at.n - 1), at.p)
        sem = self.rz.at[a, jnp.clip(j, 0, at.n - 1)]
        copy = remote(view, view, self.sz.at[2 * t + (0 if up else 1), a], sem, at.along(jnp.clip(to, 0, at.n - 1)))
        return came, came & goes, copy

    def line(self, a, t):
        for up in (True, False):
            _, goes, _ = self.forward(a, t, up)

            @pl.when(goes)
            def _():
                copy = self.forward(a, t, up)[2]
                copy.wait_recv()
                copy.start()

    def send(self, view, a, j, k, kind, bit):
        remote(view, view, self.sp.at[kind, a, k - 1], self.rp.at[kind, a, j], self.at.across(bit)).start()

    def wait(self, view, a, j, kind):
        remote(view, view, self.sp.at[kind, a, 0], self.rp.at[kind, a, j], self.at.across(1)).wait_recv()

    def place(self, k):
        return item(k, self.at.s, self.at.n)[0]

    def spread(self, a, k):
        j = self.place(k)
        view = self.got(a, j, self.at.p)

        @pl.when((self.at.s == 0) | (self.at.s == self.at.n - 1))
        def _():
            remote(view, view, self.sz.at[0, a], self.rz.at[a, j], self.at.across(1)).wait_recv()

        self.send(view, a, j, k, 0, 2)
        self.send(view, a, j, k, 1, 4)
        self.send(view, a, j, k, 3, 1)

    def corner(self, a, k):
        at, j = self.at, self.place(k)
        from_x, from_y = self.got(a, j, at.q2), self.got(a, j, at.q4)
        self.wait(from_x, a, j, 0)
        self.send(self.half(a, j, at.q2, True), a, j, k, 7, 4)
        self.send(from_x, a, j, k, 4, 1)
        self.wait(from_y, a, j, 1)
        self.send(self.half(a, j, at.q4, False), a, j, k, 2, 2)
        self.send(from_y, a, j, k, 5, 1)

    def twin(self, a, k):
        at, j = self.at, self.place(k)
        self.wait(self.half(a, j, at.q6, False), a, j, 2)
        self.wait(self.half(a, j, at.q6, True), a, j, 7)
        self.send(self.got(a, j, at.q6), a, j, k, 6, 1)

    def ready(self, a, k):
        at, j = self.at, self.place(k)
        for kind, q in ((3, at.q1), (4, at.q3), (5, at.q5), (6, at.q7)):
            self.wait(self.got(a, j, q), a, j, kind)

    def drain(self):
        at = self.at
        for a in range(len(self.geo)):
            pl.when(at.s < at.n - 1)(lambda: self.own_copy(a, True).wait_send())
            pl.when(at.s > 0)(lambda: self.own_copy(a, False).wait_send())

            def body(k, carry):
                for up in (True, False):
                    _, goes, copy = self.forward(a, k, up)
                    pl.when(goes)(lambda: copy.wait_send())
                j = self.place(k)
                whole = self.got(a, j, at.p)
                for kind, view in (
                    (0, whole), (1, whole), (2, self.half(a, j, at.p, False)), (3, whole), (4, whole), (5, whole), (6, whole),
                    (7, self.half(a, j, at.p, True)),
                ):
                    remote(view, view, self.sp.at[kind, a, k - 1], self.rp.at[kind, a, j], at.across(1)).wait_send()
                return carry

            lax.fori_loop(1, at.n, body, 0)


class Line:
    def __init__(self, at, i, ssem, rsem):
        self.at, self.i, self.ssem, self.rsem = at, i, ssem, rsem

    def start(self, view_of, into, only=None):
        at = self.at
        self.into = into
        for r in range(1, at.n) if only is None else (only,):
            d = lax.rem(at.s + r, at.n)
            remote(view_of(d), into.at[at.s], self.ssem.at[self.i, r], self.rsem.at[self.i, at.s], at.along(d)).start()

    def arrived(self):
        at = self.at
        for r in range(1, at.n):
            d = lax.rem(at.s + r, at.n)
            view = self.into.at[d]
            remote(view, view, self.ssem.at[self.i, r], self.rsem.at[self.i, d], at.along(d)).wait_recv()

    def sent(self):
        view = self.into.at[0]
        for r in range(1, self.at.n):
            remote(view, view, self.ssem.at[self.i, r], self.rsem.at[self.i, 0], self.at.across(1)).wait_send()


def iota(shape, axis):
    return lax.broadcasted_iota(jnp.int32, shape, axis)


def one_hot(hit):
    return jnp.where(hit, 1.0, 0.0).astype(BF16)


def sources(deal, n, rows):
    src = jnp.zeros_like(deal)
    for k in range(1, n):
        src = src + jnp.where(deal >= k * rows, 1, 0)
    return src


def sending_order(deal_ref, s, n, rows):
    cap = rows // n
    before = one_hot(iota((rows, rows), 0) < iota((rows, rows), 1))
    deal = jnp.concatenate([deal_ref[:, b * rows : (b + 1) * rows] for b in range(n)], axis=0)
    if n < 8:
        deal = jnp.concatenate([deal, jnp.full((8 - n, rows), -1, jnp.int32)], axis=0)
    hit = (sources(deal, n, rows) == s) & (deal >= 0)
    rank = nn(one_hot(hit), before).astype(jnp.int32)
    place = jnp.where(hit, rank + iota(deal.shape, 0) * cap, -1)
    mine = deal - s * rows
    total = jnp.zeros((rows, rows), F32)
    row = iota((rows, rows), 0)
    for b in range(n):
        total = total + nt(one_hot(row == place[b : b + 1, :]), one_hot(row == mine[b : b + 1, :]))
    return total.astype(BF16)


def collecting_order(deal_ref, before, s, n, rows):
    cap = rows // n
    deal = deal_ref[:, pl.ds(pl.multiple_of(s * rows, 128), rows)]
    kind = iota((8, rows), 0)
    hit = jnp.broadcast_to(sources(deal, n, rows), (8, rows)) == kind
    rank = nn(one_hot(hit), before).astype(jnp.int32)
    place = jnp.sum(jnp.where(hit, rank + kind * cap, 0).astype(F32), axis=0, keepdims=True).astype(jnp.int32)
    return one_hot(iota((rows, LIVE), 0) == place[:, :LIVE])


def slots_of(len_ref, idx_ref, pos_ref, mask_ref):
    slot = iota((LIVE, NAR), 0)
    lane = iota((LIVE, NAR), 1)
    count = len_ref.shape[1]
    start = jnp.zeros((LIVE, NAR), jnp.int32)
    chosen = jnp.full((LIVE, NAR), idx_ref[0, 0], jnp.int32)
    end = jnp.int32(0)
    for i in range(count):
        end = end + len_ref[0, i]
        passed = slot >= end
        start = jnp.where(passed, end, start)
        chosen = jnp.where(passed, idx_ref[0, i + 1] if i + 1 < count else -1, chosen)
    pos_ref[...] = slot - start
    low = chosen * R
    mask_ref[...] = jnp.where((lane >= low) & (lane < low + R), 1.0, 0.0)


REC_PARTS = ("db", "dg", "dgates", "dm", "ub", "ug", "ugates", "um")
FFN_PARTS = ("dfg", "dfu", "dfd", "ufg", "ufu", "ufd")


def first_kernel(z, geo, *refs):
    n, w, d, h, hp = z.n, z.w, z.d, z.h, z.hp
    refs = list(refs)

    def take(count):
        out, refs[:count] = refs[:count], []
        return out

    len_r, idx_r, deal_r, small_r = take(4)
    tokens, cotangent = take(2)
    ob, og, ogw, om, ofg, ofu, ofd = take(7)
    pieces_r, pieces_f = take(8), take(6)
    gb, gg, ggw, gr, gm, gfg, gfu, gf, gfd = gathered = take(9)
    gtok, gcot, gsm = take(3)
    act1_h, xin_h, mixed_h, ranks_h, rt_h, s_h = take(6)
    conv_h, gi_h, ig_h, rg_h, st_h = take(5)
    out_h, gres_h, grad_h = take(3)
    pack_r, pack_f, rows_out, smv, s_v, rt_v, pos_r, mask_r, act1, resid, ranks = take(11)
    sz, sp, rz, rp, lss, lrs, lsem, psem, osem = take(9)
    at = Plane(n)
    s = at.s
    at.greet()
    net = Gather(at, geo, [ob, og, ogw, pack_r, om, ofg, ofu, pack_f, ofd], gathered, sz, sp, rz, rp)
    rec, ffn = [0, 1, 3, 2, 4], [5, 6, 8]
    net.own(0)
    net.own(1)
    packing = []
    for i, (dst, table, names, parts) in enumerate(((pack_r, z.rec, REC_PARTS, pieces_r), (pack_f, z.ffn, FFN_PARTS, pieces_f))):
        for k, (name, ref) in enumerate(zip(names, parts)):
            size = ref.shape[1]
            copy = pltpu.make_async_copy(ref, dst.at[:, table[name] : table[name] + size], psem.at[i, k])
            copy.start()
            packing.append(copy)
    smv[s] = small_r[...]
    lines = [Line(at, i, lss, lrs) for i in range(3)]
    lines[2].start(lambda place: small_r, gsm)
    for copy in packing:
        copy.wait()
    net.own(3)

    def sending(rows_in):
        toks = [pltpu.make_async_copy(ref, rows_in.at[i], lsem.at[0, i]) for i, ref in enumerate((tokens, cotangent))]
        for copy in toks:
            copy.start()
        order = sending_order(deal_r, s, n, z.rows)
        s_v[...] = order
        for i in range(2):
            toks[i].wait()
            rows_out[i] = nn(order, rows_in[i]).astype(BF16).reshape(n, z.cap, d)

    pl.run_scoped(sending, pltpu.VMEM((2, z.rows, d), BF16))
    before = one_hot(iota((z.rows, z.rows), 0) < iota((z.rows, z.rows), 1))
    rt_v[...] = collecting_order(deal_r, before, s, n, z.rows)
    slots_of(len_r, idx_r, pos_r, mask_r)
    outs = []

    def put(src, dst):
        copy = pltpu.make_async_copy(src, dst, osem.at[len(outs)])
        copy.start()
        outs.append(copy)

    put(s_v, s_h)
    put(rt_v, rt_h)
    put(pack_r, gr.at[s])
    put(small_r, gsm.at[s])
    items = [(a, k) for k in range(1, n) for a in rec] + [(7, k) for k in range(1, n)] + [(a, 1) for a in ffn]
    count = len(items)
    for i in range(count):
        if i in (4, 7, 10):
            for r in range(1, n):
                if (r - 1) % 3 == (4, 7, 10).index(i):
                    lines[0].start(lambda place: rows_out.at[0, place], gtok, r)
        if i + 3 < len(rec):
            net.own(rec[i + 3])
        if i == len(rec):
            net.own(7)
        if 0 <= i - 9 < len(ffn):
            net.own(ffn[i - 9])
        net.line(*items[i])
        net.spread(*items[i])
        if i >= 2 and items[i - 2][0] not in ffn:
            net.corner(*items[i - 2])
        if i >= 4 and items[i - 4][0] not in ffn:
            net.twin(*items[i - 4])
    for i in range(count - 4, count):
        if items[i][0] not in ffn:
            net.twin(*items[i])
    for a, k in items:
        if a in rec:
            net.ready(a, k)
    lines[2].arrived()
    small_in = []
    for r in range(1, n):
        o = lax.rem(s + r, n)
        copy = pltpu.make_async_copy(gsm.at[o], smv.at[o], lsem.at[1, r])
        copy.start()
        small_in.append(copy)
    lines[0].arrived()
    mask = mask_r[...]

    def rows_of(i, got, into, sem):
        keep = into.at[pl.ds(pl.multiple_of(s * z.cap, 8), z.cap)]
        copies = [pltpu.make_async_copy(rows_out.at[i, s], keep, sem.at[0])]
        for r in range(1, n):
            o = lax.rem(s + r, n)
            copies.append(pltpu.make_async_copy(got.at[o], into.at[pl.ds(pl.multiple_of(o * z.cap, 8), z.cap)], sem.at[r]))
        for copy in copies:
            copy.start()
        for copy in copies:
            copy.wait()

    for copy in small_in:
        copy.wait()
    gain1, gain2 = gain_row(smv, 8, n, d), gain_row(smv, 9, n, d)

    def load_pack(pack, got, into, sem):
        rows = NAR // n
        copies = []
        for j in range(n):
            dst = into.at[pl.ds(j * rows, rows)]
            start_either(s, j, pack, got.at[j], dst, sem.at[j])
            copies.append(pltpu.make_async_copy(got.at[j], dst, sem.at[j]))
        return copies

    def recurrent(tok, wb, wg, wgw, wm, adp, conv, gi, hold, cl, mix, acc, lg, tsem, wsem, hsem):
        col = z.rec

        def cols(name, size, j=0):
            return pl.ds(pl.multiple_of(col[name] + j * size, 128), size)

        def load_a(j, slot):
            start_either(s, j, ob, gb.at[j], wb.at[slot], wsem.at[slot, 0])
            start_either(s, j, og, gg.at[j], wg.at[slot], wsem.at[slot, 1])

        def load_b(j, slot):
            start_either(s, j, ogw, ggw.at[j], wgw.at[slot], wsem.at[slot, 2])
            start_either(s, j, om, gm.at[j], wm.at[slot], wsem.at[slot, 3])

        adp_in = load_pack(pack_r, gr, adp, tsem.at[1])
        load_a(jnp.int32(0), 0)
        load_b(jnp.int32(0), 0)
        rows_of(0, gtok, tok, tsem.at[0])
        xin = tn(rt_v[...], tok[...])
        resid[...] = xin
        tok[pl.ds(0, LIVE)] = xin.astype(BF16)
        put(tok.at[pl.ds(0, LIVE)], xin_h)
        act1[...] = (xin * norm_scale(xin) * gain1).astype(BF16)
        put(act1, act1_h)
        for copy in adp_in:
            copy.wait()
        ranks[0] = (nt(act1[...], adp[:, cols("db", d)]) * mask).astype(BF16)
        ranks[1] = (nt(act1[...], adp[:, cols("dg", d)]) * mask).astype(BF16)
        acc[...] = jnp.zeros_like(acc)

        def first_pass(j, carry):
            slot = lax.rem(j, 2)
            pltpu.make_async_copy(ob, wb.at[slot], wsem.at[slot, 0]).wait()
            pltpu.make_async_copy(og, wg.at[slot], wsem.at[slot, 1]).wait()

            @pl.when(j + 1 < n)
            def _():
                load_a(j + 1, 1 - slot)

            s32 = smv[j].astype(F32)
            gi[j] = nn(act1[...], wg[slot]) + nn(ranks[1], adp[:, cols("ug", w, j)])
            lg[:, :w] = nn(act1[...], wb[slot]) + nn(ranks[0], adp[:, cols("ub", w, j)])

            def block(r, last):
                at_rows = pl.ds(pl.multiple_of(r * BLOCK, BLOCK), BLOCK)
                br = lg[at_rows, :w]
                both = jnp.concatenate([last, br], axis=0)
                pos = wide(pos_r[at_rows, :], w)
                total = s32[4:5, :] + s32[0:1, :] * br
                for k in range(1, 4):
                    total = total + jnp.where(pos >= k, both[8 - k : 8 - k + BLOCK, :], 0.0) * s32[k : k + 1, :]
                conv[j, at_rows, :] = total
                cl[j, at_rows, :] = total.astype(BF16)
                return br[BLOCK - 8 :, :]

            lax.fori_loop(0, LIVE // BLOCK, block, jnp.zeros((8, w), F32))
            pltpu.make_async_copy(conv.at[j], conv_h.at[j], hsem.at[0, j]).start()
            pltpu.make_async_copy(gi.at[j], gi_h.at[j], hsem.at[1, j]).start()
            acc[...] += nt(cl[j], adp[:, cols("dgates", w, j)])
            for i, a in enumerate(ffn):
                @pl.when(j == i)
                def _():
                    if n > 2:
                        net.line(a, 2)
                    net.corner(a, 1)
            return carry

        lax.fori_loop(0, n, first_pass, 0)
        lines[1].start(lambda place: rows_out.at[1, place], gcot)
        ranks[2] = (acc[...] * mask).astype(BF16)
        acc[...] = jnp.zeros_like(acc)
        holds = (ig_h, rg_h, st_h)

        def second_pass(j, carry):
            slot = lax.rem(j, 2)
            pltpu.make_async_copy(ogw, wgw.at[slot], wsem.at[slot, 2]).wait()
            pltpu.make_async_copy(om, wm.at[slot], wsem.at[slot, 3]).wait()

            @pl.when(j + 1 < n)
            def _():
                load_b(j + 1, 1 - slot)

            @pl.when(j >= 2)
            def _():
                for i, ref in enumerate(holds):
                    pltpu.make_async_copy(hold.at[slot, i], ref.at[j - 2], hsem.at[2 + i, slot]).wait()

            s32 = smv[j].astype(F32)
            low = cl[j]
            lift = nn(ranks[2], adp[:, cols("ugates", 2 * w, j)])
            bias = jnp.concatenate([s32[6:7, :], s32[7:8, :]], axis=1)
            lg[...] = jnp.concatenate(
                [nn(low[:, i * DH : (i + 1) * DH], wgw[slot, i * DH : (i + 1) * DH, :]) for i in range(z.heads)], axis=1
            ) + bias + lift

            def block(r, carry):
                at_rows = pl.ds(pl.multiple_of(r * BLOCK, BLOCK), BLOCK)
                ig, rg = gates_of(lg[at_rows, :], z)
                first = wide(pos_r[at_rows, :], w) == 0
                _, a, scale = decay_of(s32, rg, first)
                hold[slot, 0, at_rows, :] = ig
                hold[slot, 1, at_rows, :] = rg
                state, _, carry = scan_block(a, scale * ig * conv[j, at_rows, :], carry, False)
                hold[slot, 2, at_rows, :] = state
                act, _ = gelu_parts(gi[j, at_rows, :])
                mix[j, at_rows, :] = (state * act).astype(BF16)
                return carry

            lax.fori_loop(0, LIVE // BLOCK, block, jnp.zeros((8, w), F32))
            for i, ref in enumerate(holds):
                pltpu.make_async_copy(hold.at[slot, i], ref.at[j], hsem.at[2 + i, slot]).start()
            acc[...] += nt(mix[j], adp[:, cols("dm", w, j)])
            resid[...] += nn(mix[j], wm[slot])
            for i, a in enumerate(ffn):
                @pl.when(j == i)
                def _():
                    if n > 2:
                        net.spread(a, 2)
                    if n > 3:
                        net.line(a, 3)
            return carry

        lax.fori_loop(0, n, second_pass, 0)
        put(mix, mixed_h)
        ranks[3] = (acc[...] * mask).astype(BF16)
        put(ranks, ranks_h)
        resid[...] = resid[...] + nn(ranks[3], adp[:, cols("um", d)])
        for j in range(n):
            pltpu.make_async_copy(conv.at[j], conv_h.at[j], hsem.at[0, j]).wait()
            pltpu.make_async_copy(gi.at[j], gi_h.at[j], hsem.at[1, j]).wait()
        for j in (n - 2, n - 1):
            for i, ref in enumerate(holds):
                pltpu.make_async_copy(hold.at[j % 2, i], ref.at[j], hsem.at[2 + i, j % 2]).wait()
        for copy in outs[4:]:
            copy.wait()

    V = pltpu.VMEM
    pl.run_scoped(
        recurrent,
        V((z.rows, d), BF16), V((2, d, w), BF16), V((2, d, w), BF16), V((2, w, 2 * DH), BF16), V((2, w, d), BF16),
        V((NAR, z.rec_cols), BF16), V((n, LIVE, w), F32), V((n, LIVE, w), F32), V((2, 3, LIVE, w), F32),
        V((n, LIVE, w), BF16), V((n, LIVE, w), BF16), V((LIVE, NAR), F32), V((LIVE, 2 * w), F32),
        DMA((2, n)), DMA((2, 4)), DMA((5, n)),
    )

    def feed(tok, wg, wu, wd, adp, act2, gl, acc_o, acc_g, rk, ra, grad_o, hgs, hus, ghs, low, ghg, ghu, tsem, wsem):
        col = z.ffn

        def cols(name, size, j=0, stride=0):
            return pl.ds(pl.multiple_of(col[name] + j * stride, 128), size)

        base = resid[...]
        act2[...] = (base * norm_scale(base) * gain2).astype(BF16)
        acc_o[...] = jnp.zeros_like(acc_o)
        acc_g[...] = jnp.zeros_like(acc_g)
        ra[...] = jnp.zeros_like(ra)
        weights = ((5, ofg, gfg, wg), (6, ofu, gfu, wu), (8, ofd, gfd, wd))
        for k in range(1, n):
            net.ready(7, k)

        def onward(q):
            for a in ffn:
                @pl.when(q + 3 < n)
                def _():
                    net.spread(a, q + 3)

                @pl.when(q + 4 < n)
                def _():
                    net.line(a, q + 4)

        def settle(q):
            for a in ffn:
                @pl.when(q + 1 < n)
                def _():
                    net.twin(a, q + 1)

            for a in ffn:
                @pl.when(q + 2 < n)
                def _():
                    net.corner(a, q + 2)

        def step(q, carry):
            j = jnp.where(q == 0, s, item(jnp.maximum(q, 1), s, n)[0])
            def fetch(i):
                a, mine, got, into = weights[i]

                @pl.when(q > 0)
                def _():
                    net.ready(a, q)
                    pltpu.make_async_copy(got.at[j], into, wsem.at[i]).start()

            fetch(0)
            fetch(1)
            pl.when(q < n - 1)(lambda: fetch(2))
            fg, fu, fd = cols("ufg", h, j, hp), cols("ufu", h, j, hp), cols("dfd", h, j, hp)
            pltpu.make_async_copy(ofg, wg, wsem.at[0]).wait()
            hgs[...] = nn(act2[...], wg[...]) + nn(rk[0], adp[:, fg])
            onward(q)
            pltpu.make_async_copy(ofu, wu, wsem.at[1]).wait()
            hus[...] = nn(act2[...], wu[...]) + nn(rk[1], adp[:, fu])
            @pl.when(q == 0)
            def _():
                lines[1].arrived()
                rows_of(1, gcot, tok, tsem.at[0])
                gl[...] = tn(rt_v[...], tok[...]).astype(BF16)
                rk[2] = (nt(gl[...], adp[:, cols("ufd", d)]) * mask).astype(BF16)

            pl.when(q == n - 1)(lambda: fetch(2))
            pltpu.make_async_copy(ofd, wd, wsem.at[2]).wait()
            ghs[...] = nt(gl[...], wd[...]) + nn(rk[2], adp[:, fd])

            def block(r, carry):
                at_rows = pl.ds(pl.multiple_of(r * 16, 16), 16)
                act, slope = gelu_parts(hgs[at_rows, :])
                hu, gh = hus[at_rows, :], ghs[at_rows, :]
                low[at_rows, :] = (act * hu).astype(BF16)
                ghg[at_rows, :] = (gh * hu * slope).astype(BF16)
                ghu[at_rows, :] = (gh * act).astype(BF16)
                return carry

            lax.fori_loop(0, LIVE // 16, block, 0)
            acc_o[...] += nn(low[...], wd[...])
            ra[0] += nt(low[...], adp[:, fd])
            ra[1] += nt(ghg[...], adp[:, fg])
            ra[2] += nt(ghu[...], adp[:, fu])
            acc_g[...] += nt(ghg[...], wg[...]) + nt(ghu[...], wu[...])
            grad_o[:, fd] = tn(rk[2], low[...]).astype(BF16)
            grad_o[:, fg] = tn(rk[0], ghg[...]).astype(BF16)
            grad_o[:, fu] = tn(rk[1], ghu[...]).astype(BF16)
            settle(q)
            return carry

        adp_in = load_pack(pack_f, gf, adp, tsem.at[1])
        for i, (a, mine, got, into) in enumerate(weights):
            pltpu.make_async_copy(mine, into, wsem.at[i]).start()
        for copy in adp_in:
            copy.wait()
        rk[0] = (nt(act2[...], adp[:, cols("dfg", d)]) * mask).astype(BF16)
        rk[1] = (nt(act2[...], adp[:, cols("dfu", d)]) * mask).astype(BF16)
        lax.fori_loop(0, n, step, 0)
        rank = (ra[0] * mask).astype(BF16)
        work = resid[...] + acc_o[...] + nn(rank, adp[:, cols("ufd", d)])
        tok[...] = nn(rt_v[...], work.astype(BF16)).astype(BF16)
        put(tok, out_h)
        grad_o[:, cols("ufd", d)] = tn(rank, gl[...]).astype(BF16)
        rank_g = (ra[1] * mask).astype(BF16)
        rank_u = (ra[2] * mask).astype(BF16)
        grad_o[:, cols("dfg", d)] = tn(rank_g, act2[...]).astype(BF16)
        grad_o[:, cols("dfu", d)] = tn(rank_u, act2[...]).astype(BF16)
        gact = acc_g[...] + nn(rank_g, adp[:, cols("dfg", d)]) + nn(rank_u, adp[:, cols("dfu", d)])
        put(grad_o, grad_h)
        resid[...] = gl[...].astype(F32) + norm_back(resid[...], gact * gain2)
        put(resid, gres_h)
        for copy in outs[8:]:
            copy.wait()

    pl.run_scoped(
        feed,
        V((z.rows, d), BF16), V((d, h), BF16), V((d, h), BF16), V((h, d), BF16), V((NAR, z.ffn_cols), BF16),
        V((LIVE, d), BF16), V((LIVE, d), BF16), V((LIVE, d), F32), V((LIVE, d), F32),
        V((3, LIVE, NAR), BF16), V((3, LIVE, NAR), F32), V((NAR, z.ffn_cols), BF16),
        V((LIVE, h), F32), V((LIVE, h), F32), V((LIVE, h), F32), V((LIVE, h), BF16), V((LIVE, h), BF16), V((LIVE, h), BF16),
        DMA((2, n)), DMA((3,)),
    )
    for line in lines:
        line.sent()
    for copy in outs[:4]:
        copy.wait()
    net.drain()


def run_first(z, geo, *args):
    n, w, d = z.n, z.w, z.d
    S, V = jax.ShapeDtypeStruct, pltpu.VMEM
    sources_ = args[6:13]
    shapes = [sources_[0], sources_[1], sources_[2], (NAR // n, z.rec_cols), sources_[3], sources_[4], sources_[5], (NAR // n, z.ffn_cols), sources_[6]]
    outs = [S((n,) + tuple(x.shape if hasattr(x, "shape") else x), BF16) for x in shapes]
    na = len(outs)
    outs += [S((n, z.cap, d), BF16)] * 2 + [S((n, 16, w), BF16)]
    outs += [S((LIVE, d), BF16), S((LIVE, d), BF16), S((n, LIVE, w), BF16), S((4, LIVE, NAR), BF16), S((z.rows, LIVE), BF16), S((z.rows, z.rows), BF16)]
    outs += [S((n, LIVE, w), F32)] * 5
    outs += [S((z.rows, d), BF16), S((LIVE, d), F32), S((NAR, z.ffn_cols), BF16)]
    SM = pl.BlockSpec(memory_space=pltpu.SMEM)
    return pl.pallas_call(
        functools.partial(first_kernel, z, geo),
        out_shape=outs,
        in_specs=[SM, SM, VM, VM] + [ANY] * (len(args) - 4),
        out_specs=[ANY] * len(outs),
        scratch_shapes=[
            V((NAR // n, z.rec_cols), BF16), V((NAR // n, z.ffn_cols), BF16), V((2, n, z.cap, d), BF16), V((n, 16, w), BF16),
            V((z.rows, z.rows), BF16), V((z.rows, LIVE), BF16), V((LIVE, NAR), jnp.int32), V((LIVE, NAR), F32),
            V((LIVE, d), BF16), V((LIVE, d), F32), V((4, LIVE, NAR), BF16),
            DMA((2 * n, na)), DMA((8, na, n - 1)), DMA((na, n)), DMA((8, na, n)), DMA((3, n)), DMA((3, n)),
            DMA((2, n)), DMA((2, 8)), DMA((11,)),
        ],
        compiler_params=pltpu.CompilerParams(collective_id=1, has_side_effects=True, vmem_limit_bytes=VLIMIT),
        name="first",
    )(*args)


def add_rows(dst, left, right, rows, step=16):
    def body(r, carry):
        at_rows = pl.ds(pl.multiple_of(r * step, step), step)
        dst[at_rows, :] = (left[at_rows, :].astype(F32) + right[at_rows, :].astype(F32)).astype(BF16)
        return carry

    lax.fori_loop(0, rows // step, body, 0)


class Reduce:
    def __init__(self, at, t, clusters, width, source, own, fin, bufs, sems):
        self.at, self.t, self.clusters, self.c = at, t, clusters, width
        self.source, self.own, self.fin = source, own, fin
        self.rc, self.r1, self.r2, self.rg, self.rz, self.sm = bufs
        self.ss, self.rs, self.zs, self.zr, self.gs, self.gr, self.ps, self.pr = [x.at[t] for x in sems]
        p = at.p
        self.core, self.x, self.y = p % 2, (p // 2) % 2, p // 4
        self.rows, self.half = NAR // at.n, NAR // 2
        self.final = 1 if clusters > 1 else 0

    def cut(self, q):
        return pl.ds(pl.multiple_of(q * self.c, 128), self.c)

    def send(self, src, dst, a, b, device):
        remote(src, dst, a, b, device).start()

    def arrived(self, dst, a, b):
        remote(dst, dst, a, b, self.at.across(1)).wait_recv()

    def to_core(self):
        for c in range(4):
            self.send(self.source.at[:, self.cut(2 * c + 1 - self.core)], self.rc.at[c], self.ss.at[c], self.rs.at[c], self.at.across(1))

    def to_first(self):
        for c in range(4):
            self.arrived(self.rc.at[c], self.ss.at[c], self.rs.at[c])
            add_rows(self.rc.at[c], self.own(c), self.rc.at[c], NAR)
        low, high = pl.ds(0, self.half), pl.ds(self.half, self.half)
        for i in range(2):
            self.send(self.rc.at[2 * i + 1 - self.x, low], self.r1.at[0, i], self.ss.at[4 + i], self.rs.at[4 + i], self.at.across(2))
            self.send(self.rc.at[2 * (1 - self.y) + i, high], self.r1.at[1, i], self.ss.at[6 + i], self.rs.at[6 + i], self.at.across(4))

    def to_second(self):
        low, high = pl.ds(0, self.half), pl.ds(self.half, self.half)
        for i in range(2):
            self.arrived(self.r1.at[0, i], self.ss.at[4 + i], self.rs.at[4 + i])
            add_rows(self.r1.at[0, i], self.rc.at[2 * i + self.x, low], self.r1.at[0, i], self.half)
            self.arrived(self.r1.at[1, i], self.ss.at[6 + i], self.rs.at[6 + i])
            add_rows(self.r1.at[1, i], self.rc.at[2 * self.y + i, high], self.r1.at[1, i], self.half)
        self.send(self.r1.at[0, 1 - self.y], self.r2.at[0, low], self.ss.at[8], self.rs.at[8], self.at.across(4))
        self.send(self.r1.at[1, 1 - self.x], self.r2.at[0, high], self.ss.at[9], self.rs.at[9], self.at.across(2))

    def to_line(self):
        at = self.at
        low, high = pl.ds(0, self.half), pl.ds(self.half, self.half)
        self.arrived(self.r2.at[0, low], self.ss.at[8], self.rs.at[8])
        add_rows(self.r2.at[0, low], self.r1.at[0, self.y], self.r2.at[0, low], self.half)
        self.arrived(self.r2.at[0, high], self.ss.at[9], self.rs.at[9])
        add_rows(self.r2.at[0, high], self.r1.at[1, self.x], self.r2.at[0, high], self.half)
        if self.clusters > 1:
            mine = at.rep // PLANE
            for r in range(1, self.clusters):
                device = {"rep": lax.rem(at.rep + r * PLANE, self.clusters * PLANE), "shard": at.s}
                self.send(self.r2.at[0], self.rg.at[mine], self.gs.at[r], self.gr.at[mine], device)
            self.rg[mine] = self.r2[0]
            for r in range(1, self.clusters):
                other = lax.rem(mine + r, self.clusters)
                self.arrived(self.rg.at[other], self.gs.at[r], self.gr.at[other])
            add_rows(self.r2.at[1], self.rg.at[0], self.rg.at[1], NAR)
            for other in range(2, self.clusters):
                add_rows(self.r2.at[1], self.rg.at[other], self.r2.at[1], NAR)
        for r in range(1, at.n):
            d = lax.rem(at.s + r, at.n)
            chunk = pl.ds(pl.multiple_of(d * self.rows, self.rows), self.rows)
            self.send(self.r2.at[self.final, chunk], self.rz.at[at.s], self.zs.at[r], self.zr.at[at.s], at.along(d))

    def to_plane(self):
        at = self.at
        total = self.r2[self.final, pl.ds(pl.multiple_of(at.s * self.rows, self.rows), self.rows), :].astype(F32)
        for r in range(1, at.n):
            d = lax.rem(at.s + r, at.n)
            self.arrived(self.rz.at[d], self.zs.at[r], self.zr.at[d])
            total = total + self.rz[d].astype(F32)
        self.sm[...] = total.astype(BF16)
        self.fin[:, self.cut(at.p)] = total.astype(BF16)
        for kind, bit in ((0, 2), (1, 4), (3, 1)):
            self.spread(kind, at.p, bit, self.sm)

    def spread(self, kind, q, bit, src=None):
        view = self.fin.at[:, self.cut(q)]
        self.send(view if src is None else src, view, self.ps.at[kind], self.pr.at[kind], self.at.across(bit))

    def spread_wait(self, kind, q):
        self.arrived(self.fin.at[:, self.cut(q)], self.ps.at[kind], self.pr.at[kind])

    def over(self):
        at = self.at
        self.spread_wait(0, at.q2)
        if self.t % 2 == 0:
            self.spread(2, at.q2, 4)
        self.spread(4, at.q2, 1)
        self.spread_wait(1, at.q4)
        if self.t % 2 == 1:
            self.spread(2, at.q4, 2)
        self.spread(5, at.q4, 1)

    def last(self):
        self.spread_wait(2, self.at.q6)
        self.spread(6, self.at.q6, 1)

    def end(self):
        at = self.at
        for kind, q in ((3, at.q1), (4, at.q3), (5, at.q5), (6, at.q7)):
            self.spread_wait(kind, q)
        sent = [(self.rc.at[0], self.ss.at[c]) for c in range(4)]
        sent += [(self.r1.at[0, 0], self.ss.at[4 + i]) for i in range(4)]
        sent += [(self.r2.at[0, pl.ds(0, self.half)], self.ss.at[8 + i]) for i in range(2)]
        sent += [(self.rg.at[0], self.gs.at[r]) for r in range(1, self.clusters)]
        sent += [(self.rz.at[0], self.zs.at[r]) for r in range(1, at.n)]
        sent += [(self.sm, self.ps.at[kind]) for kind in range(7)]
        for view, sem in sent:
            remote(view, view, sem, sem, at.across(1)).wait_send()


def early_table(z):
    return {"um": 0, "dm": z.d, "ugates": z.d + z.n * z.w}, up_to(z.d + 3 * z.n * z.w, 128 * PLANE)


def late_table(z):
    lru = z.n * z.w
    return {"dgates": 0, "ub": lru, "ug": 2 * lru, "db": 3 * lru, "dg": 3 * lru + z.d}, up_to(3 * lru + 2 * z.d, 128 * PLANE)


def second_kernel(z, clusters, *refs):
    n, w, d = z.n, z.w, z.d
    refs = list(refs)

    def take(count):
        out, refs[:count] = refs[:count], []
        return out

    len_r, idx_r, rt_v, gres, ranks = take(5)
    sm_h, ob, og, ogw, om, gb, gg, ggw, gm, gr = take(10)
    conv_h, gi_h, ig_h, rg_h, st_h, act1_h, xin_h, mixed_h, out_h, gradf_h = take(10)
    back_out, back_tok, fin_f, fin_e, fin_l = take(5)
    pos_r, mask_r, smv, adp, glm, gdir, glow, gilow, gmix, acc, rk, accg, tokv, grad_e, grad_l, own_f = take(16)
    bufs = [take(6) for _ in range(3)]
    sems = take(8)
    lss, lrs, lsem = take(3)
    at = Plane(n)
    s = at.s
    at.greet(clusters)
    lines = [Line(at, i, lss, lrs) for i in range(2)]
    lines[0].start(lambda place: out_h.at[place], back_out)
    keep = pltpu.make_async_copy(out_h.at[s], back_out.at[s], lsem.at[0, 0])
    keep.start()
    (early, _), (late, _) = early_table(z), late_table(z)
    core = at.p % 2

    def own_of(ref, width):
        return lambda c: ref.at[:, pl.ds(pl.multiple_of((2 * c + core) * width, 128), width)]

    widths = [x.shape[2] for x in (bufs[0][0], bufs[1][0], bufs[2][0])]
    red_f = Reduce(at, 0, clusters, widths[0], gradf_h, lambda c: own_f.at[c], fin_f, bufs[0], sems)
    red_e = Reduce(at, 1, clusters, widths[1], grad_e, own_of(grad_e, widths[1]), fin_e, bufs[1], sems)
    red_l = Reduce(at, 2, clusters, widths[2], grad_l, own_of(grad_l, widths[2]), fin_l, bufs[2], sems)
    red_f.to_core()
    rows = NAR // n
    own_in = [pltpu.make_async_copy(own_of(gradf_h, widths[0])(c), own_f.at[c], lsem.at[1, c]) for c in range(4)]
    packs = [pltpu.make_async_copy(gr.at[j], adp.at[pl.ds(j * rows, rows)], lsem.at[2, j]) for j in range(n)]
    small_in = pltpu.make_async_copy(sm_h, smv, lsem.at[0, 1])
    for copy in own_in + packs + [small_in]:
        copy.start()
    slots_of(len_r, idx_r, pos_r, mask_r)
    mask = mask_r[...]
    col = z.rec

    def cols(name, size, j=0):
        return pl.ds(pl.multiple_of(col[name] + j * size, 128), size)

    def put_at(table, name, size, j=0):
        return pl.ds(pl.multiple_of(table[name] + j * size, 128), size)

    def rows_at(r):
        return pl.ds(pl.multiple_of(r * BLOCK, BLOCK), BLOCK)

    blocks = LIVE // BLOCK

    def state_pass(sav, wm, mixed, ssem):
        saved = (conv_h, gi_h, ig_h, rg_h, st_h)

        def load(j, slot):
            start_either(s, j, om, gm.at[j], wm.at[slot], ssem.at[slot, 5])
            for i, ref in enumerate(saved):
                pltpu.make_async_copy(ref.at[j], sav.at[slot, i], ssem.at[slot, i]).start()
            pltpu.make_async_copy(mixed_h.at[j], mixed.at[slot], ssem.at[slot, 6]).start()

        def load_wait(slot):
            pltpu.make_async_copy(om, wm.at[slot], ssem.at[slot, 5]).wait()
            for i, ref in enumerate(saved):
                pltpu.make_async_copy(ref.at[0], sav.at[slot, i], ssem.at[slot, i]).wait()
            pltpu.make_async_copy(mixed_h.at[0], mixed.at[slot], ssem.at[slot, 6]).wait()

        load(jnp.int32(0), 0)
        glm[...] = gres[...].astype(BF16)
        for copy in packs + [small_in]:
            copy.wait()
        rk[0] = (nt(glm[...], adp[:, cols("um", d)]) * mask).astype(BF16)
        grad_e[:, put_at(early, "um", d)] = tn(ranks[3], glm[...]).astype(BF16)
        acc[...] = jnp.zeros_like(acc)
        for copy in own_in:
            copy.wait()
        red_f.to_first()

        def body(j, carry):
            slot = lax.rem(j, 2)
            load_wait(slot)

            @pl.when(j + 1 < n)
            def _():
                load(j + 1, 1 - slot)

            s32 = smv[j].astype(F32)
            gmix[...] = nt(glm[...], wm[slot]) + nn(rk[0], adp[:, cols("dm", w, j)])
            grad_e[:, put_at(early, "dm", w, j)] = tn(rk[0], mixed[slot]).astype(BF16)

            def block(i, carry):
                at_rows = rows_at(blocks - 1 - i)
                gmx, conv, ig = gmix[at_rows, :], sav[slot, 0, at_rows, :], sav[slot, 2, at_rows, :]
                rg, state = sav[slot, 3, at_rows, :], sav[slot, 4, at_rows, :]
                act, slope = gelu_parts(sav[slot, 1, at_rows, :])
                gilow[j, at_rows, :] = (gmx * state * slope).astype(BF16)
                first = wide(pos_r[at_rows, :], w) == 0
                soft, a, scale = decay_of(s32, rg, first)
                x = gmx * act
                _, after, carry = scan_block(a, a * x, carry, True)
                total = x + after
                drive = total * scale
                gdir[j, at_rows, :] = drive * ig
                fed = ig * conv
                kept = total * (state - scale * fed)
                g_log = jnp.where(first, 0.0, kept - total * fed * (a * a) / scale)
                l_in = drive * conv * ig * (1.0 - ig)
                l_rec = -soft * g_log * rg * (1.0 - rg)
                for i in range(z.heads):
                    glow[j, at_rows, 2 * i * DH : (2 * i + 1) * DH] = l_in[:, i * DH : (i + 1) * DH].astype(BF16)
                    glow[j, at_rows, (2 * i + 1) * DH : (2 * i + 2) * DH] = l_rec[:, i * DH : (i + 1) * DH].astype(BF16)
                return carry

            lax.fori_loop(0, blocks, block, jnp.zeros((8, w), F32))
            acc[...] += nt(glow[j], adp[:, cols("ugates", 2 * w, j)])
            grad_e[:, put_at(early, "ugates", 2 * w, j)] = tn(ranks[2], glow[j]).astype(BF16)
            pl.when(j == 1)(red_f.to_second)
            pl.when(j == 2)(red_f.to_line)
            return carry

        lax.fori_loop(0, n, body, 0)

    V = pltpu.VMEM
    pl.run_scoped(state_pass, V((2, 5, LIVE, w), F32), V((2, w, d), BF16), V((2, LIVE, w), BF16), DMA((2, 7)))
    rk[1] = (acc[...] * mask).astype(BF16)
    red_e.to_core()

    def branch_pass(wb, wg, wgw, conv, blow, act1, xin, grads_rank, wsem, asem):
        def load(j, slot):
            start_either(s, j, ob, gb.at[j], wb.at[slot], wsem.at[slot, 0])
            start_either(s, j, og, gg.at[j], wg.at[slot], wsem.at[slot, 1])
            start_either(s, j, ogw, ggw.at[j], wgw.at[slot], wsem.at[slot, 2])
            pltpu.make_async_copy(conv_h.at[j], conv.at[slot], wsem.at[slot, 3]).start()

        ends = [pltpu.make_async_copy(act1_h, act1, asem.at[0]), pltpu.make_async_copy(xin_h, xin, asem.at[1])]
        load(jnp.int32(0), 0)
        for copy in ends:
            copy.start()
        accg[...] = jnp.zeros_like(accg)
        grads_rank[...] = jnp.zeros_like(grads_rank)

        def body(j, carry):
            slot = lax.rem(j, 2)
            for i, (ref, into) in enumerate(((ob, wb), (og, wg), (ogw, wgw), (conv_h.at[0], conv))):
                pltpu.make_async_copy(ref, into.at[slot], wsem.at[slot, i]).wait()

            @pl.when(j + 1 < n)
            def _():
                load(j + 1, 1 - slot)

            s32 = smv[j].astype(F32)
            grad_l[:, put_at(late, "dgates", w, j)] = tn(rk[1], conv[slot].astype(BF16)).astype(BF16)
            low = glow[j]
            heads = jnp.concatenate(
                [nt(low[:, 2 * i * DH : 2 * (i + 1) * DH], wgw[slot, i * DH : (i + 1) * DH, :]) for i in range(z.heads)], axis=1
            )
            gmix[...] = gdir[j] + heads + nn(rk[1], adp[:, cols("dgates", w, j)])

            def block(i, carry):
                later, later_pos = carry
                at_rows = rows_at(blocks - 1 - i)
                cur, pos = gmix[at_rows, :], pos_r[at_rows, :]
                both = jnp.concatenate([cur, later], axis=0)
                both_pos = jnp.concatenate([pos, later_pos], axis=0)
                total = cur * s32[0:1, :]
                for k in range(1, 4):
                    inside = wide(both_pos[k : k + BLOCK, :], w) >= k
                    total = total + jnp.where(inside, both[k : k + BLOCK, :], 0.0) * s32[k : k + 1, :]
                blow[at_rows, :] = total.astype(BF16)
                return cur[:8, :], pos[:8, :]

            lax.fori_loop(0, blocks, block, (jnp.zeros((8, w), F32), jnp.zeros((8, NAR), jnp.int32)))
            gil = gilow[j]
            grad_l[:, put_at(late, "ub", w, j)] = tn(ranks[0], blow[...]).astype(BF16)
            grad_l[:, put_at(late, "ug", w, j)] = tn(ranks[1], gil).astype(BF16)
            accg[...] += nt(blow[...], wb[slot]) + nt(gil, wg[slot])
            grads_rank[0] += nt(blow[...], adp[:, cols("ub", w, j)])
            grads_rank[1] += nt(gil, adp[:, cols("ug", w, j)])
            pl.when(j == 0)(red_e.to_first)
            pl.when(j == 2)(red_e.to_second)
            pl.when(j == 3)(red_e.to_line)
            return carry

        lax.fori_loop(0, n, body, 0)
        rank_b = (grads_rank[0] * mask).astype(BF16)
        rank_g = (grads_rank[1] * mask).astype(BF16)
        for copy in ends:
            copy.wait()
        gain1 = gain_row(smv, 8, n, d)
        gact = accg[...] + nn(rank_b, adp[:, cols("db", d)]) + nn(rank_g, adp[:, cols("dg", d)])
        gwork = gres[...] + norm_back(xin[...].astype(F32), gact * gain1)
        tokv[...] = nn(rt_v[...], gwork.astype(BF16)).astype(BF16).reshape(n, z.cap, d)
        lines[1].start(lambda place: tokv.at[place], back_tok)
        grad_l[:, put_at(late, "db", d)] = tn(rank_b, act1[...]).astype(BF16)
        grad_l[:, put_at(late, "dg", d)] = tn(rank_g, act1[...]).astype(BF16)

    pl.run_scoped(
        branch_pass, V((2, d, w), BF16), V((2, d, w), BF16), V((2, w, 2 * DH), BF16), V((2, LIVE, w), F32),
        V((LIVE, w), BF16), V((LIVE, d), BF16), V((LIVE, d), BF16), V((2, LIVE, NAR), F32), DMA((2, 4)), DMA((2,)),
    )
    red_l.to_core()
    keep_tok = pltpu.make_async_copy(tokv.at[s], back_tok.at[s], lsem.at[0, 2])
    keep_tok.start()
    red_l.to_first()
    red_f.to_plane()
    red_l.to_second()
    red_f.over()
    red_e.to_plane()
    red_l.to_line()
    red_f.last()
    red_e.over()
    red_e.last()
    red_l.to_plane()
    red_l.over()
    red_l.last()
    for red in (red_f, red_e, red_l):
        red.end()
    for line in lines:
        line.arrived()
        line.sent()
    keep.wait()
    keep_tok.wait()


def run_second(z, clusters, *args):
    n, w, d = z.n, z.w, z.d
    S, V = jax.ShapeDtypeStruct, pltpu.VMEM
    cols = [z.ffn_cols, early_table(z)[1], late_table(z)[1]]
    rows, half = NAR // n, NAR // 2
    outs = [S((n, z.cap, d), BF16)] * 2 + [S((rows, c), BF16) for c in cols]
    scratch = [
        V((LIVE, NAR), jnp.int32), V((LIVE, NAR), F32), V((n, 16, w), BF16), V((NAR, z.rec_cols), BF16), V((LIVE, d), BF16),
        V((n, LIVE, w), F32), V((n, LIVE, 2 * w), BF16), V((n, LIVE, w), BF16), V((LIVE, w), F32), V((LIVE, NAR), F32),
        V((2, LIVE, NAR), BF16), V((LIVE, d), F32), V((n, z.cap, d), BF16), V((NAR, cols[1]), BF16), V((NAR, cols[2]), BF16),
        V((4, NAR, cols[0] // PLANE), BF16),
    ]
    more = clusters > 1
    for size in cols:
        c = size // PLANE
        scratch += [
            V((4, NAR, c), BF16), V((2, 2, half, c), BF16), V((2 if more else 1, NAR, c), BF16),
            V((clusters, NAR, c) if more else (1, 16, 128), BF16), V((n, rows, c), BF16), V((rows, c), BF16),
        ]
    scratch += [DMA((3, 10)), DMA((3, 10)), DMA((3, n)), DMA((3, n)), DMA((3, clusters)), DMA((3, clusters)), DMA((3, 7)), DMA((3, 7))]
    scratch += [DMA((2, n)), DMA((2, n)), DMA((3, max(n, 4)))]
    SM = pl.BlockSpec(memory_space=pltpu.SMEM)
    return pl.pallas_call(
        functools.partial(second_kernel, z, clusters),
        out_shape=outs,
        in_specs=[SM, SM, VM, VM, VM] + [ANY] * (len(args) - 5),
        out_specs=[ANY, ANY, VM, VM, VM],
        scratch_shapes=scratch,
        compiler_params=pltpu.CompilerParams(collective_id=2, has_side_effects=True, vmem_limit_bytes=VLIMIT),
        name="second",
    )(*args)


def local(
    tokens, cotangent, norm_first, branch_weight, gelu_weight, conv_weight, conv_bias, gate_weight, gate_bias,
    decay_param, merge_weight, norm_second, feed_gate, feed_up, feed_down, down_branch, up_branch, down_gelu,
    up_gelu, down_gates, up_gates, down_merge, up_merge, down_feed_gate, up_feed_gate, down_feed_up, up_feed_up,
    down_feed_down, up_feed_down, seq_lengths, adapter_index, deal_order,
):
    n = lax.axis_size("shard")
    clusters = lax.axis_size("rep") // PLANE
    rows, d = tokens.shape
    z = Sizes(n, d, branch_weight.shape[1] * n, feed_gate.shape[1] * n, rows)
    w, pad = z.w, z.hp - z.h

    def spaced(values):
        if pad == 0:
            return values
        parts = values.reshape(values.shape[0], n, z.h)
        return jnp.pad(parts, ((0, 0), (0, 0), (0, pad))).reshape(values.shape[0], n * z.hp)

    rec_own = (down_branch.T, down_gelu.T, down_gates.T, down_merge.T, up_branch, up_gelu, up_gates, up_merge)
    ffn_own = (
        down_feed_gate.T, down_feed_up.T, spaced(down_feed_down.T), spaced(up_feed_gate), spaced(up_feed_up), up_feed_down
    )

    def gain(values):
        return jnp.pad(values, (0, w - values.shape[0]))

    small = jnp.concatenate(
        [conv_weight.reshape(-1), conv_bias, decay_param, gate_bias.reshape(-1), gain(norm_first), gain(norm_second), jnp.zeros((6 * w,), BF16)]
    ).reshape(16, w)
    gates = gate_weight.reshape(w, 2 * DH)
    arrays = [branch_weight, gelu_weight, gates, None, merge_weight, feed_gate, feed_up, None, feed_down]
    sizes = [x.shape[0] if x is not None else 0 for x in arrays]
    geo = [(0, size // PLANE) for size in sizes]
    geo[3], geo[7] = (1, z.rec_cols // PLANE), (1, z.ffn_cols // PLANE)
    weights = (branch_weight, gelu_weight, gates, merge_weight)
    got = run_first(
        z, geo, seq_lengths, adapter_index, deal_order, small, tokens, cotangent, *weights, feed_gate, feed_up, feed_down,
        *rec_own, *ffn_own,
    )
    gb, gg, ggw, gr, gm, _, _, _, _, _, _, sm = got[:12]
    act1, xin, mixed, ranks, rt, order = got[12:18]
    saved = got[18:23]
    out_send, gres, grad_ffn = got[23:]
    back_out, back_tok, fin_f, fin_e, fin_l = run_second(
        z, clusters, seq_lengths, adapter_index, rt, gres, ranks, sm, *weights, gb, gg, ggw, gm, gr, *saved, act1, xin, mixed,
        out_send.reshape(n, z.cap, d), grad_ffn,
    )

    def arrival(received):
        return tn(order, received.reshape(rows, d))

    (early, _), (late, _) = early_table(z), late_table(z)

    def part(values, table, name, size):
        return values[:, table[name] : table[name] + size].astype(F32)

    def unspaced(values):
        if pad == 0:
            return values
        return values.reshape(values.shape[0], n, z.hp)[:, :, : z.h].reshape(values.shape[0], n * z.h)

    lru, ffp = n * w, n * z.hp
    return (
        arrival(back_out),
        arrival(back_tok),
        part(fin_l, late, "db", d).T,
        part(fin_l, late, "ub", lru),
        part(fin_l, late, "dg", d).T,
        part(fin_l, late, "ug", lru),
        part(fin_l, late, "dgates", lru).T,
        part(fin_e, early, "ugates", 2 * lru),
        part(fin_e, early, "dm", lru).T,
        part(fin_e, early, "um", d),
        part(fin_f, z.ffn, "dfg", d).T,
        unspaced(part(fin_f, z.ffn, "ufg", ffp)),
        part(fin_f, z.ffn, "dfu", d).T,
        unspaced(part(fin_f, z.ffn, "ufu", ffp)),
        unspaced(part(fin_f, z.ffn, "dfd", ffp)).T,
        part(fin_f, z.ffn, "ufd", d),
    )


def solution(mesh):
    tok, line, col, row = P(("rep", "shard"), None), P("shard"), P(None, "shard"), P("shard", None)
    in_specs = (
        tok, tok, line, col, col, col, line, P("shard", None, None), row, line, row, line, col, col, row,
    ) + (col, row) * 7 + (tok, tok, P("rep", None))
    out_specs = (tok, tok) + (col, row) * 7
    return jax.shard_map(local, mesh=mesh, in_specs=in_specs, out_specs=out_specs, check_vma=False)
```

```python
import functools

import jax
import jax.numpy as jnp
from jax import lax
from jax.experimental import pallas as pl
from jax.experimental.pallas import tpu as pltpu
from jax.sharding import PartitionSpec as P

NA = 8
R = 16
NAR = NA * R
DH = 128
LIVE = 384
PLANE = 8
EPS = 1e-06
DECAY = 8.0
F32 = jnp.float32
BF16 = jnp.bfloat16
MESH_ID = pl.DeviceIdType.MESH
DMA = pltpu.SemaphoreType.DMA
ANY = pl.BlockSpec(memory_space=pl.ANY)
VM = pl.BlockSpec(memory_space=pltpu.VMEM)
VLIMIT = 60 << 20
GC = 0.7978845608028654
GA = 0.044715


def up_to(size, step):
    return -(-size // step) * step


def nn(a, b):
    return lax.dot_general(a, b, (((1,), (0,)), ((), ())), preferred_element_type=F32)


def nt(a, b):
    return lax.dot_general(a, b, (((1,), (1,)), ((), ())), preferred_element_type=F32)


def tn(a, b):
    return lax.dot_general(a, b, (((0,), (0,)), ((), ())), preferred_element_type=F32)


def gelu_parts(x):
    x2 = x * x
    th = jnp.tanh(GC * x * (1.0 + GA * x2))
    half = 0.5 * (1.0 + th)
    return x * half, half + 0.5 * x * (1.0 - th * th) * (GC * (1.0 + 3.0 * GA * x2))


def neg_expm1(x):
    series = x * (1.0 + x * (1 / 2) * (1.0 + x * (1 / 3) * (1.0 + x * (1 / 4) * (1.0 + x * (1 / 5) * (1.0 + x * (1 / 6))))))
    return jnp.where(x > -0.5, -series, 1.0 - jnp.exp(x))


class Sizes:
    def __init__(self, n, width, lru, ff, rows):
        self.n, self.d, self.rows = n, width, rows
        self.w = lru // n
        self.h = ff // n
        self.hp = up_to(self.h, 128)
        self.heads = self.w // DH
        self.cap = rows // n
        d, w, hp = width, self.w, self.hp
        self.rec = {}
        at = 0
        for name, size in (
            ("db", d), ("dg", d), ("dgates", n * w), ("dm", n * w),
            ("ub", n * w), ("ug", n * w), ("ugates", 2 * n * w), ("um", d),
        ):
            self.rec[name] = at
            at += size
        self.rec_used, self.rec_cols = at, up_to(at, 128 * PLANE)
        self.ffn = {}
        at = 0
        for name, size in (("dfg", d), ("dfu", d), ("dfd", n * hp), ("ufg", n * hp), ("ufu", n * hp), ("ufd", d)):
            self.ffn[name] = at
            at += size
        self.ffn_used, self.ffn_cols = at, up_to(at, 128 * PLANE)


def item(k, s, n):
    m = jnp.minimum(s, n - 1 - s)
    paired = k <= 2 * m
    t = jnp.where(paired, (k + 1) // 2, k - m)
    below = jnp.where(paired, k % 2 == 1, s > n - 1 - s)
    return jnp.where(below, s - t, s + t), below


def remote(src, dst, send, recv, device):
    return pltpu.make_async_remote_copy(src, dst, send, recv, device_id=device, device_id_type=MESH_ID)


def start_either(s, j, own, gathered, dst, sem):
    @pl.when(j == s)
    def _():
        pltpu.make_async_copy(own, dst, sem).start()

    @pl.when(j != s)
    def _():
        pltpu.make_async_copy(gathered, dst, sem).start()


def wide(mask, width):
    return jnp.tile(mask, (1, width // 128))


BLOCK = 32


def scan_block(a, x, carry, reverse):
    rows, width = a.shape
    groups = rows // 8
    a, x = a.reshape(groups, 8, width), x.reshape(groups, 8, width)
    row = lax.broadcasted_iota(jnp.int32, (groups, 8, width), 1)
    for step in (1, 2, 4):
        shift = 8 - step if reverse else step
        inside = row < 8 - step if reverse else row >= step
        x = x + a * jnp.where(inside, pltpu.roll(x, shift, 1), 0.0)
        a = a * jnp.where(inside, pltpu.roll(a, shift, 1), 1.0)
    order = range(groups - 1, -1, -1) if reverse else range(groups)
    edge, far, back = (0, 7, 7) if reverse else (7, 0, 1)
    line = lax.broadcasted_iota(jnp.int32, (8, width), 0)
    values, beside = [None] * groups, [None] * groups
    for g in order:
        value = x[g] + a[g] * carry
        values[g] = value
        beside[g] = jnp.where(line == far, carry, pltpu.roll(value, back, 0))
        carry = jnp.broadcast_to(value[edge : edge + 1, :], (8, width))
    return jnp.concatenate(values, axis=0), jnp.concatenate(beside, axis=0), carry


def norm_scale(values):
    return lax.rsqrt(jnp.mean(values * values, axis=-1, keepdims=True) + EPS)


def gain_row(smv, row, n, d):
    pieces = [smv[j, row : row + 1, : d // n].astype(F32) for j in range(n)]
    return jnp.concatenate(pieces, axis=1)


def gates_of(logits, z):
    heads = z.heads
    ig = jnp.concatenate([logits[:, 2 * i * DH : (2 * i + 1) * DH] for i in range(heads)], axis=1)
    rg = jnp.concatenate([logits[:, (2 * i + 1) * DH : (2 * i + 2) * DH] for i in range(heads)], axis=1)
    return jax.nn.sigmoid(ig), jax.nn.sigmoid(rg)


def decay_of(s32, rg, first):
    soft = DECAY * jnp.log1p(jnp.exp(-s32[5:6, :]))
    log_a = -rg * soft
    a = jnp.where(first, 0.0, jnp.exp(log_a))
    scale = jnp.where(first, 1.0, jnp.sqrt(neg_expm1(2.0 * log_a)))
    return soft, a, scale


def norm_back(values, u):
    scale = norm_scale(values)
    return scale * u - values * (scale * scale * scale * jnp.mean(u * values, axis=-1, keepdims=True))


class Plane:
    def __init__(self, n):
        self.n = n
        self.rep, self.s = lax.axis_index("rep"), lax.axis_index("shard")
        self.p = p = self.rep % PLANE
        self.q1, self.q2, self.q4 = p + self.flip(1) - self.rep, p + self.flip(2) - self.rep, p + self.flip(4) - self.rep
        self.q6 = self.q4 + self.flip(2) - self.rep
        self.q3, self.q5, self.q7 = self.q1 + self.q2 - p, self.q1 + self.q4 - p, self.q1 + self.q6 - p

    def flip(self, bit):
        return self.rep + bit * (1 - 2 * ((self.rep // bit) % 2))

    def across(self, bit):
        return {"rep": self.flip(bit), "shard": self.s}

    def along(self, place):
        return {"rep": self.rep, "shard": place}

    def greet(self, clusters=1):
        barrier = pltpu.get_barrier_semaphore()
        for bit in (1, 2, 4):
            pl.semaphore_signal(barrier, inc=1, device_id=self.across(bit), device_id_type=MESH_ID)
        for r in range(1, self.n):
            pl.semaphore_signal(barrier, inc=1, device_id=self.along(lax.rem(self.s + r, self.n)), device_id_type=MESH_ID)
        for r in range(1, clusters):
            other = {"rep": lax.rem(self.rep + r * PLANE, clusters * PLANE), "shard": self.s}
            pl.semaphore_signal(barrier, inc=1, device_id=other, device_id_type=MESH_ID)
        pl.semaphore_wait(barrier, 3 + self.n - 1 + clusters - 1)


class Gather:
    def __init__(self, at, geo, src, dst, sz, sp, rz, rp):
        self.at, self.geo, self.src, self.dst = at, geo, src, dst
        self.sz, self.sp, self.rz, self.rp = sz, sp, rz, rp

    def cut(self, view, a, start, size):
        if self.geo[a][0] == 0:
            return view.at[pl.ds(pl.multiple_of(start, 8), size)]
        return view.at[:, pl.ds(pl.multiple_of(start, 128), size)]

    def part(self, view, a, q):
        size = self.geo[a][1]
        return self.cut(view, a, q * size, size)

    def got(self, a, j, q):
        return self.part(self.dst[a].at[j], a, q)

    def half(self, a, j, q, second):
        axis, size = self.geo[a]
        step = 8 if axis == 0 else 128
        first = (size // step + 1) // 2 * step
        if second:
            return self.cut(self.dst[a].at[j], a, q * size + first, size - first)
        return self.cut(self.dst[a].at[j], a, q * size, first)

    def own_copy(self, a, up):
        at = self.at
        to = at.s + 1 if up else at.s - 1
        return remote(
            self.part(self.src[a], a, at.p), self.got(a, at.s, at.p), self.sz.at[0 if up else 1, a], self.rz.at[a, at.s],
            at.along(jnp.clip(to, 0, at.n - 1)),
        )

    def own(self, a):
        pl.when(self.at.s < self.at.n - 1)(lambda: self.own_copy(a, True).start())
        pl.when(self.at.s > 0)(lambda: self.own_copy(a, False).start())

    def forward(self, a, t, up):
        at = self.at
        j = at.s - t if up else at.s + t
        to = at.s + 1 if up else at.s - 1
        came = (j >= 0) if up else (j < at.n)
        goes = (to < at.n) if up else (to >= 0)
        view = self.got(a, jnp.clip(j, 0, at.n - 1), at.p)
        sem = self.rz.at[a, jnp.clip(j, 0, at.n - 1)]
        copy = remote(view, view, self.sz.at[2 * t + (0 if up else 1), a], sem, at.along(jnp.clip(to, 0, at.n - 1)))
        return came, came & goes, copy

    def line(self, a, t):
        for up in (True, False):
            _, goes, _ = self.forward(a, t, up)

            @pl.when(goes)
            def _():
                copy = self.forward(a, t, up)[2]
                copy.wait_recv()
                copy.start()

    def send(self, view, a, j, k, kind, bit):
        remote(view, view, self.sp.at[kind, a, k - 1], self.rp.at[kind, a, j], self.at.across(bit)).start()

    def wait(self, view, a, j, kind):
        remote(view, view, self.sp.at[kind, a, 0], self.rp.at[kind, a, j], self.at.across(1)).wait_recv()

    def place(self, k):
        return item(k, self.at.s, self.at.n)[0]

    def spread(self, a, k):
        j = self.place(k)
        view = self.got(a, j, self.at.p)

        @pl.when((self.at.s == 0) | (self.at.s == self.at.n - 1))
        def _():
            remote(view, view, self.sz.at[0, a], self.rz.at[a, j], self.at.across(1)).wait_recv()

        self.send(view, a, j, k, 0, 2)
        self.send(view, a, j, k, 1, 4)
        self.send(view, a, j, k, 3, 1)

    def corner(self, a, k):
        at, j = self.at, self.place(k)
        from_x, from_y = self.got(a, j, at.q2), self.got(a, j, at.q4)
        self.wait(from_x, a, j, 0)
        self.send(self.half(a, j, at.q2, True), a, j, k, 7, 4)
        self.send(from_x, a, j, k, 4, 1)
        self.wait(from_y, a, j, 1)
        self.send(self.half(a, j, at.q4, False), a, j, k, 2, 2)
        self.send(from_y, a, j, k, 5, 1)

    def twin(self, a, k):
        at, j = self.at, self.place(k)
        self.wait(self.half(a, j, at.q6, False), a, j, 2)
        self.wait(self.half(a, j, at.q6, True), a, j, 7)
        self.send(self.got(a, j, at.q6), a, j, k, 6, 1)

    def ready(self, a, k):
        at, j = self.at, self.place(k)
        for kind, q in ((3, at.q1), (4, at.q3), (5, at.q5), (6, at.q7)):
            self.wait(self.got(a, j, q), a, j, kind)

    def drain(self):
        at = self.at
        for a in range(len(self.geo)):
            pl.when(at.s < at.n - 1)(lambda: self.own_copy(a, True).wait_send())
            pl.when(at.s > 0)(lambda: self.own_copy(a, False).wait_send())

            def body(k, carry):
                for up in (True, False):
                    _, goes, copy = self.forward(a, k, up)
                    pl.when(goes)(lambda: copy.wait_send())
                j = self.place(k)
                whole = self.got(a, j, at.p)
                for kind, view in (
                    (0, whole), (1, whole), (2, self.half(a, j, at.p, False)), (3, whole), (4, whole), (5, whole), (6, whole),
                    (7, self.half(a, j, at.p, True)),
                ):
                    remote(view, view, self.sp.at[kind, a, k - 1], self.rp.at[kind, a, j], at.across(1)).wait_send()
                return carry

            lax.fori_loop(1, at.n, body, 0)


class Line:
    def __init__(self, at, i, ssem, rsem):
        self.at, self.i, self.ssem, self.rsem = at, i, ssem, rsem

    def start(self, view_of, into, only=None):
        at = self.at
        self.into = into
        for r in range(1, at.n) if only is None else (only,):
            d = lax.rem(at.s + r, at.n)
            remote(view_of(d), into.at[at.s], self.ssem.at[self.i, r], self.rsem.at[self.i, at.s], at.along(d)).start()

    def arrived(self):
        at = self.at
        for r in range(1, at.n):
            d = lax.rem(at.s + r, at.n)
            view = self.into.at[d]
            remote(view, view, self.ssem.at[self.i, r], self.rsem.at[self.i, d], at.along(d)).wait_recv()

    def sent(self):
        view = self.into.at[0]
        for r in range(1, self.at.n):
            remote(view, view, self.ssem.at[self.i, r], self.rsem.at[self.i, 0], self.at.across(1)).wait_send()


def iota(shape, axis):
    return lax.broadcasted_iota(jnp.int32, shape, axis)


def one_hot(hit):
    return jnp.where(hit, 1.0, 0.0).astype(BF16)


def sources(deal, n, rows):
    src = jnp.zeros_like(deal)
    for k in range(1, n):
        src = src + jnp.where(deal >= k * rows, 1, 0)
    return src


def sending_order(deal_ref, s, n, rows):
    cap = rows // n
    before = one_hot(iota((rows, rows), 0) < iota((rows, rows), 1))
    deal = jnp.concatenate([deal_ref[:, b * rows : (b + 1) * rows] for b in range(n)], axis=0)
    if n < 8:
        deal = jnp.concatenate([deal, jnp.full((8 - n, rows), -1, jnp.int32)], axis=0)
    hit = (sources(deal, n, rows) == s) & (deal >= 0)
    rank = nn(one_hot(hit), before).astype(jnp.int32)
    place = jnp.where(hit, rank + iota(deal.shape, 0) * cap, -1)
    mine = deal - s * rows
    total = jnp.zeros((rows, rows), F32)
    row = iota((rows, rows), 0)
    for b in range(n):
        total = total + nt(one_hot(row == place[b : b + 1, :]), one_hot(row == mine[b : b + 1, :]))
    return total.astype(BF16)


def collecting_order(deal_ref, before, s, n, rows):
    cap = rows // n
    deal = deal_ref[:, pl.ds(pl.multiple_of(s * rows, 128), rows)]
    kind = iota((8, rows), 0)
    hit = jnp.broadcast_to(sources(deal, n, rows), (8, rows)) == kind
    rank = nn(one_hot(hit), before).astype(jnp.int32)
    place = jnp.sum(jnp.where(hit, rank + kind * cap, 0).astype(F32), axis=0, keepdims=True).astype(jnp.int32)
    return one_hot(iota((rows, LIVE), 0) == place[:, :LIVE])


def slots_of(len_ref, idx_ref, pos_ref, mask_ref):
    slot = iota((LIVE, NAR), 0)
    lane = iota((LIVE, NAR), 1)
    count = len_ref.shape[1]
    start = jnp.zeros((LIVE, NAR), jnp.int32)
    chosen = jnp.full((LIVE, NAR), idx_ref[0, 0], jnp.int32)
    end = jnp.int32(0)
    for i in range(count):
        end = end + len_ref[0, i]
        passed = slot >= end
        start = jnp.where(passed, end, start)
        chosen = jnp.where(passed, idx_ref[0, i + 1] if i + 1 < count else -1, chosen)
    pos_ref[...] = slot - start
    low = chosen * R
    mask_ref[...] = jnp.where((lane >= low) & (lane < low + R), 1.0, 0.0)


REC_PARTS = ("db", "dg", "dgates", "dm", "ub", "ug", "ugates", "um")
FFN_PARTS = ("dfg", "dfu", "dfd", "ufg", "ufu", "ufd")


def first_kernel(z, geo, *refs):
    n, w, d, h, hp = z.n, z.w, z.d, z.h, z.hp
    refs = list(refs)

    def take(count):
        out, refs[:count] = refs[:count], []
        return out

    len_r, idx_r, deal_r, small_r = take(4)
    tokens, cotangent = take(2)
    ob, og, ogw, om, ofg, ofu, ofd = take(7)
    pieces_r, pieces_f = take(8), take(6)
    gb, gg, ggw, gr, gm, gfg, gfu, gf, gfd = gathered = take(9)
    gtok, gcot, gsm = take(3)
    act1_h, xin_h, mixed_h, ranks_h, rt_h, s_h = take(6)
    conv_h, gi_h, ig_h, rg_h, st_h = take(5)
    out_h, gres_h, grad_h = take(3)
    pack_r, pack_f, rows_out, smv, s_v, rt_v, pos_r, mask_r, act1, resid, ranks = take(11)
    sz, sp, rz, rp, lss, lrs, lsem, psem, osem = take(9)
    at = Plane(n)
    s = at.s
    at.greet()
    net = Gather(at, geo, [ob, og, ogw, pack_r, om, ofg, ofu, pack_f, ofd], gathered, sz, sp, rz, rp)
    rec, ffn = [0, 1, 3, 2, 4], [5, 6, 8]
    net.own(0)
    net.own(1)
    packing = []
    for i, (dst, table, names, parts) in enumerate(((pack_r, z.rec, REC_PARTS, pieces_r), (pack_f, z.ffn, FFN_PARTS, pieces_f))):
        for k, (name, ref) in enumerate(zip(names, parts)):
            size = ref.shape[1]
            copy = pltpu.make_async_copy(ref, dst.at[:, table[name] : table[name] + size], psem.at[i, k])
            copy.start()
            packing.append(copy)
    smv[s] = small_r[...]
    lines = [Line(at, i, lss, lrs) for i in range(3)]
    lines[2].start(lambda place: small_r, gsm)
    for copy in packing:
        copy.wait()
    net.own(3)

    def sending(rows_in):
        toks = [pltpu.make_async_copy(ref, rows_in.at[i], lsem.at[0, i]) for i, ref in enumerate((tokens, cotangent))]
        for copy in toks:
            copy.start()
        order = sending_order(deal_r, s, n, z.rows)
        s_v[...] = order
        for i in range(2):
            toks[i].wait()
            rows_out[i] = nn(order, rows_in[i]).astype(BF16).reshape(n, z.cap, d)

    pl.run_scoped(sending, pltpu.VMEM((2, z.rows, d), BF16))
    before = one_hot(iota((z.rows, z.rows), 0) < iota((z.rows, z.rows), 1))
    rt_v[...] = collecting_order(deal_r, before, s, n, z.rows)
    slots_of(len_r, idx_r, pos_r, mask_r)
    outs = []

    def put(src, dst):
        copy = pltpu.make_async_copy(src, dst, osem.at[len(outs)])
        copy.start()
        outs.append(copy)

    put(s_v, s_h)
    put(rt_v, rt_h)
    put(pack_r, gr.at[s])
    put(small_r, gsm.at[s])
    items = [(a, k) for k in range(1, n) for a in rec] + [(7, k) for k in range(1, n)] + [(a, 1) for a in ffn]
    count = len(items)
    for i in range(count):
        if i in (4, 7, 10):
            for r in range(1, n):
                if (r - 1) % 3 == (4, 7, 10).index(i):
                    lines[0].start(lambda place: rows_out.at[0, place], gtok, r)
        if i + 3 < len(rec):
            net.own(rec[i + 3])
        if i == len(rec):
            net.own(7)
        if 0 <= i - 12 < len(ffn):
            net.own(ffn[i - 12])
        net.line(*items[i])
        net.spread(*items[i])
        if i >= 2 and items[i - 2][0] not in ffn:
            net.corner(*items[i - 2])
        if i >= 4 and items[i - 4][0] not in ffn:
            net.twin(*items[i - 4])
    for i in range(count - 4, count):
        if items[i][0] not in ffn:
            net.twin(*items[i])
    for a, k in items:
        if a in rec:
            net.ready(a, k)
    lines[2].arrived()
    small_in = []
    for r in range(1, n):
        o = lax.rem(s + r, n)
        copy = pltpu.make_async_copy(gsm.at[o], smv.at[o], lsem.at[1, r])
        copy.start()
        small_in.append(copy)
    lines[0].arrived()
    mask = mask_r[...]

    def rows_of(i, got, into, sem):
        keep = into.at[pl.ds(pl.multiple_of(s * z.cap, 8), z.cap)]
        copies = [pltpu.make_async_copy(rows_out.at[i, s], keep, sem.at[0])]
        for r in range(1, n):
            o = lax.rem(s + r, n)
            copies.append(pltpu.make_async_copy(got.at[o], into.at[pl.ds(pl.multiple_of(o * z.cap, 8), z.cap)], sem.at[r]))
        for copy in copies:
            copy.start()
        for copy in copies:
            copy.wait()

    for copy in small_in:
        copy.wait()
    gain1, gain2 = gain_row(smv, 8, n, d), gain_row(smv, 9, n, d)

    def load_pack(pack, got, into, sem):
        rows = NAR // n
        copies = []
        for j in range(n):
            dst = into.at[pl.ds(j * rows, rows)]
            start_either(s, j, pack, got.at[j], dst, sem.at[j])
            copies.append(pltpu.make_async_copy(got.at[j], dst, sem.at[j]))
        return copies

    def recurrent(tok, wb, wg, wgw, wm, adp, conv, gi, hold, cl, mix, acc, lg, tsem, wsem, hsem):
        col = z.rec

        def cols(name, size, j=0):
            return pl.ds(pl.multiple_of(col[name] + j * size, 128), size)

        def load_a(j, slot):
            start_either(s, j, ob, gb.at[j], wb.at[slot], wsem.at[slot, 0])
            start_either(s, j, og, gg.at[j], wg.at[slot], wsem.at[slot, 1])

        def load_b(j, slot):
            start_either(s, j, ogw, ggw.at[j], wgw.at[slot], wsem.at[slot, 2])
            start_either(s, j, om, gm.at[j], wm.at[slot], wsem.at[slot, 3])

        adp_in = load_pack(pack_r, gr, adp, tsem.at[1])
        load_a(jnp.int32(0), 0)
        load_b(jnp.int32(0), 0)
        rows_of(0, gtok, tok, tsem.at[0])
        xin = tn(rt_v[...], tok[...])
        resid[...] = xin
        tok[pl.ds(0, LIVE)] = xin.astype(BF16)
        put(tok.at[pl.ds(0, LIVE)], xin_h)
        act1[...] = (xin * norm_scale(xin) * gain1).astype(BF16)
        put(act1, act1_h)
        for copy in adp_in:
            copy.wait()
        ranks[0] = (nt(act1[...], adp[:, cols("db", d)]) * mask).astype(BF16)
        ranks[1] = (nt(act1[...], adp[:, cols("dg", d)]) * mask).astype(BF16)
        acc[...] = jnp.zeros_like(acc)

        def first_pass(j, carry):
            slot = lax.rem(j, 2)
            pltpu.make_async_copy(ob, wb.at[slot], wsem.at[slot, 0]).wait()
            pltpu.make_async_copy(og, wg.at[slot], wsem.at[slot, 1]).wait()

            @pl.when(j + 1 < n)
            def _():
                load_a(j + 1, 1 - slot)

            s32 = smv[j].astype(F32)
            gi[j] = nn(act1[...], wg[slot]) + nn(ranks[1], adp[:, cols("ug", w, j)])
            lg[:, :w] = nn(act1[...], wb[slot]) + nn(ranks[0], adp[:, cols("ub", w, j)])

            def block(r, last):
                at_rows = pl.ds(pl.multiple_of(r * BLOCK, BLOCK), BLOCK)
                br = lg[at_rows, :w]
                both = jnp.concatenate([last, br], axis=0)
                pos = wide(pos_r[at_rows, :], w)
                total = s32[4:5, :] + s32[0:1, :] * br
                for k in range(1, 4):
                    total = total + jnp.where(pos >= k, both[8 - k : 8 - k + BLOCK, :], 0.0) * s32[k : k + 1, :]
                conv[j, at_rows, :] = total
                cl[j, at_rows, :] = total.astype(BF16)
                return br[BLOCK - 8 :, :]

            lax.fori_loop(0, LIVE // BLOCK, block, jnp.zeros((8, w), F32))
            pltpu.make_async_copy(conv.at[j], conv_h.at[j], hsem.at[0, j]).start()
            pltpu.make_async_copy(gi.at[j], gi_h.at[j], hsem.at[1, j]).start()
            acc[...] += nt(cl[j], adp[:, cols("dgates", w, j)])
            for i, a in enumerate(ffn):
                @pl.when(j == i)
                def _():
                    if n > 2:
                        net.line(a, 2)
                    net.corner(a, 1)
            return carry

        lax.fori_loop(0, n, first_pass, 0)
        ranks[2] = (acc[...] * mask).astype(BF16)
        acc[...] = jnp.zeros_like(acc)
        holds = (ig_h, rg_h, st_h)

        def second_pass(j, carry):
            slot = lax.rem(j, 2)
            pltpu.make_async_copy(ogw, wgw.at[slot], wsem.at[slot, 2]).wait()
            pltpu.make_async_copy(om, wm.at[slot], wsem.at[slot, 3]).wait()

            @pl.when(j + 1 < n)
            def _():
                load_b(j + 1, 1 - slot)

            @pl.when(j >= 2)
            def _():
                for i, ref in enumerate(holds):
                    pltpu.make_async_copy(hold.at[slot, i], ref.at[j - 2], hsem.at[2 + i, slot]).wait()

            s32 = smv[j].astype(F32)
            low = cl[j]
            lift = nn(ranks[2], adp[:, cols("ugates", 2 * w, j)])
            bias = jnp.concatenate([s32[6:7, :], s32[7:8, :]], axis=1)
            lg[...] = jnp.concatenate(
                [nn(low[:, i * DH : (i + 1) * DH], wgw[slot, i * DH : (i + 1) * DH, :]) for i in range(z.heads)], axis=1
            ) + bias + lift

            def block(r, carry):
                at_rows = pl.ds(pl.multiple_of(r * BLOCK, BLOCK), BLOCK)
                ig, rg = gates_of(lg[at_rows, :], z)
                first = wide(pos_r[at_rows, :], w) == 0
                _, a, scale = decay_of(s32, rg, first)
                hold[slot, 0, at_rows, :] = ig
                hold[slot, 1, at_rows, :] = rg
                state, _, carry = scan_block(a, scale * ig * conv[j, at_rows, :], carry, False)
                hold[slot, 2, at_rows, :] = state
                act, _ = gelu_parts(gi[j, at_rows, :])
                mix[j, at_rows, :] = (state * act).astype(BF16)
                return carry

            lax.fori_loop(0, LIVE // BLOCK, block, jnp.zeros((8, w), F32))
            for i, ref in enumerate(holds):
                pltpu.make_async_copy(hold.at[slot, i], ref.at[j], hsem.at[2 + i, slot]).start()
            acc[...] += nt(mix[j], adp[:, cols("dm", w, j)])
            resid[...] += nn(mix[j], wm[slot])
            for i, a in enumerate(ffn):
                @pl.when(j == i)
                def _():
                    if n > 2:
                        net.spread(a, 2)
                    if n > 3:
                        net.line(a, 3)
            return carry

        lax.fori_loop(0, n, second_pass, 0)
        lines[1].start(lambda place: rows_out.at[1, place], gcot)
        put(mix, mixed_h)
        ranks[3] = (acc[...] * mask).astype(BF16)
        put(ranks, ranks_h)
        resid[...] = resid[...] + nn(ranks[3], adp[:, cols("um", d)])
        for j in range(n):
            pltpu.make_async_copy(conv.at[j], conv_h.at[j], hsem.at[0, j]).wait()
            pltpu.make_async_copy(gi.at[j], gi_h.at[j], hsem.at[1, j]).wait()
        for j in (n - 2, n - 1):
            for i, ref in enumerate(holds):
                pltpu.make_async_copy(hold.at[j % 2, i], ref.at[j], hsem.at[2 + i, j % 2]).wait()
        for copy in outs[4:]:
            copy.wait()

    V = pltpu.VMEM
    pl.run_scoped(
        recurrent,
        V((z.rows, d), BF16), V((2, d, w), BF16), V((2, d, w), BF16), V((2, w, 2 * DH), BF16), V((2, w, d), BF16),
        V((NAR, z.rec_cols), BF16), V((n, LIVE, w), F32), V((n, LIVE, w), F32), V((2, 3, LIVE, w), F32),
        V((n, LIVE, w), BF16), V((n, LIVE, w), BF16), V((LIVE, NAR), F32), V((LIVE, 2 * w), F32),
        DMA((2, n)), DMA((2, 4)), DMA((5, n)),
    )

    def feed(tok, wg, wu, wd, adp, act2, gl, acc_o, acc_g, rk, ra, grad_o, hgs, hus, ghs, low, ghg, ghu, tsem, wsem):
        col = z.ffn

        def cols(name, size, j=0, stride=0):
            return pl.ds(pl.multiple_of(col[name] + j * stride, 128), size)

        base = resid[...]
        act2[...] = (base * norm_scale(base) * gain2).astype(BF16)
        acc_o[...] = jnp.zeros_like(acc_o)
        acc_g[...] = jnp.zeros_like(acc_g)
        ra[...] = jnp.zeros_like(ra)
        weights = ((5, ofg, gfg, wg), (6, ofu, gfu, wu), (8, ofd, gfd, wd))
        for k in range(1, n):
            net.ready(7, k)

        def onward(q):
            for a in ffn:
                @pl.when(q + 3 < n)
                def _():
                    net.spread(a, q + 3)

                @pl.when(q + 4 < n)
                def _():
                    net.line(a, q + 4)

        def settle(q):
            for a in ffn:
                @pl.when(q + 1 < n)
                def _():
                    net.twin(a, q + 1)

            for a in ffn:
                @pl.when(q + 2 < n)
                def _():
                    net.corner(a, q + 2)

        def step(q, carry):
            j = jnp.where(q == 0, s, item(jnp.maximum(q, 1), s, n)[0])
            def fetch(i):
                a, mine, got, into = weights[i]

                @pl.when(q > 0)
                def _():
                    net.ready(a, q)
                    pltpu.make_async_copy(got.at[j], into, wsem.at[i]).start()

            fetch(0)
            fetch(1)
            pl.when(q < n - 1)(lambda: fetch(2))
            fg, fu, fd = cols("ufg", h, j, hp), cols("ufu", h, j, hp), cols("dfd", h, j, hp)
            pltpu.make_async_copy(ofg, wg, wsem.at[0]).wait()
            hgs[...] = nn(act2[...], wg[...]) + nn(rk[0], adp[:, fg])
            onward(q)
            pltpu.make_async_copy(ofu, wu, wsem.at[1]).wait()
            hus[...] = nn(act2[...], wu[...]) + nn(rk[1], adp[:, fu])
            @pl.when(q == 0)
            def _():
                lines[1].arrived()
                rows_of(1, gcot, tok, tsem.at[0])
                gl[...] = tn(rt_v[...], tok[...]).astype(BF16)
                rk[2] = (nt(gl[...], adp[:, cols("ufd", d)]) * mask).astype(BF16)

            pl.when(q == n - 1)(lambda: fetch(2))
            pltpu.make_async_copy(ofd, wd, wsem.at[2]).wait()
            ghs[...] = nt(gl[...], wd[...]) + nn(rk[2], adp[:, fd])

            def block(r, carry):
                at_rows = pl.ds(pl.multiple_of(r * 16, 16), 16)
                act, slope = gelu_parts(hgs[at_rows, :])
                hu, gh = hus[at_rows, :], ghs[at_rows, :]
                low[at_rows, :] = (act * hu).astype(BF16)
                ghg[at_rows, :] = (gh * hu * slope).astype(BF16)
                ghu[at_rows, :] = (gh * act).astype(BF16)
                return carry

            lax.fori_loop(0, LIVE // 16, block, 0)
            acc_o[...] += nn(low[...], wd[...])
            ra[0] += nt(low[...], adp[:, fd])
            ra[1] += nt(ghg[...], adp[:, fg])
            ra[2] += nt(ghu[...], adp[:, fu])
            acc_g[...] += nt(ghg[...], wg[...]) + nt(ghu[...], wu[...])
            grad_o[:, fd] = tn(rk[2], low[...]).astype(BF16)
            grad_o[:, fg] = tn(rk[0], ghg[...]).astype(BF16)
            grad_o[:, fu] = tn(rk[1], ghu[...]).astype(BF16)
            settle(q)
            return carry

        adp_in = load_pack(pack_f, gf, adp, tsem.at[1])
        for i, (a, mine, got, into) in enumerate(weights):
            pltpu.make_async_copy(mine, into, wsem.at[i]).start()
        for copy in adp_in:
            copy.wait()
        rk[0] = (nt(act2[...], adp[:, cols("dfg", d)]) * mask).astype(BF16)
        rk[1] = (nt(act2[...], adp[:, cols("dfu", d)]) * mask).astype(BF16)
        lax.fori_loop(0, n, step, 0)
        rank = (ra[0] * mask).astype(BF16)
        work = resid[...] + acc_o[...] + nn(rank, adp[:, cols("ufd", d)])
        tok[...] = nn(rt_v[...], work.astype(BF16)).astype(BF16)
        put(tok, out_h)
        grad_o[:, cols("ufd", d)] = tn(rank, gl[...]).astype(BF16)
        rank_g = (ra[1] * mask).astype(BF16)
        rank_u = (ra[2] * mask).astype(BF16)
        grad_o[:, cols("dfg", d)] = tn(rank_g, act2[...]).astype(BF16)
        grad_o[:, cols("dfu", d)] = tn(rank_u, act2[...]).astype(BF16)
        gact = acc_g[...] + nn(rank_g, adp[:, cols("dfg", d)]) + nn(rank_u, adp[:, cols("dfu", d)])
        put(grad_o, grad_h)
        resid[...] = gl[...].astype(F32) + norm_back(resid[...], gact * gain2)
        put(resid, gres_h)
        for copy in outs[8:]:
            copy.wait()

    pl.run_scoped(
        feed,
        V((z.rows, d), BF16), V((d, h), BF16), V((d, h), BF16), V((h, d), BF16), V((NAR, z.ffn_cols), BF16),
        V((LIVE, d), BF16), V((LIVE, d), BF16), V((LIVE, d), F32), V((LIVE, d), F32),
        V((3, LIVE, NAR), BF16), V((3, LIVE, NAR), F32), V((NAR, z.ffn_cols), BF16),
        V((LIVE, h), F32), V((LIVE, h), F32), V((LIVE, h), F32), V((LIVE, h), BF16), V((LIVE, h), BF16), V((LIVE, h), BF16),
        DMA((2, n)), DMA((3,)),
    )
    for line in lines:
        line.sent()
    for copy in outs[:4]:
        copy.wait()
    net.drain()


def run_first(z, geo, *args):
    n, w, d = z.n, z.w, z.d
    S, V = jax.ShapeDtypeStruct, pltpu.VMEM
    sources_ = args[6:13]
    shapes = [sources_[0], sources_[1], sources_[2], (NAR // n, z.rec_cols), sources_[3], sources_[4], sources_[5], (NAR // n, z.ffn_cols), sources_[6]]
    outs = [S((n,) + tuple(x.shape if hasattr(x, "shape") else x), BF16) for x in shapes]
    na = len(outs)
    outs += [S((n, z.cap, d), BF16)] * 2 + [S((n, 16, w), BF16)]
    outs += [S((LIVE, d), BF16), S((LIVE, d), BF16), S((n, LIVE, w), BF16), S((4, LIVE, NAR), BF16), S((z.rows, LIVE), BF16), S((z.rows, z.rows), BF16)]
    outs += [S((n, LIVE, w), F32)] * 5
    outs += [S((z.rows, d), BF16), S((LIVE, d), F32), S((NAR, z.ffn_cols), BF16)]
    SM = pl.BlockSpec(memory_space=pltpu.SMEM)
    return pl.pallas_call(
        functools.partial(first_kernel, z, geo),
        out_shape=outs,
        in_specs=[SM, SM, VM, VM] + [ANY] * (len(args) - 4),
        out_specs=[ANY] * len(outs),
        scratch_shapes=[
            V((NAR // n, z.rec_cols), BF16), V((NAR // n, z.ffn_cols), BF16), V((2, n, z.cap, d), BF16), V((n, 16, w), BF16),
            V((z.rows, z.rows), BF16), V((z.rows, LIVE), BF16), V((LIVE, NAR), jnp.int32), V((LIVE, NAR), F32),
            V((LIVE, d), BF16), V((LIVE, d), F32), V((4, LIVE, NAR), BF16),
            DMA((2 * n, na)), DMA((8, na, n - 1)), DMA((na, n)), DMA((8, na, n)), DMA((3, n)), DMA((3, n)),
            DMA((2, n)), DMA((2, 8)), DMA((11,)),
        ],
        compiler_params=pltpu.CompilerParams(collective_id=1, has_side_effects=True, vmem_limit_bytes=VLIMIT),
        name="first",
    )(*args)


def add_rows(dst, left, right, rows, step=16):
    def body(r, carry):
        at_rows = pl.ds(pl.multiple_of(r * step, step), step)
        dst[at_rows, :] = (left[at_rows, :].astype(F32) + right[at_rows, :].astype(F32)).astype(BF16)
        return carry

    lax.fori_loop(0, rows // step, body, 0)


class Reduce:
    def __init__(self, at, t, clusters, width, source, own, fin, bufs, sems):
        self.at, self.t, self.clusters, self.c = at, t, clusters, width
        self.source, self.own, self.fin = source, own, fin
        self.rc, self.r1, self.r2, self.rg, self.rz, self.sm = bufs
        self.ss, self.rs, self.zs, self.zr, self.gs, self.gr, self.ps, self.pr = [x.at[t] for x in sems]
        p = at.p
        self.core, self.x, self.y = p % 2, (p // 2) % 2, p // 4
        self.rows, self.half = NAR // at.n, NAR // 2
        self.final = 1 if clusters > 1 else 0

    def cut(self, q):
        return pl.ds(pl.multiple_of(q * self.c, 128), self.c)

    def send(self, src, dst, a, b, device):
        remote(src, dst, a, b, device).start()

    def arrived(self, dst, a, b):
        remote(dst, dst, a, b, self.at.across(1)).wait_recv()

    def to_core(self):
        for c in range(4):
            self.send(self.source.at[:, self.cut(2 * c + 1 - self.core)], self.rc.at[c], self.ss.at[c], self.rs.at[c], self.at.across(1))

    def to_first(self):
        for c in range(4):
            self.arrived(self.rc.at[c], self.ss.at[c], self.rs.at[c])
            add_rows(self.rc.at[c], self.own(c), self.rc.at[c], NAR)
        low, high = pl.ds(0, self.half), pl.ds(self.half, self.half)
        for i in range(2):
            self.send(self.rc.at[2 * i + 1 - self.x, low], self.r1.at[0, i], self.ss.at[4 + i], self.rs.at[4 + i], self.at.across(2))
            self.send(self.rc.at[2 * (1 - self.y) + i, high], self.r1.at[1, i], self.ss.at[6 + i], self.rs.at[6 + i], self.at.across(4))

    def to_second(self):
        low, high = pl.ds(0, self.half), pl.ds(self.half, self.half)
        for i in range(2):
            self.arrived(self.r1.at[0, i], self.ss.at[4 + i], self.rs.at[4 + i])
            add_rows(self.r1.at[0, i], self.rc.at[2 * i + self.x, low], self.r1.at[0, i], self.half)
            self.arrived(self.r1.at[1, i], self.ss.at[6 + i], self.rs.at[6 + i])
            add_rows(self.r1.at[1, i], self.rc.at[2 * self.y + i, high], self.r1.at[1, i], self.half)
        self.send(self.r1.at[0, 1 - self.y], self.r2.at[0, low], self.ss.at[8], self.rs.at[8], self.at.across(4))
        self.send(self.r1.at[1, 1 - self.x], self.r2.at[0, high], self.ss.at[9], self.rs.at[9], self.at.across(2))

    def to_line(self):
        at = self.at
        low, high = pl.ds(0, self.half), pl.ds(self.half, self.half)
        self.arrived(self.r2.at[0, low], self.ss.at[8], self.rs.at[8])
        add_rows(self.r2.at[0, low], self.r1.at[0, self.y], self.r2.at[0, low], self.half)
        self.arrived(self.r2.at[0, high], self.ss.at[9], self.rs.at[9])
        add_rows(self.r2.at[0, high], self.r1.at[1, self.x], self.r2.at[0, high], self.half)
        if self.clusters > 1:
            mine = at.rep // PLANE
            for r in range(1, self.clusters):
                device = {"rep": lax.rem(at.rep + r * PLANE, self.clusters * PLANE), "shard": at.s}
                self.send(self.r2.at[0], self.rg.at[mine], self.gs.at[r], self.gr.at[mine], device)
            self.rg[mine] = self.r2[0]
            for r in range(1, self.clusters):
                other = lax.rem(mine + r, self.clusters)
                self.arrived(self.rg.at[other], self.gs.at[r], self.gr.at[other])
            add_rows(self.r2.at[1], self.rg.at[0], self.rg.at[1], NAR)
            for other in range(2, self.clusters):
                add_rows(self.r2.at[1], self.rg.at[other], self.r2.at[1], NAR)
        for r in range(1, at.n):
            d = lax.rem(at.s + r, at.n)
            chunk = pl.ds(pl.multiple_of(d * self.rows, self.rows), self.rows)
            self.send(self.r2.at[self.final, chunk], self.rz.at[at.s], self.zs.at[r], self.zr.at[at.s], at.along(d))

    def to_plane(self):
        at = self.at
        total = self.r2[self.final, pl.ds(pl.multiple_of(at.s * self.rows, self.rows), self.rows), :].astype(F32)
        for r in range(1, at.n):
            d = lax.rem(at.s + r, at.n)
            self.arrived(self.rz.at[d], self.zs.at[r], self.zr.at[d])
            total = total + self.rz[d].astype(F32)
        self.sm[...] = total.astype(BF16)
        self.fin[:, self.cut(at.p)] = total.astype(BF16)
        for kind, bit in ((0, 2), (1, 4), (3, 1)):
            self.spread(kind, at.p, bit, self.sm)

    def spread(self, kind, q, bit, src=None):
        view = self.fin.at[:, self.cut(q)]
        self.send(view if src is None else src, view, self.ps.at[kind], self.pr.at[kind], self.at.across(bit))

    def spread_wait(self, kind, q):
        self.arrived(self.fin.at[:, self.cut(q)], self.ps.at[kind], self.pr.at[kind])

    def over(self):
        at = self.at
        self.spread_wait(0, at.q2)
        if self.t % 2 == 0:
            self.spread(2, at.q2, 4)
        self.spread(4, at.q2, 1)
        self.spread_wait(1, at.q4)
        if self.t % 2 == 1:
            self.spread(2, at.q4, 2)
        self.spread(5, at.q4, 1)

    def last(self):
        self.spread_wait(2, self.at.q6)
        self.spread(6, self.at.q6, 1)

    def end(self):
        at = self.at
        for kind, q in ((3, at.q1), (4, at.q3), (5, at.q5), (6, at.q7)):
            self.spread_wait(kind, q)
        sent = [(self.rc.at[0], self.ss.at[c]) for c in range(4)]
        sent += [(self.r1.at[0, 0], self.ss.at[4 + i]) for i in range(4)]
        sent += [(self.r2.at[0, pl.ds(0, self.half)], self.ss.at[8 + i]) for i in range(2)]
        sent += [(self.rg.at[0], self.gs.at[r]) for r in range(1, self.clusters)]
        sent += [(self.rz.at[0], self.zs.at[r]) for r in range(1, at.n)]
        sent += [(self.sm, self.ps.at[kind]) for kind in range(7)]
        for view, sem in sent:
            remote(view, view, sem, sem, at.across(1)).wait_send()


def early_table(z):
    return {"um": 0, "dm": z.d, "ugates": z.d + z.n * z.w}, up_to(z.d + 3 * z.n * z.w, 128 * PLANE)


def late_table(z):
    lru = z.n * z.w
    return {"dgates": 0, "ub": lru, "ug": 2 * lru, "db": 3 * lru, "dg": 3 * lru + z.d}, up_to(3 * lru + 2 * z.d, 128 * PLANE)


def second_kernel(z, clusters, *refs):
    n, w, d = z.n, z.w, z.d
    refs = list(refs)

    def take(count):
        out, refs[:count] = refs[:count], []
        return out

    len_r, idx_r, rt_v, gres, ranks = take(5)
    sm_h, ob, og, ogw, om, gb, gg, ggw, gm, gr = take(10)
    conv_h, gi_h, ig_h, rg_h, st_h, act1_h, xin_h, mixed_h, out_h, gradf_h = take(10)
    back_out, back_tok, fin_f, fin_e, fin_l = take(5)
    pos_r, mask_r, smv, adp, glm, gdir, glow, gilow, gmix, acc, rk, accg, tokv, grad_e, grad_l, own_f = take(16)
    bufs = [take(6) for _ in range(3)]
    sems = take(8)
    lss, lrs, lsem = take(3)
    at = Plane(n)
    s = at.s
    at.greet(clusters)
    lines = [Line(at, i, lss, lrs) for i in range(2)]
    lines[0].start(lambda place: out_h.at[place], back_out)
    keep = pltpu.make_async_copy(out_h.at[s], back_out.at[s], lsem.at[0, 0])
    keep.start()
    (early, _), (late, _) = early_table(z), late_table(z)
    core = at.p % 2

    def own_of(ref, width):
        return lambda c: ref.at[:, pl.ds(pl.multiple_of((2 * c + core) * width, 128), width)]

    widths = [x.shape[2] for x in (bufs[0][0], bufs[1][0], bufs[2][0])]
    red_f = Reduce(at, 0, clusters, widths[0], gradf_h, lambda c: own_f.at[c], fin_f, bufs[0], sems)
    red_e = Reduce(at, 1, clusters, widths[1], grad_e, own_of(grad_e, widths[1]), fin_e, bufs[1], sems)
    red_l = Reduce(at, 2, clusters, widths[2], grad_l, own_of(grad_l, widths[2]), fin_l, bufs[2], sems)
    red_f.to_core()
    rows = NAR // n
    own_in = [pltpu.make_async_copy(own_of(gradf_h, widths[0])(c), own_f.at[c], lsem.at[1, c]) for c in range(4)]
    packs = [pltpu.make_async_copy(gr.at[j], adp.at[pl.ds(j * rows, rows)], lsem.at[2, j]) for j in range(n)]
    small_in = pltpu.make_async_copy(sm_h, smv, lsem.at[0, 1])
    for copy in own_in + packs + [small_in]:
        copy.start()
    slots_of(len_r, idx_r, pos_r, mask_r)
    mask = mask_r[...]
    col = z.rec

    def cols(name, size, j=0):
        return pl.ds(pl.multiple_of(col[name] + j * size, 128), size)

    def put_at(table, name, size, j=0):
        return pl.ds(pl.multiple_of(table[name] + j * size, 128), size)

    def rows_at(r):
        return pl.ds(pl.multiple_of(r * BLOCK, BLOCK), BLOCK)

    blocks = LIVE // BLOCK

    def state_pass(sav, wm, mixed, ssem):
        saved = (conv_h, gi_h, ig_h, rg_h, st_h)

        def load(j, slot):
            start_either(s, j, om, gm.at[j], wm.at[slot], ssem.at[slot, 5])
            for i, ref in enumerate(saved):
                pltpu.make_async_copy(ref.at[j], sav.at[slot, i], ssem.at[slot, i]).start()
            pltpu.make_async_copy(mixed_h.at[j], mixed.at[slot], ssem.at[slot, 6]).start()

        def load_wait(slot):
            pltpu.make_async_copy(om, wm.at[slot], ssem.at[slot, 5]).wait()
            for i, ref in enumerate(saved):
                pltpu.make_async_copy(ref.at[0], sav.at[slot, i], ssem.at[slot, i]).wait()
            pltpu.make_async_copy(mixed_h.at[0], mixed.at[slot], ssem.at[slot, 6]).wait()

        load(jnp.int32(0), 0)
        glm[...] = gres[...].astype(BF16)
        for copy in packs + [small_in]:
            copy.wait()
        rk[0] = (nt(glm[...], adp[:, cols("um", d)]) * mask).astype(BF16)
        grad_e[:, put_at(early, "um", d)] = tn(ranks[3], glm[...]).astype(BF16)
        acc[...] = jnp.zeros_like(acc)
        for copy in own_in:
            copy.wait()

        def body(j, carry):
            slot = lax.rem(j, 2)
            load_wait(slot)

            @pl.when(j + 1 < n)
            def _():
                load(j + 1, 1 - slot)

            s32 = smv[j].astype(F32)
            gmix[...] = nt(glm[...], wm[slot]) + nn(rk[0], adp[:, cols("dm", w, j)])
            grad_e[:, put_at(early, "dm", w, j)] = tn(rk[0], mixed[slot]).astype(BF16)

            def block(i, carry):
                at_rows = rows_at(blocks - 1 - i)
                gmx, conv, ig = gmix[at_rows, :], sav[slot, 0, at_rows, :], sav[slot, 2, at_rows, :]
                rg, state = sav[slot, 3, at_rows, :], sav[slot, 4, at_rows, :]
                act, slope = gelu_parts(sav[slot, 1, at_rows, :])
                gilow[j, at_rows, :] = (gmx * state * slope).astype(BF16)
                first = wide(pos_r[at_rows, :], w) == 0
                soft, a, scale = decay_of(s32, rg, first)
                x = gmx * act
                _, after, carry = scan_block(a, a * x, carry, True)
                total = x + after
                drive = total * scale
                gdir[j, at_rows, :] = drive * ig
                fed = ig * conv
                kept = total * (state - scale * fed)
                g_log = jnp.where(first, 0.0, kept - total * fed * (a * a) / scale)
                l_in = drive * conv * ig * (1.0 - ig)
                l_rec = -soft * g_log * rg * (1.0 - rg)
                for i in range(z.heads):
                    glow[j, at_rows, 2 * i * DH : (2 * i + 1) * DH] = l_in[:, i * DH : (i + 1) * DH].astype(BF16)
                    glow[j, at_rows, (2 * i + 1) * DH : (2 * i + 2) * DH] = l_rec[:, i * DH : (i + 1) * DH].astype(BF16)
                return carry

            lax.fori_loop(0, blocks, block, jnp.zeros((8, w), F32))
            acc[...] += nt(glow[j], adp[:, cols("ugates", 2 * w, j)])
            grad_e[:, put_at(early, "ugates", 2 * w, j)] = tn(ranks[2], glow[j]).astype(BF16)
            pl.when(j == 0)(red_f.to_first)
            pl.when(j == 2)(red_f.to_second)
            pl.when(j == 3)(red_f.to_line)
            return carry

        lax.fori_loop(0, n, body, 0)

    V = pltpu.VMEM
    pl.run_scoped(state_pass, V((2, 5, LIVE, w), F32), V((2, w, d), BF16), V((2, LIVE, w), BF16), DMA((2, 7)))
    rk[1] = (acc[...] * mask).astype(BF16)
    red_e.to_core()

    def branch_pass(wb, wg, wgw, conv, blow, act1, xin, grads_rank, wsem, asem):
        def load(j, slot):
            start_either(s, j, ob, gb.at[j], wb.at[slot], wsem.at[slot, 0])
            start_either(s, j, og, gg.at[j], wg.at[slot], wsem.at[slot, 1])
            start_either(s, j, ogw, ggw.at[j], wgw.at[slot], wsem.at[slot, 2])
            pltpu.make_async_copy(conv_h.at[j], conv.at[slot], wsem.at[slot, 3]).start()

        ends = [pltpu.make_async_copy(act1_h, act1, asem.at[0]), pltpu.make_async_copy(xin_h, xin, asem.at[1])]
        load(jnp.int32(0), 0)
        for copy in ends:
            copy.start()
        accg[...] = jnp.zeros_like(accg)
        grads_rank[...] = jnp.zeros_like(grads_rank)

        def body(j, carry):
            slot = lax.rem(j, 2)
            for i, (ref, into) in enumerate(((ob, wb), (og, wg), (ogw, wgw), (conv_h.at[0], conv))):
                pltpu.make_async_copy(ref, into.at[slot], wsem.at[slot, i]).wait()

            @pl.when(j + 1 < n)
            def _():
                load(j + 1, 1 - slot)

            s32 = smv[j].astype(F32)
            grad_l[:, put_at(late, "dgates", w, j)] = tn(rk[1], conv[slot].astype(BF16)).astype(BF16)
            low = glow[j]
            heads = jnp.concatenate(
                [nt(low[:, 2 * i * DH : 2 * (i + 1) * DH], wgw[slot, i * DH : (i + 1) * DH, :]) for i in range(z.heads)], axis=1
            )
            gmix[...] = gdir[j] + heads + nn(rk[1], adp[:, cols("dgates", w, j)])

            def block(i, carry):
                later, later_pos = carry
                at_rows = rows_at(blocks - 1 - i)
                cur, pos = gmix[at_rows, :], pos_r[at_rows, :]
                both = jnp.concatenate([cur, later], axis=0)
                both_pos = jnp.concatenate([pos, later_pos], axis=0)
                total = cur * s32[0:1, :]
                for k in range(1, 4):
                    inside = wide(both_pos[k : k + BLOCK, :], w) >= k
                    total = total + jnp.where(inside, both[k : k + BLOCK, :], 0.0) * s32[k : k + 1, :]
                blow[at_rows, :] = total.astype(BF16)
                return cur[:8, :], pos[:8, :]

            lax.fori_loop(0, blocks, block, (jnp.zeros((8, w), F32), jnp.zeros((8, NAR), jnp.int32)))
            gil = gilow[j]
            grad_l[:, put_at(late, "ub", w, j)] = tn(ranks[0], blow[...]).astype(BF16)
            grad_l[:, put_at(late, "ug", w, j)] = tn(ranks[1], gil).astype(BF16)
            accg[...] += nt(blow[...], wb[slot]) + nt(gil, wg[slot])
            grads_rank[0] += nt(blow[...], adp[:, cols("ub", w, j)])
            grads_rank[1] += nt(gil, adp[:, cols("ug", w, j)])
            pl.when(j == 0)(red_e.to_first)
            pl.when(j == 2)(red_e.to_second)
            pl.when(j == 3)(red_e.to_line)
            return carry

        lax.fori_loop(0, n, body, 0)
        rank_b = (grads_rank[0] * mask).astype(BF16)
        rank_g = (grads_rank[1] * mask).astype(BF16)
        for copy in ends:
            copy.wait()
        gain1 = gain_row(smv, 8, n, d)
        gact = accg[...] + nn(rank_b, adp[:, cols("db", d)]) + nn(rank_g, adp[:, cols("dg", d)])
        gwork = gres[...] + norm_back(xin[...].astype(F32), gact * gain1)
        tokv[...] = nn(rt_v[...], gwork.astype(BF16)).astype(BF16).reshape(n, z.cap, d)
        lines[1].start(lambda place: tokv.at[place], back_tok)
        grad_l[:, put_at(late, "db", d)] = tn(rank_b, act1[...]).astype(BF16)
        grad_l[:, put_at(late, "dg", d)] = tn(rank_g, act1[...]).astype(BF16)

    pl.run_scoped(
        branch_pass, V((2, d, w), BF16), V((2, d, w), BF16), V((2, w, 2 * DH), BF16), V((2, LIVE, w), F32),
        V((LIVE, w), BF16), V((LIVE, d), BF16), V((LIVE, d), BF16), V((2, LIVE, NAR), F32), DMA((2, 4)), DMA((2,)),
    )
    red_l.to_core()
    keep_tok = pltpu.make_async_copy(tokv.at[s], back_tok.at[s], lsem.at[0, 2])
    keep_tok.start()
    red_l.to_first()
    red_f.to_plane()
    red_l.to_second()
    red_f.over()
    red_e.to_plane()
    red_l.to_line()
    red_f.last()
    red_e.over()
    red_e.last()
    red_l.to_plane()
    red_l.over()
    red_l.last()
    for red in (red_f, red_e, red_l):
        red.end()
    for line in lines:
        line.arrived()
        line.sent()
    keep.wait()
    keep_tok.wait()


def run_second(z, clusters, *args):
    n, w, d = z.n, z.w, z.d
    S, V = jax.ShapeDtypeStruct, pltpu.VMEM
    cols = [z.ffn_cols, early_table(z)[1], late_table(z)[1]]
    rows, half = NAR // n, NAR // 2
    outs = [S((n, z.cap, d), BF16)] * 2 + [S((rows, c), BF16) for c in cols]
    scratch = [
        V((LIVE, NAR), jnp.int32), V((LIVE, NAR), F32), V((n, 16, w), BF16), V((NAR, z.rec_cols), BF16), V((LIVE, d), BF16),
        V((n, LIVE, w), F32), V((n, LIVE, 2 * w), BF16), V((n, LIVE, w), BF16), V((LIVE, w), F32), V((LIVE, NAR), F32),
        V((2, LIVE, NAR), BF16), V((LIVE, d), F32), V((n, z.cap, d), BF16), V((NAR, cols[1]), BF16), V((NAR, cols[2]), BF16),
        V((4, NAR, cols[0] // PLANE), BF16),
    ]
    more = clusters > 1
    for size in cols:
        c = size // PLANE
        scratch += [
            V((4, NAR, c), BF16), V((2, 2, half, c), BF16), V((2 if more else 1, NAR, c), BF16),
            V((clusters, NAR, c) if more else (1, 16, 128), BF16), V((n, rows, c), BF16), V((rows, c), BF16),
        ]
    scratch += [DMA((3, 10)), DMA((3, 10)), DMA((3, n)), DMA((3, n)), DMA((3, clusters)), DMA((3, clusters)), DMA((3, 7)), DMA((3, 7))]
    scratch += [DMA((2, n)), DMA((2, n)), DMA((3, max(n, 4)))]
    SM = pl.BlockSpec(memory_space=pltpu.SMEM)
    return pl.pallas_call(
        functools.partial(second_kernel, z, clusters),
        out_shape=outs,
        in_specs=[SM, SM, VM, VM, VM] + [ANY] * (len(args) - 5),
        out_specs=[ANY, ANY, VM, VM, VM],
        scratch_shapes=scratch,
        compiler_params=pltpu.CompilerParams(collective_id=2, has_side_effects=True, vmem_limit_bytes=VLIMIT),
        name="second",
    )(*args)


def local(
    tokens, cotangent, norm_first, branch_weight, gelu_weight, conv_weight, conv_bias, gate_weight, gate_bias,
    decay_param, merge_weight, norm_second, feed_gate, feed_up, feed_down, down_branch, up_branch, down_gelu,
    up_gelu, down_gates, up_gates, down_merge, up_merge, down_feed_gate, up_feed_gate, down_feed_up, up_feed_up,
    down_feed_down, up_feed_down, seq_lengths, adapter_index, deal_order,
):
    n = lax.axis_size("shard")
    clusters = lax.axis_size("rep") // PLANE
    rows, d = tokens.shape
    z = Sizes(n, d, branch_weight.shape[1] * n, feed_gate.shape[1] * n, rows)
    w, pad = z.w, z.hp - z.h

    def spaced(values):
        if pad == 0:
            return values
        parts = values.reshape(values.shape[0], n, z.h)
        return jnp.pad(parts, ((0, 0), (0, 0), (0, pad))).reshape(values.shape[0], n * z.hp)

    rec_own = (down_branch.T, down_gelu.T, down_gates.T, down_merge.T, up_branch, up_gelu, up_gates, up_merge)
    ffn_own = (
        down_feed_gate.T, down_feed_up.T, spaced(down_feed_down.T), spaced(up_feed_gate), spaced(up_feed_up), up_feed_down
    )

    def gain(values):
        return jnp.pad(values, (0, w - values.shape[0]))

    small = jnp.concatenate(
        [conv_weight.reshape(-1), conv_bias, decay_param, gate_bias.reshape(-1), gain(norm_first), gain(norm_second), jnp.zeros((6 * w,), BF16)]
    ).reshape(16, w)
    gates = gate_weight.reshape(w, 2 * DH)
    arrays = [branch_weight, gelu_weight, gates, None, merge_weight, feed_gate, feed_up, None, feed_down]
    sizes = [x.shape[0] if x is not None else 0 for x in arrays]
    geo = [(0, size // PLANE) for size in sizes]
    geo[3], geo[7] = (1, z.rec_cols // PLANE), (1, z.ffn_cols // PLANE)
    weights = (branch_weight, gelu_weight, gates, merge_weight)
    got = run_first(
        z, geo, seq_lengths, adapter_index, deal_order, small, tokens, cotangent, *weights, feed_gate, feed_up, feed_down,
        *rec_own, *ffn_own,
    )
    gb, gg, ggw, gr, gm, _, _, _, _, _, _, sm = got[:12]
    act1, xin, mixed, ranks, rt, order = got[12:18]
    saved = got[18:23]
    out_send, gres, grad_ffn = got[23:]
    back_out, back_tok, fin_f, fin_e, fin_l = run_second(
        z, clusters, seq_lengths, adapter_index, rt, gres, ranks, sm, *weights, gb, gg, ggw, gm, gr, *saved, act1, xin, mixed,
        out_send.reshape(n, z.cap, d), grad_ffn,
    )

    def arrival(received):
        return tn(order, received.reshape(rows, d))

    (early, _), (late, _) = early_table(z), late_table(z)

    def part(values, table, name, size):
        return values[:, table[name] : table[name] + size].astype(F32)

    def unspaced(values):
        if pad == 0:
            return values
        return values.reshape(values.shape[0], n, z.hp)[:, :, : z.h].reshape(values.shape[0], n * z.h)

    lru, ffp = n * w, n * z.hp
    return (
        arrival(back_out),
        arrival(back_tok),
        part(fin_l, late, "db", d).T,
        part(fin_l, late, "ub", lru),
        part(fin_l, late, "dg", d).T,
        part(fin_l, late, "ug", lru),
        part(fin_l, late, "dgates", lru).T,
        part(fin_e, early, "ugates", 2 * lru),
        part(fin_e, early, "dm", lru).T,
        part(fin_e, early, "um", d),
        part(fin_f, z.ffn, "dfg", d).T,
        unspaced(part(fin_f, z.ffn, "ufg", ffp)),
        part(fin_f, z.ffn, "dfu", d).T,
        unspaced(part(fin_f, z.ffn, "ufu", ffp)),
        unspaced(part(fin_f, z.ffn, "dfd", ffp)).T,
        part(fin_f, z.ffn, "ufd", d),
    )


def solution(mesh):
    tok, line, col, row = P(("rep", "shard"), None), P("shard"), P(None, "shard"), P("shard", None)
    in_specs = (
        tok, tok, line, col, col, col, line, P("shard", None, None), row, line, row, line, col, col, row,
    ) + (col, row) * 7 + (tok, tok, P("rep", None))
    out_specs = (tok, tok) + (col, row) * 7
    return jax.shard_map(local, mesh=mesh, in_specs=in_specs, out_specs=out_specs, check_vma=False)
```
